256 devices in a mesh: dp: 16 (over z, core), expert: 16 (over x, y).
Axes of the slice: x: 4, y: 4, z: 8, core: 2. Of those that a mesh axis runs over, the one named last changes fastest.
Arguments:
- tokens: bfloat16 [4096, 16, 1536], P('dp', 'expert'), may hold values from -6 to 6
- route_ids: int32 [16, 4096, 2], P('expert', 'dp'), may hold values from 0 to 15, all different within a row; in each aligned block of 256 rows (0 to 255, 256 to 511, ..., all dimensions but the last counted through in order) at most 48 rows name the same one
- router: bfloat16 [16, 1536, 16], P('expert'), may hold values from -0.15625 to 0.15625
- norm_gain: float32 [16, 1536], P('expert'), may hold values from 0.5 to 1.5
- w_in: bfloat16 [16, 16, 1536, 768], P('expert', 'dp'), may hold values from -0.15625 to 0.15625
- w_out: bfloat16 [16, 16, 768, 1536], P('expert', 'dp'), may hold values from -0.21875 to 0.21875
- cotangent: bfloat16 [4096, 16, 1536], P('dp', 'expert'), may hold values from -6 to 6
Outputs:
- normed_out: bfloat16 [4096, 16, 1536], P('dp', 'expert')
- grad_tokens: bfloat16 [4096, 16, 1536], P('dp', 'expert')
- grad_router: float32 [16, 1536, 16], P('expert')
- grad_gain: float32 [16, 1536], P('expert')
- grad_w_in: bfloat16 [16, 16, 1536, 768], P('expert', 'dp')
- grad_w_out: bfloat16 [16, 16, 768, 1536], P('expert', 'dp')
The draws below stay inside these ranges and needn't reach their ends.
Inputs may be any that keep to these rules, and one draw needn't show every extreme that they name: `route_ids`: the two ids of a row differ. Among the rows of one device (one mixed token, 256 samples, two choices each) no expert is named more than 48 times.
All inputs are finite; a program needn't handle non-finite values.
Results may differ from the reference program's by a relative error of at most 0.015.
Values may be sent and summed in bfloat16 or wider, within the bound.
A program may use at most 64 MiB of HBM per device.

```python
import math
import jax
import jax.numpy as jnp
import numpy as np
from jax import lax

D = 1536
HID = 768
TOP = 2
SAMP_DEV = 256
FEAT = 16
EXPERTS = 16
CAP = 48
SAMPLES = 4096
N_DP = 16


def block_levels(key, dims, shards, smallest, largest):
    loudness, own = 1.0, jax.random.fold_in(key, 6)
    for axis_at, parts in shards:
        steps = jnp.exp(jax.random.uniform(jax.random.fold_in(own, axis_at), (parts,), jnp.float32, smallest / len(shards), largest / len(shards)))
        loudness = loudness * jnp.repeat(steps, dims[axis_at] // parts).reshape([-1 if axis == axis_at else 1 for axis in range(len(dims))])
    return loudness


def shared_out(own_key, own, number, rows, number_of, top, limit, skew):
    sequence = jax.random.permutation(own_key, number_of)
    packed, ordinary = portions_of(number_of, rows * top, limit, skew, True), portions_of(number_of, rows * top, limit, skew, False)
    places = jnp.arange(number_of)

    def named(tallies, offset_by):
        used = int((tallies > 0).sum())
        fixed = max(1, used // 4)
        moved = fixed + (places - fixed + offset_by * (used - fixed)) % max(1, number_of - fixed)
        return jnp.zeros((number_of,), jnp.int32).at[sequence[jnp.where(places < fixed, places, moved)]].set(jnp.asarray(tallies, jnp.int32))

    tallies = jnp.where(number % 4 == 0, named(packed, number // 4), named(ordinary, number - number // 4 - 1))
    mixed = jax.random.permutation(jax.random.fold_in(own, 3), number_of)
    source_of, sink = mixed[0:number_of // 2 * 2:2], mixed[1:number_of // 2 * 2:2]
    margin = jnp.minimum(tallies[source_of] - 1, limit - tallies[sink]) // 2
    margin = jnp.where((source_of == sequence[0]) | (sink == sequence[0]) | (tallies[sink] == 0), 0, jnp.maximum(margin, 0))
    moved = jax.random.randint(jax.random.fold_in(own, 4), (number_of // 2,), 0, 1 << 20) % (margin + 1)
    tallies = tallies.at[source_of].add(-moved).at[sink].add(moved)
    items = jnp.searchsorted(jnp.cumsum(tallies), jnp.arange(rows * top), side="right").astype(jnp.int32)
    grid = items.reshape(top, rows).T
    grid = grid[jax.random.permutation(jax.random.fold_in(own, 1), rows)]
    offset_by = jax.random.randint(jax.random.fold_in(own, 2), (rows, 1), 0, top)
    return jnp.take_along_axis(grid, (jnp.arange(top)[None, :] + offset_by) % top, axis=1)


def portions_of(number_of, total, bound, slope, full):
    weights = [(1 << 20) // math.isqrt(grade ** slope) + 1 for grade in range(1, number_of + 1)]
    largest = bound if full else min(bound, max(-(-total // number_of), total * weights[0] // sum(weights)))
    least = 1 if total - largest >= number_of - 1 else 0
    counts, rest = [largest] + [least] * (number_of - 1), total - largest - least * (number_of - 1)
    while rest > 0:
        candidates = [i for i in range(1, number_of) if counts[i] < largest] or [i for i in range(1, number_of) if counts[i] < bound]
        pool, remaining = sum([weights[i] for i in candidates]), rest
        for i in candidates:
            addition = min(bound - counts[i], max(1, remaining * weights[i] // pool), rest)
            counts[i] = counts[i] + addition
            rest = rest - addition
    return np.array(counts)


def scatter_about(key, dims, scale, limit, cuts=(), kind=jnp.bfloat16):
    array = jax.random.normal(key, dims, jnp.float32) * scale
    if len(cuts) > 0:
        array = block_levels(key, dims, cuts, -0.22, 0.18) * array
    return jnp.clip(array, min=-limit, max=limit).astype(kind)


def setup_inputs(seed: int = 0) -> dict:
    streams_of = jax.random.split(jax.random.key(seed), 8)
    tokens = scatter_about(streams_of[0], (SAMPLES, FEAT, D), 1.0, 6.0, ((0, 16), (1, 16)))
    route_ids_keys = jax.random.split(jax.random.fold_in(streams_of[1], 1), FEAT * SAMPLES // SAMP_DEV)
    route_ids_turns = jax.random.permutation(jax.random.fold_in(streams_of[1], 3), FEAT * SAMPLES // SAMP_DEV)
    route_ids = jax.vmap(lambda own, number: shared_out(jax.random.fold_in(streams_of[1], 2), own, number, SAMP_DEV, EXPERTS, 2, CAP, 2))(route_ids_keys, route_ids_turns).reshape((FEAT, SAMPLES, TOP))
    router = scatter_about(streams_of[2], (FEAT, D, EXPERTS), D ** -0.5, 0.15625, ((0, 16),))
    norm_gain = jnp.clip(1.0 + 0.1 * jax.random.normal(streams_of[3], (FEAT, D), jnp.float32), 0.5, 1.5)
    w_in = scatter_about(streams_of[4], (FEAT, EXPERTS, D, HID), D ** -0.5, 0.15625, ((0, 16), (1, 16)))
    w_out = scatter_about(streams_of[5], (FEAT, EXPERTS, HID, D), HID ** -0.5, 0.21875, ((0, 16), (1, 16)))
    cotangent = scatter_about(streams_of[6], (SAMPLES, FEAT, D), 1.0, 6.0, ((0, 16), (1, 16)))
    return {"tokens": tokens, "route_ids": route_ids, "router": router, "norm_gain": norm_gain, "w_in": w_in, "w_out": w_out, "cotangent": cotangent}


gelu_coef = 0.7978845608028654
cubic_coef = 0.044715
norm_eps = 1e-05

def gelu_tanh(value):
    inner = gelu_coef * (value + cubic_coef * value * value * value)
    return 0.5 * value * (1.0 + jnp.tanh(inner))

def gelu_slope(value):
    inner = gelu_coef * (value + cubic_coef * value * value * value)
    tangent = jnp.tanh(inner)
    return 0.5 * (1.0 + tangent) + 0.5 * value * (1.0 - tangent * tangent) * gelu_coef * (1.0 + 3.0 * cubic_coef * value * value)

def swap_heads(values):
    samples, token_count, model_width = values.shape
    head_size = model_width // token_count
    return values.reshape(samples, token_count, token_count, head_size).transpose(0, 2, 1, 3).reshape(samples, token_count, model_width)

def one_token(inputs):
    mixed_rows, route_rows, router_row, gain_row, weight_in, weight_out, cot_rows = inputs
    samples = mixed_rows.shape[0]
    model_width = mixed_rows.shape[1]
    experts = weight_in.shape[0]
    slot_rows = N_DP * CAP
    labels = jnp.arange(experts, dtype=jnp.int32)
    chosen = (route_rows[:, :, None] == labels[None, None, :]).astype(jnp.int32)
    flat_hot = chosen.reshape(samples * 2, experts)
    before = jnp.cumsum(flat_hot, axis=0, dtype=jnp.int32) - flat_hot
    slot_place = lax.optimization_barrier(jnp.sum(before * flat_hot, axis=1, dtype=jnp.int32)).reshape(samples, 2)
    chosen_f = chosen.astype(jnp.float32)
    logits = jnp.dot(mixed_rows, router_row, preferred_element_type=jnp.float32)
    picked = lax.optimization_barrier(jnp.sum(logits[:, None, :] * chosen_f, axis=2))
    gate_value = jax.nn.sigmoid(picked)
    doubled = jnp.broadcast_to(mixed_rows[:, None, :], (samples, 2, model_width))
    buffer = jnp.zeros((experts, slot_rows, model_width), jnp.bfloat16).at[route_rows, slot_place].set(doubled)
    pre_act = jnp.einsum('erd,edh->erh', buffer.astype(jnp.float32), weight_in.astype(jnp.float32))
    act_values = gelu_tanh(pre_act).astype(jnp.bfloat16)
    result = jnp.einsum('erh,ehd->erd', act_values.astype(jnp.float32), weight_out.astype(jnp.float32)).astype(jnp.bfloat16)
    routed_f = result[route_rows, slot_place].astype(jnp.float32)
    expert_sum = gate_value[:, 0:1] * routed_f[:, 0] + gate_value[:, 1:2] * routed_f[:, 1]
    residual = mixed_rows.astype(jnp.float32) + expert_sum
    row_mean = lax.optimization_barrier(jnp.mean(residual, axis=1, keepdims=True))
    centered = residual - row_mean
    row_var = lax.optimization_barrier(jnp.mean(centered * centered, axis=1, keepdims=True))
    inv_std = lax.rsqrt(row_var + norm_eps)
    normed = centered * inv_std
    normed_out = (normed * gain_row[None, :]).astype(jnp.bfloat16)
    cot_f = cot_rows.astype(jnp.float32)
    grad_gain = lax.optimization_barrier(jnp.sum(cot_f * normed, axis=0))
    grad_normed = cot_f * gain_row[None, :]
    grad_resid = inv_std * (grad_normed - lax.optimization_barrier(jnp.mean(grad_normed, axis=1, keepdims=True)) - normed * lax.optimization_barrier(jnp.mean(grad_normed * normed, axis=1, keepdims=True)))
    grad_rounded = lax.optimization_barrier(grad_resid.astype(jnp.bfloat16)).astype(jnp.float32)
    grad_exp_out = (gate_value[:, :, None] * grad_rounded[:, None, :]).astype(jnp.bfloat16)
    grad_buffer = jnp.zeros((experts, slot_rows, model_width), jnp.bfloat16).at[route_rows, slot_place].set(grad_exp_out)
    grad_gate = lax.optimization_barrier(jnp.sum(grad_resid[:, None, :] * routed_f, axis=2))
    grad_logit = grad_gate * gate_value * (1.0 - gate_value)
    route_grad = lax.optimization_barrier(jnp.sum(grad_logit[:, :, None] * chosen_f, axis=1))
    grad_buffer_f = grad_buffer.astype(jnp.float32)
    grad_act = jnp.einsum('erd,ehd->erh', grad_buffer_f, weight_out.astype(jnp.float32))
    grad_pre = (grad_act * gelu_slope(pre_act)).astype(jnp.bfloat16)
    grad_w_out = jnp.einsum('erh,erd->ehd', act_values.astype(jnp.float32), grad_buffer_f).astype(jnp.bfloat16)
    grad_w_in = jnp.einsum('erd,erh->edh', buffer.astype(jnp.float32), grad_pre.astype(jnp.float32)).astype(jnp.bfloat16)
    grad_input = jnp.einsum('erh,edh->erd', grad_pre.astype(jnp.float32), weight_in.astype(jnp.float32)).astype(jnp.bfloat16)
    grad_routed = grad_input[route_rows, slot_place].astype(jnp.float32)
    router_f = router_row.astype(jnp.float32)
    grad_mixed = grad_resid + grad_routed[:, 0] + grad_routed[:, 1] + jnp.dot(route_grad, router_f.T, precision=lax.Precision.HIGHEST)
    grad_router = jnp.dot(mixed_rows.astype(jnp.float32).T, route_grad, precision=lax.Precision.HIGHEST)
    return (normed_out, grad_mixed.astype(jnp.bfloat16), grad_router, grad_gain, grad_w_in, grad_w_out)

def reference(tokens, route_ids, router, norm_gain, w_in, w_out, cotangent):
    mixed_all = swap_heads(tokens).transpose(1, 0, 2)
    cot_all = cotangent.transpose(1, 0, 2)
    normed_out, grad_mixed, grad_router, grad_gain, grad_w_in, grad_w_out = lax.map(one_token, (mixed_all, route_ids, router, norm_gain, w_in, w_out, cot_all))
    normed_out = normed_out.transpose(1, 0, 2)
    grad_tokens = swap_heads(grad_mixed.transpose(1, 0, 2))
    return (normed_out, grad_tokens, grad_router, grad_gain, grad_w_in, grad_w_out)
```

```python
import functools

import jax
import jax.numpy as jnp
from jax import lax
from jax.experimental import pallas as pl
from jax.experimental.pallas import tpu as pltpu
from jax.sharding import PartitionSpec as P

MESH = pl.DeviceIdType.MESH
F32 = jnp.float32
BF16 = jnp.bfloat16

gelu_coef = 0.7978845608028654
cubic_coef = 0.044715
norm_eps = 1e-05

N = 16
NC = 4
NG = 4
RING = 8
STEPS = (0, 1, -1, 2, -2, 3, -3, 4)
BACK = (0, 2, 1, 4, 3, 6, 5, 7)
TILE = 32


def inverse(r):
    return 2 * BACK[r // 2] + r % 2


def dot(a, b):
    return lax.dot_general(a, b, (((1,), (0,)), ((), ())), preferred_element_type=F32)


def dot_nt(a, b):
    return lax.dot_general(a, b, (((1,), (1,)), ((), ())), preferred_element_type=F32)


def dot_tn(a, b):
    return lax.dot_general(a, b, (((0,), (0,)), ((), ())), preferred_element_type=F32)


def gelu_and_slope(value):
    inner = gelu_coef * (value + cubic_coef * value * value * value)
    tangent = jnp.tanh(inner)
    half = 0.5 * (1.0 + tangent)
    slope = half + 0.5 * value * (1.0 - tangent * tangent) * gelu_coef * (
        1.0 + 3.0 * cubic_coef * value * value
    )
    return value * half, slope


def kernel(
    tok_h, ids_ref, rt_ref, gain_ref, win_h, wout_h, cot_h,
    no_h, gt_h, gr_ref, gg_ref, gwi_h, gwo_h,
    tok, tok_t, mix_t, mixed, cot, win, wout, rt4, place_m, place_t,
    xs, xr, pre, logit, gate, act, ys, yr, acc, grd, gs, gr, gp, dos, ds, dr,
    norm_o, gwi, gwo, gm_t, gt_t, gt_o, ggp, rcol, small,
    gain_s, gain_r, col_s, col_r,
    load_sem, mix_ss, mix_rs, a_ss, a_rs, b_ss, b_rs, c_ss, c_rs, d_ss, d_rs,
    e_ss, e_rs, gn_ss, gn_rs, cl_ss, cl_rs, out_sem,
):
    rows, width = tok.shape
    head = width // N
    part = width // NC
    hidden = win.shape[1]
    depth = xs.shape[2]
    group = depth * 4
    slots = N * depth
    tokens4 = N // NC
    dp = lax.axis_index("dp")
    ex = lax.axis_index("expert")
    z, co = dp // 2, dp % 2
    xm, ym = ex // 4, ex % 4

    def partner(r):
        return ((z + STEPS[r // 2] + RING) % RING) * 2 + (co + r % 2) % 2

    def load(src, dst, k):
        copy = pltpu.make_async_copy(src, dst, load_sem.at[k])
        copy.start()
        return copy

    got_tok = load(tok_h, tok, 0)
    got_win = load(win_h, win, 1)
    got_wout = load(wout_h, wout, 2)
    got_cot = load(cot_h, cot, 3)

    barrier = pltpu.get_barrier_semaphore()
    for r in range(1, N):
        pl.semaphore_signal(barrier, inc=1, device_id=(partner(r), ex), device_id_type=MESH)
    for k in range(1, N):
        pl.semaphore_signal(barrier, inc=1, device_id=(dp, (ex + k) % N), device_id_type=MESH)
    got_tok.wait()
    tok_t[...] = tok[...].T.reshape(N, head, rows)
    pl.semaphore_wait(barrier, 2 * (N - 1))

    mix_cp = {}
    for i in range(NC):
        for yy in range(4):
            k = i * 4 + yy
            to = ((xm - i + 4) % 4) * 4 + (ym + yy) % 4
            if k == 0:
                mix_t[ex] = tok_t[ex]
                continue
            mix_cp[k] = pltpu.make_async_remote_copy(
                src_ref=tok_t.at[to], dst_ref=mix_t.at[ex],
                send_sem=mix_ss.at[k], recv_sem=mix_rs.at[k],
                device_id=(dp, to), device_id_type=MESH,
            )
            mix_cp[k].start()

    ids0, ids1 = ids_ref[0:1, :], ids_ref[1:2, :]
    label = lax.broadcasted_iota(jnp.int32, (N, rows), 0)
    hot0 = (label == ids0).astype(F32)
    hot1 = (label == ids1).astype(F32)
    earlier = (
        lax.broadcasted_iota(jnp.int32, (rows, rows), 0)
        < lax.broadcasted_iota(jnp.int32, (rows, rows), 1)
    ).astype(F32)
    before = dot((hot0 + hot1).astype(BF16), earlier.astype(BF16))
    at0 = jnp.sum(before * hot0, axis=0, keepdims=True).astype(jnp.int32)
    at1 = jnp.sum(before * hot1, axis=0, keepdims=True).astype(jnp.int32)
    slot = lax.broadcasted_iota(jnp.int32, (depth, rows), 0)
    for g in range(NG):
        blocks = []
        for r in range(4 * g, 4 * g + 4):
            e = partner(r)
            goal0 = jnp.where(ids0 == e, at0, -1)
            goal1 = jnp.where(ids1 == e, at1, -1)
            blocks.append(jnp.logical_or(slot == goal0, slot == goal1).astype(F32))
        placed = jnp.concatenate(blocks, axis=0)
        place_m[g * group : (g + 1) * group, :] = placed.astype(BF16)
        place_t[g] = placed.T.astype(BF16)
    for c in range(NC):
        rt4[c] = rt_ref[:, c * part : (c + 1) * part]

    a_cp = {}
    for i in range(NC):
        c = (xm + i) % 4
        for yy in range(4):
            if i * 4 + yy:
                mix_cp[i * 4 + yy].wait_recv()
        mixed[c] = mix_t[pl.ds(c * tokens4, tokens4)].reshape(part, rows).T
        sent = dot(place_m[...], mixed[c]).astype(BF16).reshape(N, depth, part)
        xs[:, c] = sent
        xr[0, c] = sent[0]
        for r in range(1, N):
            a_cp[r, i] = pltpu.make_async_remote_copy(
                src_ref=xs.at[r, c], dst_ref=xr.at[inverse(r), c],
                send_sem=a_ss.at[r, i], recv_sem=a_rs.at[inverse(r), i],
                device_id=(partner(r), ex), device_id_type=MESH,
            )
            a_cp[r, i].start()

    got_win.wait()
    got_wout.wait()
    mine = lax.broadcasted_iota(jnp.int32, (group, N), 1) == dp
    for i in range(NC - 1):
        c = (xm + i) % 4
        for r in range(1, N):
            a_cp[inverse(r), i].wait_recv()
        for g in range(NG):
            at = slice(g * group, (g + 1) * group)
            block = xr[4 * g : 4 * g + 4, c].reshape(group, part)
            more = dot(block, win[pl.ds(pl.multiple_of(c * part, part), part), :])
            more_logit = dot_nt(block, rt4[c])
            if i == 0:
                pre[at, :] = more
                logit[at, :] = more_logit
            else:
                pre[at, :] += more
                logit[at, :] += more_logit
    b_cp = {}
    c = (xm + NC - 1) % 4
    for g in range(NG):
        at = slice(g * group, (g + 1) * group)
        for r in range(4 * g, 4 * g + 4):
            if r:
                a_cp[inverse(r), NC - 1].wait_recv()
        block = xr[4 * g : 4 * g + 4, c].reshape(group, part)
        value = pre[at, :] + dot(block, win[pl.ds(pl.multiple_of(c * part, part), part), :])
        score = logit[at, :] + dot_nt(block, rt4[c])
        share = jax.nn.sigmoid(jnp.sum(jnp.where(mine, score, 0.0), axis=1, keepdims=True))
        gate[at, :] = share
        activated, slope = gelu_and_slope(value)
        pre[at, :] = slope
        act[at, :] = activated.astype(BF16)
        for q in range(NC):
            out = dot(act[at, :], wout[:, q * part : (q + 1) * part])
            result = (share * out).astype(BF16).reshape(4, depth, part)
            ys[4 * g : 4 * g + 4, q] = result
            if g == 0:
                yr[0, q] = result[0]
        for r in range(4 * g, 4 * g + 4):
            if r:
                b_cp[r] = pltpu.make_async_remote_copy(
                    src_ref=ys.at[r], dst_ref=yr.at[inverse(r)],
                    send_sem=b_ss.at[r], recv_sem=b_rs.at[inverse(r)],
                    device_id=(partner(r), ex), device_id_type=MESH,
                )
                b_cp[r].start()

    for q in range(NC):
        acc[q] = mixed[q].astype(F32)
    for g in range(NG):
        for r in range(4 * g, 4 * g + 4):
            if r:
                b_cp[inverse(r)].wait_recv()
        for q in range(NC):
            acc[q] += dot(place_t[g], yr[4 * g : 4 * g + 4, q].reshape(group, part))

    got_cot.wait()
    ggp[...] = jnp.zeros_like(ggp)

    def norm_rows(j, carry):
        at = pl.ds(pl.multiple_of(j * TILE, TILE), TILE)
        cols = [slice(q * part, (q + 1) * part) for q in range(NC)]
        resid = [acc[q, at, :] for q in range(NC)]
        mean = sum(jnp.sum(v, axis=1, keepdims=True) for v in resid) / width
        resid = [v - mean for v in resid]
        var = sum(jnp.sum(v * v, axis=1, keepdims=True) for v in resid) / width
        inv_std = lax.rsqrt(var + norm_eps)
        normed = [v * inv_std for v in resid]
        grads, m1, m2 = [], 0.0, 0.0
        for q in range(NC):
            gain = gain_ref[0:1, cols[q]]
            norm_o[at, cols[q]] = (normed[q] * gain).astype(BF16)
            cot_f = cot[at, cols[q]].astype(F32)
            ggp[0:1, cols[q]] += jnp.sum(cot_f * normed[q], axis=0, keepdims=True)
            grad = cot_f * gain
            grads.append(grad)
            m1 += jnp.sum(grad, axis=1, keepdims=True)
            m2 += jnp.sum(grad * normed[q], axis=1, keepdims=True)
        m1, m2 = m1 / width, m2 / width
        for q in range(NC):
            grad = inv_std * (grads[q] - m1 - normed[q] * m2)
            acc[q, at, :] = grad
            grd[q, at, :] = grad.astype(BF16)
        return carry

    lax.fori_loop(0, rows // TILE, norm_rows, 0)

    for q in range(NC):
        sent = dot(place_m[...], grd[q]).astype(BF16).reshape(N, depth, part)
        gs[:, q] = sent
        gr[0, q] = sent[0]
    c_cp = {}
    for r in range(1, N):
        c_cp[r] = pltpu.make_async_remote_copy(
            src_ref=gs.at[r], dst_ref=gr.at[inverse(r)],
            send_sem=c_ss.at[r], recv_sem=c_rs.at[inverse(r)],
            device_id=(partner(r), ex), device_id_type=MESH,
        )
        c_cp[r].start()

    def spread(vector, source, target, gathered, send_sems, recv_sems):
        source[...] = jnp.zeros_like(source)
        for j in range(width // 128):
            source[j : j + 1, :] = vector[0:1, j * 128 : (j + 1) * 128]
        target[...] = source[...].astype(BF16)
        gathered[dp] = target[...]
        copies = {}
        for r in range(1, N):
            copies[r] = pltpu.make_async_remote_copy(
                src_ref=target, dst_ref=gathered.at[dp],
                send_sem=send_sems.at[r], recv_sem=recv_sems.at[inverse(r)],
                device_id=(partner(r), ex), device_id_type=MESH,
            )
            copies[r].start()
        return copies

    gn_cp = spread(ggp, small, gain_s, gain_r, gn_ss, gn_rs)
    put_norm = pltpu.make_async_copy(norm_o, no_h, out_sem.at[0])
    put_norm.start()

    rcol[...] = jnp.zeros_like(rcol)
    mine_row = lax.broadcasted_iota(jnp.int32, (N, part), 0) == dp
    d_cp = {}

    def send_back(r, i):
        c = (xm + 1 + i) % 4
        d_cp[r, i] = pltpu.make_async_remote_copy(
            src_ref=ds.at[r, c], dst_ref=dr.at[inverse(r), c],
            send_sem=d_ss.at[r, i], recv_sem=d_rs.at[inverse(r), i],
            device_id=(partner(r), ex), device_id_type=MESH,
        )
        d_cp[r, i].start()

    for g in range(NG):
        at = slice(g * group, (g + 1) * group)
        for r in range(4 * g, 4 * g + 4):
            if r:
                c_cp[inverse(r)].wait_recv()
        share = gate[at, :]
        grad_act, grad_gate = 0.0, 0.0
        for q in range(NC):
            grad = gr[4 * g : 4 * g + 4, q].reshape(group, part).astype(F32)
            result = ys[4 * g : 4 * g + 4, q].reshape(group, part).astype(F32)
            grad_gate += jnp.sum(grad * result, axis=1, keepdims=True)
            grad_out = (share * grad).astype(BF16)
            dos[q, at, :] = grad_out
            grad_act += dot_nt(grad_out, wout[:, q * part : (q + 1) * part])
        grad_logit = grad_gate * (1.0 - share)
        gp[at, :] = (grad_act * pre[at, :]).astype(BF16)
        for q in range(NC):
            weights = jnp.sum(jnp.where(mine_row, rt4[q].astype(F32), 0.0), axis=0, keepdims=True)
            back = dot_nt(gp[at, :], win[q * part : (q + 1) * part, :]) + grad_logit * weights
            back = back.astype(BF16).reshape(4, depth, part)
            ds[4 * g : 4 * g + 4, q] = back
            if g == 0:
                dr[0, q] = back[0]
            block = xr[4 * g : 4 * g + 4, q].reshape(group, part).astype(F32)
            rcol[0:1, q * part : (q + 1) * part] += jnp.sum(
                grad_logit * block, axis=0, keepdims=True
            )
        for i in range(2):
            for r in range(4 * g, 4 * g + 4):
                if r:
                    send_back(r, i)
    for i in range(2, NC):
        for r in range(1, N):
            send_back(r, i)
    cl_cp = spread(rcol, small, col_s, col_r, cl_ss, cl_rs)

    for q in range(NC):
        cols = slice(q * part, (q + 1) * part)
        gwi[cols, :] = dot_tn(xr[:, q].reshape(slots, part), gp[...]).astype(BF16)
        gwo[:, cols] = dot_tn(act[...], dos[q]).astype(BF16)
    put_gwi = pltpu.make_async_copy(gwi, gwi_h, out_sem.at[1])
    put_gwi.start()
    put_gwo = pltpu.make_async_copy(gwo, gwo_h, out_sem.at[2])
    put_gwo.start()

    e_cp = {}
    for i in range(NC):
        c = (xm + 1 + i) % 4
        for r in range(1, N):
            d_cp[inverse(r), i].wait_recv()
        total = acc[c]
        for g in range(NG):
            total += dot(place_t[g], dr[4 * g : 4 * g + 4, c].reshape(group, part))
        gm_t[pl.ds(c * tokens4, tokens4)] = total.astype(BF16).T.reshape(tokens4, head, rows)
        for yy in range(4):
            to = c * tokens4 + (ym + yy) % 4
            if i == NC - 1 and yy == 0:
                gt_t[ex] = gm_t[ex]
                continue
            k = i * 4 + yy
            e_cp[k] = pltpu.make_async_remote_copy(
                src_ref=gm_t.at[to], dst_ref=gt_t.at[ex],
                send_sem=e_ss.at[k], recv_sem=e_rs.at[k],
                device_id=(dp, to), device_id_type=MESH,
            )
            e_cp[k].start()

    for r in range(1, N):
        gn_cp[inverse(r)].wait_recv()
        cl_cp[inverse(r)].wait_recv()
    total = gain_r[0].astype(F32)
    for e in range(1, N):
        total += gain_r[e].astype(F32)
    small[...] = total
    for j in range(width // 128):
        gg_ref[0:1, j * 128 : (j + 1) * 128] = small[j : j + 1, :]
    for e in range(N):
        small[...] = col_r[e].astype(F32)
        for j in range(width // 128):
            gr_ref[e : e + 1, j * 128 : (j + 1) * 128] = small[j : j + 1, :]

    for k in e_cp:
        e_cp[k].wait_recv()
    gt_o[...] = gt_t[...].reshape(width, rows).T
    put_gt = pltpu.make_async_copy(gt_o, gt_h, out_sem.at[3])
    put_gt.start()
    for copies in (mix_cp, a_cp, b_cp, c_cp, d_cp, e_cp, gn_cp, cl_cp):
        for k in copies:
            copies[k].wait_send()
    put_norm.wait()
    put_gwi.wait()
    put_gwo.wait()
    put_gt.wait()


def body(tokens, route_ids, router, norm_gain, w_in, w_out, cotangent):
    rows, width = tokens.shape[0], tokens.shape[2]
    hidden = w_in.shape[3]
    depth = 3 * rows // N
    slots = N * depth
    part = width // NC
    head = width // N
    group = 4 * depth
    shape = jax.ShapeDtypeStruct
    vmem = pl.BlockSpec(memory_space=pltpu.VMEM)
    hbm = pl.BlockSpec(memory_space=pl.ANY)
    dma = pltpu.SemaphoreType.DMA
    blocks = pltpu.VMEM((N, NC, depth, part), BF16)
    flipped = pltpu.VMEM((N, head, rows), BF16)
    row_block = pltpu.VMEM((rows, width), BF16)
    out = pl.pallas_call(
        kernel,
        out_shape=(
            shape((rows, width), BF16),
            shape((rows, width), BF16),
            shape((N, width), F32),
            shape((1, width), F32),
            shape((width, hidden), BF16),
            shape((hidden, width), BF16),
        ),
        in_specs=[hbm, vmem, vmem, vmem, hbm, hbm, hbm],
        out_specs=[hbm, hbm, vmem, vmem, hbm, hbm],
        scratch_shapes=[
            row_block,
            flipped,
            flipped,
            pltpu.VMEM((NC, rows, part), BF16),
            row_block,
            pltpu.VMEM((width, hidden), BF16),
            pltpu.VMEM((hidden, width), BF16),
            pltpu.VMEM((NC, N, part), BF16),
            pltpu.VMEM((slots, rows), BF16),
            pltpu.VMEM((NG, rows, group), BF16),
            blocks,
            blocks,
            pltpu.VMEM((slots, hidden), F32),
            pltpu.VMEM((slots, N), F32),
            pltpu.VMEM((slots, 1), F32),
            pltpu.VMEM((slots, hidden), BF16),
            blocks,
            blocks,
            pltpu.VMEM((NC, rows, part), F32),
            pltpu.VMEM((NC, rows, part), BF16),
            blocks,
            blocks,
            pltpu.VMEM((slots, hidden), BF16),
            pltpu.VMEM((NC, slots, part), BF16),
            blocks,
            blocks,
            row_block,
            pltpu.VMEM((width, hidden), BF16),
            pltpu.VMEM((hidden, width), BF16),
            flipped,
            flipped,
            row_block,
            pltpu.VMEM((8, width), F32),
            pltpu.VMEM((8, width), F32),
            pltpu.VMEM((16, 128), F32),
            pltpu.VMEM((16, 128), BF16),
            pltpu.VMEM((N, 16, 128), BF16),
            pltpu.VMEM((16, 128), BF16),
            pltpu.VMEM((N, 16, 128), BF16),
            dma((4,)),
            dma((N,)), dma((N,)),
            dma((N, NC)), dma((N, NC)),
            dma((N,)), dma((N,)),
            dma((N,)), dma((N,)),
            dma((N, NC)), dma((N, NC)),
            dma((N,)), dma((N,)),
            dma((N,)), dma((N,)),
            dma((N,)), dma((N,)),
            dma((4,)),
        ],
        name="rank_mixer",
        compiler_params=pltpu.CompilerParams(
            collective_id=0, has_side_effects=True, vmem_limit_bytes=60 << 20
        ),
    )(
        tokens.reshape(rows, width),
        route_ids.reshape(rows, 2).T,
        router.reshape(width, N).T,
        norm_gain.reshape(1, width),
        w_in.reshape(width, hidden),
        w_out.reshape(hidden, width),
        cotangent.reshape(rows, width),
    )
    normed_out, grad_tokens, grad_router, grad_gain, grad_w_in, grad_w_out = out
    return (
        normed_out.reshape(rows, 1, width),
        grad_tokens.reshape(rows, 1, width),
        grad_router.T.reshape(1, width, N),
        grad_gain,
        grad_w_in.reshape(1, 1, width, hidden),
        grad_w_out.reshape(1, 1, hidden, width),
    )


def solution(mesh):
    return jax.shard_map(
        body,
        mesh=mesh,
        in_specs=(
            P("dp", "expert", None),
            P("expert", "dp", None),
            P("expert", None, None),
            P("expert", None),
            P("expert", "dp", None, None),
            P("expert", "dp", None, None),
            P("dp", "expert", None),
        ),
        out_specs=(
            P("dp", "expert", None),
            P("dp", "expert", None),
            P("expert", None, None),
            P("expert", None),
            P("expert", "dp", None, None),
            P("expert", "dp", None, None),
        ),
        check_vma=False,
    )
```

```python
import functools

import jax
import jax.numpy as jnp
from jax import lax
from jax.experimental import pallas as pl
from jax.experimental.pallas import tpu as pltpu
from jax.sharding import PartitionSpec as P

MESH = pl.DeviceIdType.MESH
F32 = jnp.float32
BF16 = jnp.bfloat16

gelu_coef = 0.7978845608028654
cubic_coef = 0.044715
norm_eps = 1e-05

N = 16
NC = 4
NG = 4
RING = 8
STEPS = (0, 1, -1, 2, -2, 3, -3, 4)
BACK = (0, 2, 1, 4, 3, 6, 5, 7)
HOPS = (0, 0, 0, 0, 0, 0, -1, -1, 1, 1, -2, -2, 2, 2, 3, -3)
FROM_LOW = (4, 5, 8, 9, 12, 13, 14)
FROM_HIGH = (2, 3, 6, 7, 10, 11, 15)
OWN = (0, 1)
HERE = (0, 2, 4)
AWAY = tuple(r for r in range(N) if r not in HERE)
TILE = 32
RUNS = 4


def inverse(r):
    return 2 * BACK[r // 2] + r % 2


def dot(a, b):
    return lax.dot_general(a, b, (((1,), (0,)), ((), ())), preferred_element_type=F32)


def dot_nt(a, b):
    return lax.dot_general(a, b, (((1,), (1,)), ((), ())), preferred_element_type=F32)


def dot_tn(a, b):
    return lax.dot_general(a, b, (((0,), (0,)), ((), ())), preferred_element_type=F32)


def gelu_and_slope(value):
    inner = gelu_coef * (value + cubic_coef * value * value * value)
    tangent = jnp.tanh(inner)
    half = 0.5 * (1.0 + tangent)
    slope = half + 0.5 * value * (1.0 - tangent * tangent) * gelu_coef * (
        1.0 + 3.0 * cubic_coef * value * value
    )
    return value * half, slope


def kernel(
    tok_h, ids_ref, rt_ref, gain_ref, win_h, wout_h, cot_h,
    no_h, gt_h, gr_ref, gg_ref, gwi_h, gwo_h,
    tok, tok_t, mix_t, mixed, cot, win, wout, rt4,
    ids_o, ids_l, ids_h, pl_m, ph_m, po_m, pl_t, ph_t, po_t,
    raw_l, raw_h, xs, xr, pre, logit, gate, act, ys, yr,
    part_l, part_h, sum_h, sum_l, acc, grd, raw2_l, raw2_h, gs, gr, gp, dos, ds, dr,
    part2_l, part2_h, sum2_h, sum2_l,
    norm_o, gwi, gwo, gm_t, gt_t, gt_o, ggp, rcol, small,
    gain_s, gain_r, col_s, col_r,
    load_sem, ids_ss, ids_rs, mix_ss, mix_rs, raw_ss, raw_rs, a_ss, a_rs, b_ss, b_rs,
    sum_ss, sum_rs, raw2_ss, raw2_rs, c_ss, c_rs, d_ss, d_rs, sum2_ss, sum2_rs,
    e_ss, e_rs, gn_ss, gn_rs, cl_ss, cl_rs, out_sem,
):
    rows, width = tok.shape
    head = width // N
    part = width // NC
    hidden = win.shape[1]
    depth = xs.shape[2]
    group = depth * 4
    slots = N * depth
    tokens4 = N // NC
    dp = lax.axis_index("dp")
    ex = lax.axis_index("expert")
    z, co = dp // 2, dp % 2
    xm, ym = ex // 4, ex % 4

    def partner(r):
        return ((z + STEPS[r // 2] + RING) % RING) * 2 + (co + r % 2) % 2

    def target(r):
        return ((z + HOPS[r] + RING) % RING) * 2 + (co + r % 2) % 2

    def origin(r):
        return ((z - HOPS[r] + RING) % RING) * 2 + (co + r % 2) % 2

    high = ((z + 1) % RING) * 2 + co
    low = ((z + RING - 1) % RING) * 2 + co

    def send(src, dst, send_sem, recv_sem, to):
        copy = pltpu.make_async_remote_copy(
            src_ref=src, dst_ref=dst, send_sem=send_sem, recv_sem=recv_sem,
            device_id=(to, ex), device_id_type=MESH,
        )
        copy.start()
        return copy

    def load(src, dst, k):
        copy = pltpu.make_async_copy(src, dst, load_sem.at[k])
        copy.start()
        return copy

    got_tok = load(tok_h, tok, 0)
    got_win = load(win_h, win, 1)
    got_wout = load(wout_h, wout, 2)
    got_cot = load(cot_h, cot, 3)

    barrier = pltpu.get_barrier_semaphore()
    for r in range(1, N):
        pl.semaphore_signal(barrier, inc=1, device_id=(partner(r), ex), device_id_type=MESH)
    for k in range(1, N):
        pl.semaphore_signal(barrier, inc=1, device_id=(dp, (ex + k) % N), device_id_type=MESH)
    got_tok.wait()
    tok_t[...] = tok[...].T.reshape(N, head, rows)
    ids_o[...] = jnp.zeros_like(ids_o)
    ids_o[0:2, :] = ids_ref[...]
    pl.semaphore_wait(barrier, 2 * (N - 1))
    ids_cp = {
        0: send(ids_o, ids_l, ids_ss.at[0], ids_rs.at[0], high),
        1: send(ids_o, ids_h, ids_ss.at[1], ids_rs.at[1], low),
    }

    mix_cp = {}
    for i in range(NC):
        for yy in range(4):
            k = i * 4 + yy
            to = ((xm - i + 4) % 4) * 4 + (ym + yy) % 4
            if k == 0:
                mix_t[ex] = tok_t[ex]
                continue
            mix_cp[k] = pltpu.make_async_remote_copy(
                src_ref=tok_t.at[to], dst_ref=mix_t.at[ex],
                send_sem=mix_ss.at[k], recv_sem=mix_rs.at[k],
                device_id=(dp, to), device_id_type=MESH,
            )
            mix_cp[k].start()

    label = lax.broadcasted_iota(jnp.int32, (N, rows), 0)
    earlier = (
        lax.broadcasted_iota(jnp.int32, (rows, rows), 0)
        < lax.broadcasted_iota(jnp.int32, (rows, rows), 1)
    ).astype(F32)
    earlier = earlier.astype(BF16)
    slot = lax.broadcasted_iota(jnp.int32, (depth, rows), 0)

    def place(ids, members, matrix, flipped):
        ids0, ids1 = ids[0:1, :], ids[1:2, :]
        hot0 = (label == ids0).astype(F32)
        hot1 = (label == ids1).astype(F32)
        before = dot((hot0 + hot1).astype(BF16), earlier)
        at0 = jnp.sum(before * hot0, axis=0, keepdims=True).astype(jnp.int32)
        at1 = jnp.sum(before * hot1, axis=0, keepdims=True).astype(jnp.int32)
        blocks = []
        for r in members:
            e = target(r)
            goal0 = jnp.where(ids0 == e, at0, -1)
            goal1 = jnp.where(ids1 == e, at1, -1)
            blocks.append(jnp.logical_or(slot == goal0, slot == goal1).astype(F32))
        placed = jnp.concatenate(blocks, axis=0)
        matrix[...] = placed.astype(BF16)
        flipped[...] = placed.T.astype(BF16)

    def stack(blocks, members, q):
        return jnp.concatenate([blocks[r, q] for r in members], axis=0)

    def expand(matrix, values, members, q, out, arrived):
        sent = dot(matrix[...], values).astype(BF16)
        for n, r in enumerate(members):
            into = arrived if r in HERE else out
            into[r, q] = sent[n * depth : (n + 1) * depth]

    place(ids_o, OWN, po_m, po_t)
    for c in range(NC):
        rt4[c] = rt_ref[:, c * part : (c + 1) * part]
    ids_cp[0].wait_recv()
    ids_cp[1].wait_recv()
    place(ids_l, FROM_LOW, pl_m, pl_t)
    place(ids_h, FROM_HIGH, ph_m, ph_t)

    raw_cp, a_cp = {}, {}

    def send_mixed(r, i):
        c = (xm + i) % 4
        a_cp[r, i] = send(xs.at[r, c], xr.at[r, c], a_ss.at[r, i], a_rs.at[r, i], target(r))

    def mix_chunk(i):
        c = (xm + i) % 4
        for yy in range(4):
            if i * 4 + yy:
                mix_cp[i * 4 + yy].wait_recv()
        mixed[c] = mix_t[pl.ds(c * tokens4, tokens4)].reshape(part, rows).T
        raw_cp[0, i] = send(mixed.at[c], raw_l.at[c], raw_ss.at[0, i], raw_rs.at[0, i], high)
        raw_cp[1, i] = send(mixed.at[c], raw_h.at[c], raw_ss.at[1, i], raw_rs.at[1, i], low)
        expand(po_m, mixed[c], OWN, c, xs, xr)
        send_mixed(1, i)

    def pass_on(i):
        c = (xm + i) % 4
        raw_cp[0, i].wait_recv()
        expand(pl_m, raw_l[c], FROM_LOW, c, xs, xr)
        raw_cp[1, i].wait_recv()
        expand(ph_m, raw_h[c], FROM_HIGH, c, xs, xr)
        for r in AWAY[1:]:
            send_mixed(r, i)

    for i in range(NC):
        mix_chunk(i)
        if i:
            pass_on(i - 1)
    pass_on(NC - 1)

    got_win.wait()
    got_wout.wait()
    mine = lax.broadcasted_iota(jnp.int32, (group, N), 1) == dp
    for i in range(NC - 1):
        c = (xm + i) % 4
        for r in AWAY:
            a_cp[r, i].wait_recv()
        for g in range(NG):
            at = slice(g * group, (g + 1) * group)
            block = xr[4 * g : 4 * g + 4, c].reshape(group, part)
            more = dot(block, win[pl.ds(pl.multiple_of(c * part, part), part), :])
            more_logit = dot_nt(block, rt4[c])
            if i == 0:
                pre[at, :] = more
                logit[at, :] = more_logit
            else:
                pre[at, :] += more
                logit[at, :] += more_logit
    b_cp = {}
    c = (xm + NC - 1) % 4
    for g in range(NG):
        at = slice(g * group, (g + 1) * group)
        for r in range(4 * g, 4 * g + 4):
            if r in AWAY:
                a_cp[r, NC - 1].wait_recv()
        block = xr[4 * g : 4 * g + 4, c].reshape(group, part)
        value = pre[at, :] + dot(block, win[pl.ds(pl.multiple_of(c * part, part), part), :])
        score = logit[at, :] + dot_nt(block, rt4[c])
        share = jax.nn.sigmoid(jnp.sum(jnp.where(mine, score, 0.0), axis=1, keepdims=True))
        gate[at, :] = share
        activated, slope = gelu_and_slope(value)
        pre[at, :] = slope
        act[at, :] = activated.astype(BF16)
        for q in range(NC):
            out = dot(act[at, :], wout[:, q * part : (q + 1) * part])
            result = (share * out).astype(BF16).reshape(4, depth, part)
            ys[4 * g : 4 * g + 4, q] = result
            for r in range(4 * g, 4 * g + 4):
                if r in HERE:
                    yr[r, q] = result[r - 4 * g]
        for r in range(4 * g, 4 * g + 4):
            if r in AWAY:
                b_cp[r] = send(ys.at[r], yr.at[r], b_ss.at[r], b_rs.at[r], origin(r))

    sum_cp = {}
    for r in AWAY:
        b_cp[r].wait_recv()
    for q in range(NC):
        part_l[q] = dot(pl_t[...], stack(yr, FROM_LOW, q)).astype(BF16)
        sum_cp[0, q] = send(part_l.at[q], sum_h.at[q], sum_ss.at[0, q], sum_rs.at[0, q], low)
        part_h[q] = dot(ph_t[...], stack(yr, FROM_HIGH, q)).astype(BF16)
        sum_cp[1, q] = send(part_h.at[q], sum_l.at[q], sum_ss.at[1, q], sum_rs.at[1, q], high)
    for q in range(NC):
        acc[q] = mixed[q].astype(F32) + dot(po_t[...], stack(yr, OWN, q))
    got_cot.wait()
    ggp[...] = jnp.zeros_like(ggp)

    def norm_rows(j, carry):
        at = pl.ds(pl.multiple_of(j * TILE, TILE), TILE)
        cols = [slice(q * part, (q + 1) * part) for q in range(NC)]
        resid = [
            acc[q, at, :] + sum_h[q, at, :].astype(F32) + sum_l[q, at, :].astype(F32)
            for q in range(NC)
        ]
        mean = sum(jnp.sum(v, axis=1, keepdims=True) for v in resid) / width
        resid = [v - mean for v in resid]
        var = sum(jnp.sum(v * v, axis=1, keepdims=True) for v in resid) / width
        inv_std = lax.rsqrt(var + norm_eps)
        normed = [v * inv_std for v in resid]
        grads, m1, m2 = [], 0.0, 0.0
        for q in range(NC):
            gain = gain_ref[0:1, cols[q]]
            norm_o[at, cols[q]] = (normed[q] * gain).astype(BF16)
            cot_f = cot[at, cols[q]].astype(F32)
            ggp[0:1, cols[q]] += jnp.sum(cot_f * normed[q], axis=0, keepdims=True)
            grad = cot_f * gain
            grads.append(grad)
            m1 += jnp.sum(grad, axis=1, keepdims=True)
            m2 += jnp.sum(grad * normed[q], axis=1, keepdims=True)
        m1, m2 = m1 / width, m2 / width
        for q in range(NC):
            grad = inv_std * (grads[q] - m1 - normed[q] * m2)
            acc[q, at, :] = grad
            grd[q, at, :] = grad.astype(BF16)
        return carry

    for q in range(NC):
        sum_cp[0, q].wait_recv()
        sum_cp[1, q].wait_recv()

    raw2_cp, c_cp = {}, {}
    run = rows // RUNS
    for i in range(RUNS):
        lax.fori_loop(i * run // TILE, (i + 1) * run // TILE, norm_rows, 0)
        src = grd.at[:, i * run : (i + 1) * run, :]
        to_high, to_low = (d.at[:, i * run : (i + 1) * run, :] for d in (raw2_l, raw2_h))
        raw2_cp[0, i] = send(src, to_high, raw2_ss.at[0, i], raw2_rs.at[0, i], high)
        raw2_cp[1, i] = send(src, to_low, raw2_ss.at[1, i], raw2_rs.at[1, i], low)

    def spread(vector, source, target, gathered, send_sems, recv_sems):
        source[...] = jnp.zeros_like(source)
        for j in range(width // 128):
            source[j : j + 1, :] = vector[0:1, j * 128 : (j + 1) * 128]
        target[...] = source[...].astype(BF16)
        gathered[dp] = target[...]
        copies = {}
        for r in range(1, N):
            copies[r] = pltpu.make_async_remote_copy(
                src_ref=target, dst_ref=gathered.at[dp],
                send_sem=send_sems.at[r], recv_sem=recv_sems.at[inverse(r)],
                device_id=(partner(r), ex), device_id_type=MESH,
            )
            copies[r].start()
        return copies

    gn_cp = spread(ggp, small, gain_s, gain_r, gn_ss, gn_rs)
    put_norm = pltpu.make_async_copy(norm_o, no_h, out_sem.at[0])
    put_norm.start()
    for q in range(NC):
        expand(po_m, grd[q], OWN, q, gs, gr)
    for i in range(RUNS):
        raw2_cp[0, i].wait_recv()
        raw2_cp[1, i].wait_recv()
    for q in range(NC):
        expand(pl_m, raw2_l[q], FROM_LOW, q, gs, gr)
        expand(ph_m, raw2_h[q], FROM_HIGH, q, gs, gr)
    for r in AWAY:
        c_cp[r] = send(gs.at[r], gr.at[r], c_ss.at[r], c_rs.at[r], target(r))

    rcol[...] = jnp.zeros_like(rcol)
    mine_row = lax.broadcasted_iota(jnp.int32, (N, part), 0) == dp
    d_cp = {}

    def send_back(r, i):
        c = (xm + 1 + i) % 4
        d_cp[r, i] = send(ds.at[r, c], dr.at[r, c], d_ss.at[r, i], d_rs.at[r, i], origin(r))

    for g in range(NG):
        at = slice(g * group, (g + 1) * group)
        for r in range(4 * g, 4 * g + 4):
            if r in AWAY:
                c_cp[r].wait_recv()
        share = gate[at, :]
        grad_act, grad_gate = 0.0, 0.0
        for q in range(NC):
            grad = gr[4 * g : 4 * g + 4, q].reshape(group, part).astype(F32)
            result = ys[4 * g : 4 * g + 4, q].reshape(group, part).astype(F32)
            grad_gate += jnp.sum(grad * result, axis=1, keepdims=True)
            grad_out = (share * grad).astype(BF16)
            dos[q, at, :] = grad_out
            grad_act += dot_nt(grad_out, wout[:, q * part : (q + 1) * part])
        grad_logit = grad_gate * (1.0 - share)
        gp[at, :] = (grad_act * pre[at, :]).astype(BF16)
        for q in range(NC):
            weights = jnp.sum(jnp.where(mine_row, rt4[q].astype(F32), 0.0), axis=0, keepdims=True)
            back = dot_nt(gp[at, :], win[q * part : (q + 1) * part, :]) + grad_logit * weights
            back = back.astype(BF16).reshape(4, depth, part)
            ds[4 * g : 4 * g + 4, q] = back
            for r in range(4 * g, 4 * g + 4):
                if r in HERE:
                    dr[r, q] = back[r - 4 * g]
            block = xr[4 * g : 4 * g + 4, q].reshape(group, part).astype(F32)
            rcol[0:1, q * part : (q + 1) * part] += jnp.sum(
                grad_logit * block, axis=0, keepdims=True
            )
        for i in range(2):
            for r in range(4 * g, 4 * g + 4):
                if r in AWAY:
                    send_back(r, i)
    for i in range(2, NC):
        for r in AWAY:
            send_back(r, i)
    cl_cp = spread(rcol, small, col_s, col_r, cl_ss, cl_rs)

    for q in range(NC):
        cols = slice(q * part, (q + 1) * part)
        gwi[cols, :] = dot_tn(xr[:, q].reshape(slots, part), gp[...]).astype(BF16)
        gwo[:, cols] = dot_tn(act[...], dos[q]).astype(BF16)
    put_gwi = pltpu.make_async_copy(gwi, gwi_h, out_sem.at[1])
    put_gwi.start()
    put_gwo = pltpu.make_async_copy(gwo, gwo_h, out_sem.at[2])
    put_gwo.start()

    sum2_cp, e_cp = {}, {}

    def sum_back(i):
        c = (xm + 1 + i) % 4
        for r in AWAY:
            d_cp[r, i].wait_recv()
        part2_l[c] = dot(pl_t[...], stack(dr, FROM_LOW, c)).astype(BF16)
        sum2_cp[0, i] = send(part2_l.at[c], sum2_h.at[c], sum2_ss.at[0, i], sum2_rs.at[0, i], low)
        part2_h[c] = dot(ph_t[...], stack(dr, FROM_HIGH, c)).astype(BF16)
        sum2_cp[1, i] = send(part2_h.at[c], sum2_l.at[c], sum2_ss.at[1, i], sum2_rs.at[1, i], high)
        acc[c] += dot(po_t[...], stack(dr, OWN, c))

    def finish_chunk(i):
        c = (xm + 1 + i) % 4
        sum2_cp[0, i].wait_recv()
        sum2_cp[1, i].wait_recv()
        total = acc[c] + sum2_h[c].astype(F32) + sum2_l[c].astype(F32)
        gm_t[pl.ds(c * tokens4, tokens4)] = total.astype(BF16).T.reshape(tokens4, head, rows)
        for yy in range(4):
            to = c * tokens4 + (ym + yy) % 4
            if i == NC - 1 and yy == 0:
                gt_t[ex] = gm_t[ex]
                continue
            k = i * 4 + yy
            e_cp[k] = pltpu.make_async_remote_copy(
                src_ref=gm_t.at[to], dst_ref=gt_t.at[ex],
                send_sem=e_ss.at[k], recv_sem=e_rs.at[k],
                device_id=(dp, to), device_id_type=MESH,
            )
            e_cp[k].start()

    for i in range(NC):
        sum_back(i)
        if i:
            finish_chunk(i - 1)
    finish_chunk(NC - 1)

    for r in range(1, N):
        gn_cp[inverse(r)].wait_recv()
        cl_cp[inverse(r)].wait_recv()
    total = gain_r[0].astype(F32)
    for e in range(1, N):
        total += gain_r[e].astype(F32)
    small[...] = total
    for j in range(width // 128):
        gg_ref[0:1, j * 128 : (j + 1) * 128] = small[j : j + 1, :]
    for e in range(N):
        small[...] = col_r[e].astype(F32)
        for j in range(width // 128):
            gr_ref[e : e + 1, j * 128 : (j + 1) * 128] = small[j : j + 1, :]

    for k in e_cp:
        e_cp[k].wait_recv()
    gt_o[...] = gt_t[...].reshape(width, rows).T
    put_gt = pltpu.make_async_copy(gt_o, gt_h, out_sem.at[3])
    put_gt.start()
    for copies in (
        ids_cp, mix_cp, raw_cp, a_cp, b_cp, sum_cp, raw2_cp, c_cp, d_cp, sum2_cp, e_cp, gn_cp, cl_cp,
    ):
        for k in copies:
            copies[k].wait_send()
    put_norm.wait()
    put_gwi.wait()
    put_gwo.wait()
    put_gt.wait()


def body(tokens, route_ids, router, norm_gain, w_in, w_out, cotangent):
    rows, width = tokens.shape[0], tokens.shape[2]
    hidden = w_in.shape[3]
    depth = 3 * rows // N
    slots = N * depth
    part = width // NC
    head = width // N
    group = 4 * depth
    shape = jax.ShapeDtypeStruct
    vmem = pl.BlockSpec(memory_space=pltpu.VMEM)
    hbm = pl.BlockSpec(memory_space=pl.ANY)
    dma = pltpu.SemaphoreType.DMA
    blocks = pltpu.VMEM((N, NC, depth, part), BF16)
    flipped = pltpu.VMEM((N, head, rows), BF16)
    row_block = pltpu.VMEM((rows, width), BF16)
    chunks = pltpu.VMEM((NC, rows, part), BF16)
    ids = pltpu.VMEM((8, rows), jnp.int32)
    out = pl.pallas_call(
        kernel,
        out_shape=(
            shape((rows, width), BF16),
            shape((rows, width), BF16),
            shape((N, width), F32),
            shape((1, width), F32),
            shape((width, hidden), BF16),
            shape((hidden, width), BF16),
        ),
        in_specs=[hbm, vmem, vmem, vmem, hbm, hbm, hbm],
        out_specs=[hbm, hbm, vmem, vmem, hbm, hbm],
        scratch_shapes=[
            row_block,
            flipped,
            flipped,
            chunks,
            row_block,
            pltpu.VMEM((width, hidden), BF16),
            pltpu.VMEM((hidden, width), BF16),
            pltpu.VMEM((NC, N, part), BF16),
            ids, ids, ids,
            pltpu.VMEM((7 * depth, rows), BF16),
            pltpu.VMEM((7 * depth, rows), BF16),
            pltpu.VMEM((2 * depth, rows), BF16),
            pltpu.VMEM((rows, 7 * depth), BF16),
            pltpu.VMEM((rows, 7 * depth), BF16),
            pltpu.VMEM((rows, 2 * depth), BF16),
            chunks, chunks,
            blocks,
            blocks,
            pltpu.VMEM((slots, hidden), F32),
            pltpu.VMEM((slots, N), F32),
            pltpu.VMEM((slots, 1), F32),
            pltpu.VMEM((slots, hidden), BF16),
            blocks,
            blocks,
            chunks, chunks, chunks, chunks,
            pltpu.VMEM((NC, rows, part), F32),
            chunks,
            chunks, chunks,
            blocks,
            blocks,
            pltpu.VMEM((slots, hidden), BF16),
            pltpu.VMEM((NC, slots, part), BF16),
            blocks,
            blocks,
            chunks, chunks, chunks, chunks,
            row_block,
            pltpu.VMEM((width, hidden), BF16),
            pltpu.VMEM((hidden, width), BF16),
            flipped,
            flipped,
            row_block,
            pltpu.VMEM((8, width), F32),
            pltpu.VMEM((8, width), F32),
            pltpu.VMEM((16, 128), F32),
            pltpu.VMEM((16, 128), BF16),
            pltpu.VMEM((N, 16, 128), BF16),
            pltpu.VMEM((16, 128), BF16),
            pltpu.VMEM((N, 16, 128), BF16),
            dma((4,)),
            dma((2,)), dma((2,)),
            dma((N,)), dma((N,)),
            dma((2, NC)), dma((2, NC)),
            dma((N, NC)), dma((N, NC)),
            dma((N,)), dma((N,)),
            dma((2, NC)), dma((2, NC)),
            dma((2, RUNS)), dma((2, RUNS)),
            dma((N,)), dma((N,)),
            dma((N, NC)), dma((N, NC)),
            dma((2, NC)), dma((2, NC)),
            dma((N,)), dma((N,)),
            dma((N,)), dma((N,)),
            dma((N,)), dma((N,)),
            dma((4,)),
        ],
        name="rank_mixer",
        compiler_params=pltpu.CompilerParams(
            collective_id=0, has_side_effects=True, vmem_limit_bytes=60 << 20
        ),
    )(
        tokens.reshape(rows, width),
        route_ids.reshape(rows, 2).T,
        router.reshape(width, N).T,
        norm_gain.reshape(1, width),
        w_in.reshape(width, hidden),
        w_out.reshape(hidden, width),
        cotangent.reshape(rows, width),
    )
    normed_out, grad_tokens, grad_router, grad_gain, grad_w_in, grad_w_out = out
    return (
        normed_out.reshape(rows, 1, width),
        grad_tokens.reshape(rows, 1, width),
        grad_router.T.reshape(1, width, N),
        grad_gain,
        grad_w_in.reshape(1, 1, width, hidden),
        grad_w_out.reshape(1, 1, hidden, width),
    )


def solution(mesh):
    return jax.shard_map(
        body,
        mesh=mesh,
        in_specs=(
            P("dp", "expert", None),
            P("expert", "dp", None),
            P("expert", None, None),
            P("expert", None),
            P("expert", "dp", None, None),
            P("expert", "dp", None, None),
            P("dp", "expert", None),
        ),
        out_specs=(
            P("dp", "expert", None),
            P("dp", "expert", None),
            P("expert", None, None),
            P("expert", None),
            P("expert", "dp", None, None),
            P("expert", "dp", None, None),
        ),
        check_vma=False,
    )
```

```python
import functools

import jax
import jax.numpy as jnp
from jax import lax
from jax.experimental import pallas as pl
from jax.experimental.pallas import tpu as pltpu
from jax.sharding import PartitionSpec as P

MESH = pl.DeviceIdType.MESH
F32 = jnp.float32
BF16 = jnp.bfloat16

gelu_coef = 0.7978845608028654
cubic_coef = 0.044715
norm_eps = 1e-05

N = 16
NC = 4
NG = 4
RING = 8
STEPS = (0, 1, -1, 2, -2, 3, -3, 4)
BACK = (0, 2, 1, 4, 3, 6, 5, 7)
HOPS = (0, 0, 0, 0, 0, 0, -1, -1, 1, 1, -2, -2, 2, 2, 3, -3)
FROM_LOW = (4, 5, 8, 9, 12, 13, 14)
FROM_HIGH = (2, 3, 6, 7, 10, 11, 15)
OWN = (0, 1)
HERE = (0, 2, 4)
AWAY = tuple(r for r in range(N) if r not in HERE)
TILE = 32
RUNS = 4


def inverse(r):
    return 2 * BACK[r // 2] + r % 2


def dot(a, b):
    return lax.dot_general(a, b, (((1,), (0,)), ((), ())), preferred_element_type=F32)


def dot_nt(a, b):
    return lax.dot_general(a, b, (((1,), (1,)), ((), ())), preferred_element_type=F32)


def dot_tn(a, b):
    return lax.dot_general(a, b, (((0,), (0,)), ((), ())), preferred_element_type=F32)


def gelu_and_slope(value):
    inner = gelu_coef * (value + cubic_coef * value * value * value)
    tangent = jnp.tanh(inner)
    half = 0.5 * (1.0 + tangent)
    slope = half + 0.5 * value * (1.0 - tangent * tangent) * gelu_coef * (
        1.0 + 3.0 * cubic_coef * value * value
    )
    return value * half, slope


def kernel(
    tok_h, ids_h, rt_h, gain_h, win_h, wout_h, cot_h,
    no_h, gt_h, gr_ref, gg_ref, gwi_h, gwo_h,
    tok, ids_ref, rt_ref, gain_ref, tok_t, mix_t, mixed, cot, win, wout, rt4,
    ids_own, ids_low, ids_high, pl_m, ph_m, po_m, pl_t, ph_t, po_t,
    raw_l, raw_h, xs, xr, pre, logit, gate, act, ys, yr,
    part_l, part_h, sum_h, sum_l, acc, grd, gr, gp, dos, ds,
    norm_o, gwi, gwo, gm_t, gt_t, ggp, rcol, small,
    gain_s, gain_r, col_s, col_r,
    load_sem, ids_ss, ids_rs, mix_ss, mix_rs, raw_ss, raw_rs, a_ss, a_rs, b_ss, b_rs,
    sum_ss, sum_rs, raw2_ss, raw2_rs, c_ss, c_rs, d_ss, d_rs, sum2_ss, sum2_rs,
    e_ss, e_rs, gn_ss, gn_rs, cl_ss, cl_rs, out_sem,
):
    rows, width = tok.shape
    head = width // N
    part = width // NC
    hidden = win.shape[1]
    depth = xs.shape[2]
    group = depth * 4
    slots = N * depth
    tokens4 = N // NC
    dp = lax.axis_index("dp")
    ex = lax.axis_index("expert")
    z, co = dp // 2, dp % 2
    xm, ym = ex // 4, ex % 4

    def partner(r):
        return ((z + STEPS[r // 2] + RING) % RING) * 2 + (co + r % 2) % 2

    def target(r):
        return ((z + HOPS[r] + RING) % RING) * 2 + (co + r % 2) % 2

    def origin(r):
        return ((z - HOPS[r] + RING) % RING) * 2 + (co + r % 2) % 2

    high = ((z + 1) % RING) * 2 + co
    low = ((z + RING - 1) % RING) * 2 + co

    def send(src, dst, send_sem, recv_sem, to):
        copy = pltpu.make_async_remote_copy(
            src_ref=src, dst_ref=dst, send_sem=send_sem, recv_sem=recv_sem,
            device_id=(to, ex), device_id_type=MESH,
        )
        copy.start()
        return copy

    def load(src, dst, k):
        copy = pltpu.make_async_copy(src, dst, load_sem.at[k])
        copy.start()
        return copy

    got_tok = load(tok_h, tok, 0)
    got_ids = load(ids_h, ids_ref, 1)
    got_rt = load(rt_h, rt_ref, 2)
    got_gain = load(gain_h, gain_ref, 3)
    got_win = load(win_h, win, 4)
    got_wout = load(wout_h, wout, 5)
    got_cot = load(cot_h, cot, 6)

    barrier = pltpu.get_barrier_semaphore()
    for r in range(1, N):
        pl.semaphore_signal(barrier, inc=1, device_id=(partner(r), ex), device_id_type=MESH)
    for k in range(1, N):
        pl.semaphore_signal(barrier, inc=1, device_id=(dp, (ex + k) % N), device_id_type=MESH)
    got_tok.wait()
    got_ids.wait()
    ids_own[...] = jnp.zeros_like(ids_own)
    ids_own[0:2, :] = ids_ref[...]

    ids_cp, mix_cp = {}, {}
    for i in range(NC):
        c = (xm - i + 4) % 4
        turned = tok[:, pl.ds(pl.multiple_of(c * part, part), part)].T
        tok_t[pl.ds(c * tokens4, tokens4)] = turned.reshape(tokens4, head, rows)
        if i == 0:
            mix_t[ex] = tok_t[ex]
            pl.semaphore_wait(barrier, 2 * (N - 1))
        for yy in range(4):
            k = i * 4 + yy
            to = c * 4 + (ym + yy) % 4
            if k == 0:
                continue
            mix_cp[k] = pltpu.make_async_remote_copy(
                src_ref=tok_t.at[to], dst_ref=mix_t.at[ex],
                send_sem=mix_ss.at[k], recv_sem=mix_rs.at[k],
                device_id=(dp, to), device_id_type=MESH,
            )
            mix_cp[k].start()
        if i == 0:
            ids_cp[0] = send(ids_own, ids_low, ids_ss.at[0], ids_rs.at[0], high)
            ids_cp[1] = send(ids_own, ids_high, ids_ss.at[1], ids_rs.at[1], low)

    label = lax.broadcasted_iota(jnp.int32, (N, rows), 0)
    earlier = (
        lax.broadcasted_iota(jnp.int32, (rows, rows), 0)
        < lax.broadcasted_iota(jnp.int32, (rows, rows), 1)
    ).astype(F32)
    earlier = earlier.astype(BF16)
    slot = lax.broadcasted_iota(jnp.int32, (depth, rows), 0)

    def place(ids, members, matrix, flipped):
        ids0, ids1 = ids[0:1, :], ids[1:2, :]
        hot0 = (label == ids0).astype(F32)
        hot1 = (label == ids1).astype(F32)
        before = dot((hot0 + hot1).astype(BF16), earlier)
        at0 = jnp.sum(before * hot0, axis=0, keepdims=True).astype(jnp.int32)
        at1 = jnp.sum(before * hot1, axis=0, keepdims=True).astype(jnp.int32)
        blocks = []
        for r in members:
            e = target(r)
            goal0 = jnp.where(ids0 == e, at0, -1)
            goal1 = jnp.where(ids1 == e, at1, -1)
            blocks.append(jnp.logical_or(slot == goal0, slot == goal1).astype(F32))
        placed = jnp.concatenate(blocks, axis=0)
        matrix[...] = placed.astype(BF16)
        flipped[...] = placed.T.astype(BF16)

    def stack(blocks, members, q):
        return jnp.concatenate([blocks[r, q] for r in members], axis=0)

    def expand(matrix, values, members, q, out, arrived):
        sent = dot(matrix[...], values).astype(BF16)
        for n, r in enumerate(members):
            into = arrived if r in HERE else out
            into[r, q] = sent[n * depth : (n + 1) * depth]

    raw_cp, a_cp = {}, {}

    def send_mixed(r, i):
        c = (xm + i) % 4
        a_cp[r, i] = send(xs.at[r, c], xr.at[r, c], a_ss.at[r, i], a_rs.at[r, i], target(r))

    def mix_chunk(i):
        c = (xm + i) % 4
        for yy in range(4):
            if i * 4 + yy:
                mix_cp[i * 4 + yy].wait_recv()
        mixed[c] = mix_t[pl.ds(c * tokens4, tokens4)].reshape(part, rows).T
        raw_cp[0, i] = send(mixed.at[c], raw_l.at[c], raw_ss.at[0, i], raw_rs.at[0, i], high)
        raw_cp[1, i] = send(mixed.at[c], raw_h.at[c], raw_ss.at[1, i], raw_rs.at[1, i], low)

    def pass_on(i):
        c = (xm + i) % 4
        expand(po_m, mixed[c], OWN, c, xs, xr)
        send_mixed(1, i)
        raw_cp[0, i].wait_recv()
        expand(pl_m, raw_l[c], FROM_LOW, c, xs, xr)
        raw_cp[1, i].wait_recv()
        expand(ph_m, raw_h[c], FROM_HIGH, c, xs, xr)
        for r in AWAY[1:]:
            send_mixed(r, i)

    for i in range(NC):
        mix_chunk(i)
        if i:
            pass_on(i - 1)
            continue
        place(ids_own, OWN, po_m, po_t)
        ids_cp[0].wait_recv()
        ids_cp[1].wait_recv()
        place(ids_low, FROM_LOW, pl_m, pl_t)
        place(ids_high, FROM_HIGH, ph_m, ph_t)
    pass_on(NC - 1)

    got_rt.wait()
    got_win.wait()
    got_wout.wait()
    for c in range(NC):
        rt4[c] = rt_ref[:, c * part : (c + 1) * part]
    mine = lax.broadcasted_iota(jnp.int32, (group, N), 1) == dp
    for i in range(NC - 1):
        c = (xm + i) % 4
        for r in AWAY:
            a_cp[r, i].wait_recv()
        for g in range(NG):
            at = slice(g * group, (g + 1) * group)
            block = xr[4 * g : 4 * g + 4, c].reshape(group, part)
            more = dot(block, win[pl.ds(pl.multiple_of(c * part, part), part), :])
            more_logit = dot_nt(block, rt4[c])
            if i == 0:
                pre[at, :] = more
                logit[at, :] = more_logit
            else:
                pre[at, :] += more
                logit[at, :] += more_logit
    b_cp = {}
    c = (xm + NC - 1) % 4
    for g in range(NG):
        at = slice(g * group, (g + 1) * group)
        for r in range(4 * g, 4 * g + 4):
            if r in AWAY:
                a_cp[r, NC - 1].wait_recv()
        block = xr[4 * g : 4 * g + 4, c].reshape(group, part)
        value = pre[at, :] + dot(block, win[pl.ds(pl.multiple_of(c * part, part), part), :])
        score = logit[at, :] + dot_nt(block, rt4[c])
        share = jax.nn.sigmoid(jnp.sum(jnp.where(mine, score, 0.0), axis=1, keepdims=True))
        gate[at, :] = share
        activated, slope = gelu_and_slope(value)
        pre[at, :] = slope
        act[at, :] = activated.astype(BF16)
        for q in range(NC):
            out = dot(act[at, :], wout[:, q * part : (q + 1) * part])
            result = (share * out).astype(BF16).reshape(4, depth, part)
            ys[4 * g : 4 * g + 4, q] = result
            for r in range(4 * g, 4 * g + 4):
                if r in HERE:
                    yr[r, q] = result[r - 4 * g]
        for r in range(4 * g, 4 * g + 4):
            if r in AWAY:
                b_cp[r] = send(ys.at[r], yr.at[r], b_ss.at[r], b_rs.at[r], origin(r))

    sum_cp = {}
    for r in AWAY:
        b_cp[r].wait_recv()
    for q in range(NC):
        part_l[q] = dot(pl_t[...], stack(yr, FROM_LOW, q)).astype(BF16)
        sum_cp[0, q] = send(part_l.at[q], sum_h.at[q], sum_ss.at[0, q], sum_rs.at[0, q], low)
        part_h[q] = dot(ph_t[...], stack(yr, FROM_HIGH, q)).astype(BF16)
        sum_cp[1, q] = send(part_h.at[q], sum_l.at[q], sum_ss.at[1, q], sum_rs.at[1, q], high)
    for q in range(NC):
        acc[q] = mixed[q].astype(F32) + dot(po_t[...], stack(yr, OWN, q))
    got_cot.wait()
    got_gain.wait()
    ggp[...] = jnp.zeros_like(ggp)

    def norm_rows(j, carry):
        at = pl.ds(pl.multiple_of(j * TILE, TILE), TILE)
        cols = [slice(q * part, (q + 1) * part) for q in range(NC)]
        resid = [
            acc[q, at, :] + sum_h[q, at, :].astype(F32) + sum_l[q, at, :].astype(F32)
            for q in range(NC)
        ]
        mean = sum(jnp.sum(v, axis=1, keepdims=True) for v in resid) / width
        resid = [v - mean for v in resid]
        var = sum(jnp.sum(v * v, axis=1, keepdims=True) for v in resid) / width
        inv_std = lax.rsqrt(var + norm_eps)
        normed = [v * inv_std for v in resid]
        grads, m1, m2 = [], 0.0, 0.0
        for q in range(NC):
            gain = gain_ref[0:1, cols[q]]
            norm_o[at, cols[q]] = (normed[q] * gain).astype(BF16)
            cot_f = cot[at, cols[q]].astype(F32)
            ggp[0:1, cols[q]] += jnp.sum(cot_f * normed[q], axis=0, keepdims=True)
            grad = cot_f * gain
            grads.append(grad)
            m1 += jnp.sum(grad, axis=1, keepdims=True)
            m2 += jnp.sum(grad * normed[q], axis=1, keepdims=True)
        m1, m2 = m1 / width, m2 / width
        for q in range(NC):
            grad = inv_std * (grads[q] - m1 - normed[q] * m2)
            acc[q, at, :] = grad
            grd[q, at, :] = grad.astype(BF16)
        return carry

    for q in range(NC):
        sum_cp[0, q].wait_recv()
        sum_cp[1, q].wait_recv()

    raw2_cp, c_cp = {}, {}
    run = rows // RUNS
    for i in range(RUNS):
        lax.fori_loop(i * run // TILE, (i + 1) * run // TILE, norm_rows, 0)
        src = grd.at[:, i * run : (i + 1) * run, :]
        to_high, to_low = (d.at[:, i * run : (i + 1) * run, :] for d in (raw_l, raw_h))
        raw2_cp[0, i] = send(src, to_high, raw2_ss.at[0, i], raw2_rs.at[0, i], high)
        raw2_cp[1, i] = send(src, to_low, raw2_ss.at[1, i], raw2_rs.at[1, i], low)

    def spread(vector, source, target, gathered, send_sems, recv_sems):
        source[...] = jnp.zeros_like(source)
        for j in range(width // 128):
            source[j : j + 1, :] = vector[0:1, j * 128 : (j + 1) * 128]
        target[...] = source[...].astype(BF16)
        gathered[dp] = target[...]
        copies = {}
        for r in range(1, N):
            copies[r] = pltpu.make_async_remote_copy(
                src_ref=target, dst_ref=gathered.at[dp],
                send_sem=send_sems.at[r], recv_sem=recv_sems.at[inverse(r)],
                device_id=(partner(r), ex), device_id_type=MESH,
            )
            copies[r].start()
        return copies

    gn_cp = spread(ggp, small, gain_s, gain_r, gn_ss, gn_rs)
    put_norm = pltpu.make_async_copy(norm_o, no_h, out_sem.at[0])
    put_norm.start()
    for k in a_cp:
        a_cp[k].wait_send()
    for k in sum_cp:
        sum_cp[k].wait_send()
    for q in range(NC):
        expand(po_m, grd[q], OWN, q, xs, gr)
    for i in range(RUNS):
        raw2_cp[0, i].wait_recv()
        raw2_cp[1, i].wait_recv()
    for q in range(NC):
        expand(pl_m, raw_l[q], FROM_LOW, q, xs, gr)
        expand(ph_m, raw_h[q], FROM_HIGH, q, xs, gr)
    for r in AWAY:
        c_cp[r] = send(xs.at[r], gr.at[r], c_ss.at[r], c_rs.at[r], target(r))

    rcol[...] = jnp.zeros_like(rcol)
    mine_row = lax.broadcasted_iota(jnp.int32, (N, part), 0) == dp
    d_cp = {}

    def send_back(r, i):
        c = (xm + 1 + i) % 4
        d_cp[r, i] = send(ds.at[r, c], yr.at[r, c], d_ss.at[r, i], d_rs.at[r, i], origin(r))

    for g in range(NG):
        at = slice(g * group, (g + 1) * group)
        for r in range(4 * g, 4 * g + 4):
            if r in AWAY:
                c_cp[r].wait_recv()
        share = gate[at, :]
        grad_act, grad_gate = 0.0, 0.0
        for q in range(NC):
            grad = gr[4 * g : 4 * g + 4, q].reshape(group, part).astype(F32)
            result = ys[4 * g : 4 * g + 4, q].reshape(group, part).astype(F32)
            grad_gate += jnp.sum(grad * result, axis=1, keepdims=True)
            grad_out = (share * grad).astype(BF16)
            dos[q, at, :] = grad_out
            grad_act += dot_nt(grad_out, wout[:, q * part : (q + 1) * part])
        grad_logit = grad_gate * (1.0 - share)
        gp[at, :] = (grad_act * pre[at, :]).astype(BF16)
        for q in range(NC):
            weights = jnp.sum(jnp.where(mine_row, rt4[q].astype(F32), 0.0), axis=0, keepdims=True)
            back = dot_nt(gp[at, :], win[q * part : (q + 1) * part, :]) + grad_logit * weights
            back = back.astype(BF16).reshape(4, depth, part)
            ds[4 * g : 4 * g + 4, q] = back
            for r in range(4 * g, 4 * g + 4):
                if r in HERE:
                    yr[r, q] = back[r - 4 * g]
            block = xr[4 * g : 4 * g + 4, q].reshape(group, part).astype(F32)
            rcol[0:1, q * part : (q + 1) * part] += jnp.sum(
                grad_logit * block, axis=0, keepdims=True
            )
        for i in range(2):
            for r in range(4 * g, 4 * g + 4):
                if r in AWAY:
                    send_back(r, i)
    for i in range(2, NC):
        for r in AWAY:
            send_back(r, i)
    cl_cp = spread(rcol, small, col_s, col_r, cl_ss, cl_rs)

    for q in range(NC):
        cols = slice(q * part, (q + 1) * part)
        gwi[cols, :] = dot_tn(xr[:, q].reshape(slots, part), gp[...]).astype(BF16)
        gwo[:, cols] = dot_tn(act[...], dos[q]).astype(BF16)
    put_gwi = pltpu.make_async_copy(gwi, gwi_h, out_sem.at[1])
    put_gwi.start()
    put_gwo = pltpu.make_async_copy(gwo, gwo_h, out_sem.at[2])
    put_gwo.start()

    sum2_cp, e_cp = {}, {}

    def sum_back(i):
        c = (xm + 1 + i) % 4
        for r in AWAY:
            d_cp[r, i].wait_recv()
        part_l[c] = dot(pl_t[...], stack(yr, FROM_LOW, c)).astype(BF16)
        sum2_cp[0, i] = send(part_l.at[c], sum_h.at[c], sum2_ss.at[0, i], sum2_rs.at[0, i], low)
        part_h[c] = dot(ph_t[...], stack(yr, FROM_HIGH, c)).astype(BF16)
        sum2_cp[1, i] = send(part_h.at[c], sum_l.at[c], sum2_ss.at[1, i], sum2_rs.at[1, i], high)
        acc[c] += dot(po_t[...], stack(yr, OWN, c))

    def finish_chunk(i):
        c = (xm + 1 + i) % 4
        sum2_cp[0, i].wait_recv()
        sum2_cp[1, i].wait_recv()
        total = acc[c] + sum_h[c].astype(F32) + sum_l[c].astype(F32)
        gm_t[pl.ds(c * tokens4, tokens4)] = total.astype(BF16).T.reshape(tokens4, head, rows)
        for yy in range(4):
            to = c * tokens4 + (ym + yy) % 4
            if i == NC - 1 and yy == 0:
                gt_t[ex] = gm_t[ex]
                continue
            k = i * 4 + yy
            e_cp[k] = pltpu.make_async_remote_copy(
                src_ref=gm_t.at[to], dst_ref=gt_t.at[ex],
                send_sem=e_ss.at[k], recv_sem=e_rs.at[k],
                device_id=(dp, to), device_id_type=MESH,
            )
            e_cp[k].start()

    for i in range(NC):
        sum_back(i)
        if i:
            finish_chunk(i - 1)
    finish_chunk(NC - 1)

    for r in range(1, N):
        gn_cp[inverse(r)].wait_recv()
        cl_cp[inverse(r)].wait_recv()
    total = gain_r[0].astype(F32)
    for e in range(1, N):
        total += gain_r[e].astype(F32)
    small[...] = total
    for j in range(width // 128):
        gg_ref[0:1, j * 128 : (j + 1) * 128] = small[j : j + 1, :]
    for e in range(N):
        small[...] = col_r[e].astype(F32)
        for j in range(width // 128):
            gr_ref[e : e + 1, j * 128 : (j + 1) * 128] = small[j : j + 1, :]

    for i in range(NC):
        c = (xm + NC - 1 - i) % 4
        for yy in range(4):
            if i < NC - 1 or yy:
                e_cp[i * 4 + yy].wait_recv()
        turned = gt_t[pl.ds(c * tokens4, tokens4)].reshape(part, rows).T
        tok[:, pl.ds(pl.multiple_of(c * part, part), part)] = turned
    put_gt = pltpu.make_async_copy(tok, gt_h, out_sem.at[3])
    put_gt.start()
    for copies in (
        ids_cp, mix_cp, raw_cp, b_cp, raw2_cp, c_cp, d_cp, sum2_cp, e_cp, gn_cp, cl_cp,
    ):
        for k in copies:
            copies[k].wait_send()
    put_norm.wait()
    put_gwi.wait()
    put_gwo.wait()
    put_gt.wait()


def store_kernel(pieces, *refs):
    count = len(pieces)
    sems = refs[2 * count]
    copies = []
    for k, cut in enumerate(pieces):
        size = refs[k].shape[0] // cut
        for i in range(cut):
            at = slice(i * size, (i + 1) * size)
            copies.append(
                pltpu.make_async_copy(refs[k].at[at, :], refs[count + k].at[at, :], sems.at[len(copies)])
            )
    for copy in copies:
        copy.start()
    for copy in copies:
        copy.wait()


def body(tokens, route_ids, router, norm_gain, w_in, w_out, cotangent):
    rows, width = tokens.shape[0], tokens.shape[2]
    hidden = w_in.shape[3]
    depth = 3 * rows // N
    slots = N * depth
    part = width // NC
    head = width // N
    group = 4 * depth
    shape = jax.ShapeDtypeStruct
    vmem = pl.BlockSpec(memory_space=pltpu.VMEM)
    anywhere = pl.BlockSpec(memory_space=pl.ANY)
    hbm = pl.BlockSpec(memory_space=pltpu.HBM)
    dma = pltpu.SemaphoreType.DMA
    keep = functools.partial(pltpu.with_memory_space_constraint, memory_space=pltpu.HBM)
    blocks = pltpu.VMEM((N, NC, depth, part), BF16)
    flipped = pltpu.VMEM((N, head, rows), BF16)
    row_block = pltpu.VMEM((rows, width), BF16)
    chunks = pltpu.VMEM((NC, rows, part), BF16)
    ids = pltpu.VMEM((8, rows), jnp.int32)
    out = pl.pallas_call(
        kernel,
        out_shape=(
            shape((rows, width), BF16),
            shape((rows, width), BF16),
            shape((N, width), F32),
            shape((1, width), F32),
            shape((width, hidden), BF16),
            shape((hidden, width), BF16),
        ),
        in_specs=[hbm] * 7,
        out_specs=[anywhere, anywhere, vmem, vmem, anywhere, anywhere],
        scratch_shapes=[
            row_block,
            pltpu.VMEM((2, rows), jnp.int32),
            pltpu.VMEM((N, width), BF16),
            pltpu.VMEM((1, width), F32),
            flipped,
            flipped,
            chunks,
            row_block,
            pltpu.VMEM((width, hidden), BF16),
            pltpu.VMEM((hidden, width), BF16),
            pltpu.VMEM((NC, N, part), BF16),
            ids, ids, ids,
            pltpu.VMEM((7 * depth, rows), BF16),
            pltpu.VMEM((7 * depth, rows), BF16),
            pltpu.VMEM((2 * depth, rows), BF16),
            pltpu.VMEM((rows, 7 * depth), BF16),
            pltpu.VMEM((rows, 7 * depth), BF16),
            pltpu.VMEM((rows, 2 * depth), BF16),
            chunks, chunks,
            blocks,
            blocks,
            pltpu.VMEM((slots, hidden), F32),
            pltpu.VMEM((slots, N), F32),
            pltpu.VMEM((slots, 1), F32),
            pltpu.VMEM((slots, hidden), BF16),
            blocks,
            blocks,
            chunks, chunks, chunks, chunks,
            pltpu.VMEM((NC, rows, part), F32),
            chunks,
            blocks,
            pltpu.VMEM((slots, hidden), BF16),
            pltpu.VMEM((NC, slots, part), BF16),
            blocks,
            row_block,
            pltpu.VMEM((width, hidden), BF16),
            pltpu.VMEM((hidden, width), BF16),
            flipped,
            flipped,
            pltpu.VMEM((8, width), F32),
            pltpu.VMEM((8, width), F32),
            pltpu.VMEM((16, 128), F32),
            pltpu.VMEM((16, 128), BF16),
            pltpu.VMEM((N, 16, 128), BF16),
            pltpu.VMEM((16, 128), BF16),
            pltpu.VMEM((N, 16, 128), BF16),
            dma((7,)),
            dma((2,)), dma((2,)),
            dma((N,)), dma((N,)),
            dma((2, NC)), dma((2, NC)),
            dma((N, NC)), dma((N, NC)),
            dma((N,)), dma((N,)),
            dma((2, NC)), dma((2, NC)),
            dma((2, RUNS)), dma((2, RUNS)),
            dma((N,)), dma((N,)),
            dma((N, NC)), dma((N, NC)),
            dma((2, NC)), dma((2, NC)),
            dma((N,)), dma((N,)),
            dma((N,)), dma((N,)),
            dma((N,)), dma((N,)),
            dma((4,)),
        ],
        name="rank_mixer",
        compiler_params=pltpu.CompilerParams(
            collective_id=0, has_side_effects=True, vmem_limit_bytes=46 << 20
        ),
    )(
        keep(tokens.reshape(rows, width)),
        keep(route_ids.reshape(rows, 2).T),
        keep(router.reshape(width, N).T),
        keep(norm_gain.reshape(1, width)),
        keep(w_in.reshape(width, hidden)),
        keep(w_out.reshape(hidden, width)),
        keep(cotangent.reshape(rows, width)),
    )
    pieces = (2, 2, 1, 1, 4, 4)
    out = pl.pallas_call(
        functools.partial(store_kernel, pieces),
        out_shape=tuple(shape(v.shape, v.dtype) for v in out),
        in_specs=[anywhere] * 6,
        out_specs=[hbm] * 6,
        scratch_shapes=[dma((sum(pieces),))],
        name="store",
        compiler_params=pltpu.CompilerParams(vmem_limit_bytes=1 << 20),
    )(*out)
    normed_out, grad_tokens, grad_router, grad_gain, grad_w_in, grad_w_out = out
    return (
        normed_out.reshape(rows, 1, width),
        grad_tokens.reshape(rows, 1, width),
        grad_router.T.reshape(1, width, N),
        grad_gain,
        grad_w_in.reshape(1, 1, width, hidden),
        grad_w_out.reshape(1, 1, hidden, width),
    )


def solution(mesh):
    return jax.shard_map(
        body,
        mesh=mesh,
        in_specs=(
            P("dp", "expert", None),
            P("expert", "dp", None),
            P("expert", None, None),
            P("expert", None),
            P("expert", "dp", None, None),
            P("expert", "dp", None, None),
            P("dp", "expert", None),
        ),
        out_specs=(
            P("dp", "expert", None),
            P("dp", "expert", None),
            P("expert", None, None),
            P("expert", None),
            P("expert", "dp", None, None),
            P("expert", "dp", None, None),
        ),
        check_vma=False,
    )
```

```python
import functools

import jax
import jax.numpy as jnp
from jax import lax
from jax.experimental import pallas as pl
from jax.experimental.pallas import tpu as pltpu
from jax.sharding import PartitionSpec as P

MESH = pl.DeviceIdType.MESH
F32 = jnp.float32
BF16 = jnp.bfloat16

gelu_coef = 0.7978845608028654
cubic_coef = 0.044715
norm_eps = 1e-05

N = 16
NC = 4
NG = 4
RING = 8
STEPS = (0, 1, -1, 2, -2, 3, -3, 4)
HOPS = (0, 0, 0, 0, 0, 0, -1, -1, 1, 1, -2, -2, 2, 2, 3, -3)
FROM_LOW = (4, 5, 8, 9, 12, 13, 14)
FROM_HIGH = (2, 3, 6, 7, 10, 11, 15)
OWN = (0, 1)
HERE = (0, 2, 4)
AWAY = tuple(r for r in range(N) if r not in HERE)
TILE = 32
RUNS = 4


def dot(a, b):
    return lax.dot_general(a, b, (((1,), (0,)), ((), ())), preferred_element_type=F32)


def dot_nt(a, b):
    return lax.dot_general(a, b, (((1,), (1,)), ((), ())), preferred_element_type=F32)


def dot_tn(a, b):
    return lax.dot_general(a, b, (((0,), (0,)), ((), ())), preferred_element_type=F32)


def gelu_and_slope(value):
    inner = gelu_coef * (value + cubic_coef * value * value * value)
    tangent = jnp.tanh(inner)
    half = 0.5 * (1.0 + tangent)
    slope = half + 0.5 * value * (1.0 - tangent * tangent) * gelu_coef * (
        1.0 + 3.0 * cubic_coef * value * value
    )
    return value * half, slope


def kernel(
    tok_h, ids_h, rt_h, gain_h, win_h, wout_h, cot_h,
    no_h, gt_h, gr_ref, gg_ref, gwi_h, gwo_h,
    tok, ids_ref, rt_ref, gain_ref, tok_t, mix_t, mixed, cot, win, wout, rt4,
    ids_own, ids_low, ids_high, pl_m, ph_m, po_m, pl_t, ph_t, po_t,
    raw_l, raw_h, xs, xr, pre, logit, gate, act, ys, yr,
    part_l, part_h, sum_h, sum_l, acc, grd, gr, gp, ds, glog,
    gwi, gwo, gt_t, ggp, rcol, small,
    gain_s, gain_r, col_s, col_r,
    load_sem, ids_ss, ids_rs, mix_ss, mix_rs, raw_ss, raw_rs, a_ss, a_rs, b_ss, b_rs,
    sum_ss, sum_rs, raw2_ss, raw2_rs, c_ss, c_rs, d_ss, d_rs, sum2_ss, sum2_rs,
    e_ss, e_rs, gn_ss, gn_rs, cl_ss, cl_rs, out_sem,
):
    rows, width = tok.shape
    head = width // N
    part = width // NC
    hidden = win.shape[1]
    depth = xs.shape[2]
    group = depth * 4
    slots = N * depth
    tokens4 = N // NC
    dp = lax.axis_index("dp")
    ex = lax.axis_index("expert")
    z, co = dp // 2, dp % 2
    xm, ym = ex // 4, ex % 4

    def partner(r):
        return ((z + STEPS[r // 2] + RING) % RING) * 2 + (co + r % 2) % 2

    def target(r):
        return ((z + HOPS[r] + RING) % RING) * 2 + (co + r % 2) % 2

    def origin(r):
        return ((z - HOPS[r] + RING) % RING) * 2 + (co + r % 2) % 2

    high = ((z + 1) % RING) * 2 + co
    low = ((z + RING - 1) % RING) * 2 + co

    def send(src, dst, send_sem, recv_sem, to):
        copy = pltpu.make_async_remote_copy(
            src_ref=src, dst_ref=dst, send_sem=send_sem, recv_sem=recv_sem,
            device_id=(to, ex), device_id_type=MESH,
        )
        copy.start()
        return copy

    def load(src, dst, k):
        copy = pltpu.make_async_copy(src, dst, load_sem.at[k])
        copy.start()
        return copy

    got_tok = load(tok_h, tok, 0)
    got_ids = load(ids_h, ids_ref, 1)

    barrier = pltpu.get_barrier_semaphore()
    for r in range(1, N):
        pl.semaphore_signal(barrier, inc=1, device_id=(partner(r), ex), device_id_type=MESH)
    for k in range(1, N):
        pl.semaphore_signal(barrier, inc=1, device_id=(dp, (ex + k) % N), device_id_type=MESH)
    got_tok.wait()
    got_ids.wait()
    got_win = load(win_h, win, 4)
    got_wout = load(wout_h, wout, 5)
    got_rt = load(rt_h, rt_ref, 2)
    got_gain = load(gain_h, gain_ref, 3)
    got_cot = load(cot_h, cot, 6)
    ids_own[...] = jnp.zeros_like(ids_own)
    ids_own[0:2, :] = ids_ref[...]

    ids_cp, mix_cp = {}, {}
    for i in range(NC):
        c = (xm - i + 4) % 4
        turned = tok[:, pl.ds(pl.multiple_of(c * part, part), part)].T
        tok_t[pl.ds(c * tokens4, tokens4)] = turned.reshape(tokens4, head, rows)
        if i == 0:
            mix_t[ex] = tok_t[ex]
            pl.semaphore_wait(barrier, 2 * (N - 1))
        for yy in range(4):
            k = i * 4 + yy
            to = c * 4 + (ym + yy) % 4
            if k == 0:
                continue
            mix_cp[k] = pltpu.make_async_remote_copy(
                src_ref=tok_t.at[to], dst_ref=mix_t.at[ex],
                send_sem=mix_ss.at[k], recv_sem=mix_rs.at[k],
                device_id=(dp, to), device_id_type=MESH,
            )
            mix_cp[k].start()
        if i == 0:
            ids_cp[0] = send(ids_own, ids_low, ids_ss.at[0], ids_rs.at[0], high)
            ids_cp[1] = send(ids_own, ids_high, ids_ss.at[1], ids_rs.at[1], low)

    label = lax.broadcasted_iota(jnp.int32, (N, rows), 0)
    earlier = (
        lax.broadcasted_iota(jnp.int32, (rows, rows), 0)
        < lax.broadcasted_iota(jnp.int32, (rows, rows), 1)
    ).astype(F32)
    earlier = earlier.astype(BF16)
    slot = lax.broadcasted_iota(jnp.int32, (depth, rows), 0)

    def place(ids, members, matrix, flipped):
        ids0, ids1 = ids[0:1, :], ids[1:2, :]
        hot0 = (label == ids0).astype(F32)
        hot1 = (label == ids1).astype(F32)
        before = dot((hot0 + hot1).astype(BF16), earlier)
        at0 = jnp.sum(before * hot0, axis=0, keepdims=True).astype(jnp.int32)
        at1 = jnp.sum(before * hot1, axis=0, keepdims=True).astype(jnp.int32)
        blocks = []
        for r in members:
            e = target(r)
            goal0 = jnp.where(ids0 == e, at0, -1)
            goal1 = jnp.where(ids1 == e, at1, -1)
            blocks.append(jnp.logical_or(slot == goal0, slot == goal1).astype(F32))
        placed = jnp.concatenate(blocks, axis=0)
        matrix[...] = placed.astype(BF16)
        flipped[...] = placed.T.astype(BF16)

    def stack(blocks, members, q):
        return jnp.concatenate([blocks[r, q] for r in members], axis=0)

    def expand(matrix, values, members, q, out, arrived):
        sent = dot(matrix[...], values).astype(BF16)
        for n, r in enumerate(members):
            into = arrived if r in HERE else out
            into[r, q] = sent[n * depth : (n + 1) * depth]

    raw_cp, a_cp = {}, {}

    def send_mixed(r, i):
        c = (xm + i) % 4
        a_cp[r, i] = send(xs.at[r, c], xr.at[r, c], a_ss.at[r, i], a_rs.at[r, i], target(r))

    def mix_chunk(i):
        c = (xm + i) % 4
        for yy in range(4):
            if i * 4 + yy:
                mix_cp[i * 4 + yy].wait_recv()
        mixed[c] = mix_t[pl.ds(c * tokens4, tokens4)].reshape(part, rows).T
        raw_cp[0, i] = send(mixed.at[c], raw_l.at[c], raw_ss.at[0, i], raw_rs.at[0, i], high)
        raw_cp[1, i] = send(mixed.at[c], raw_h.at[c], raw_ss.at[1, i], raw_rs.at[1, i], low)

    def pass_on(i):
        c = (xm + i) % 4
        expand(po_m, mixed[c], OWN, c, xs, xr)
        send_mixed(1, i)
        raw_cp[0, i].wait_recv()
        expand(pl_m, raw_l[c], FROM_LOW, c, xs, xr)
        raw_cp[1, i].wait_recv()
        expand(ph_m, raw_h[c], FROM_HIGH, c, xs, xr)
        for r in AWAY[1:]:
            send_mixed(r, i)

    for i in range(NC):
        mix_chunk(i)
        if i:
            pass_on(i - 1)
            continue
        place(ids_own, OWN, po_m, po_t)
        ids_cp[0].wait_recv()
        ids_cp[1].wait_recv()
        place(ids_low, FROM_LOW, pl_m, pl_t)
        place(ids_high, FROM_HIGH, ph_m, ph_t)
    pass_on(NC - 1)

    got_rt.wait()
    got_win.wait()
    got_wout.wait()
    for c in range(NC):
        rt4[c] = rt_ref[:, c * part : (c + 1) * part]
    mine = lax.broadcasted_iota(jnp.int32, (group, N), 1) == dp
    for i in range(NC - 1):
        c = (xm + i) % 4
        for r in AWAY:
            a_cp[r, i].wait_recv()
        for g in range(NG):
            at = slice(g * group, (g + 1) * group)
            block = xr[4 * g : 4 * g + 4, c].reshape(group, part)
            more = dot(block, win[pl.ds(pl.multiple_of(c * part, part), part), :])
            more_logit = dot_nt(block, rt4[c])
            if i == 0:
                pre[at, :] = more
                logit[at, :] = more_logit
            else:
                pre[at, :] += more
                logit[at, :] += more_logit
    b_cp = {}
    c = (xm + NC - 1) % 4
    for g in range(NG):
        at = slice(g * group, (g + 1) * group)
        for r in range(4 * g, 4 * g + 4):
            if r in AWAY:
                a_cp[r, NC - 1].wait_recv()
        block = xr[4 * g : 4 * g + 4, c].reshape(group, part)
        value = pre[at, :] + dot(block, win[pl.ds(pl.multiple_of(c * part, part), part), :])
        score = logit[at, :] + dot_nt(block, rt4[c])
        share = jax.nn.sigmoid(jnp.sum(jnp.where(mine, score, 0.0), axis=1, keepdims=True))
        gate[at, :] = share
        activated, slope = gelu_and_slope(value)
        pre[at, :] = slope
        act[at, :] = activated.astype(BF16)
        for q in range(NC):
            out = dot(act[at, :], wout[:, q * part : (q + 1) * part])
            result = (share * out).astype(BF16).reshape(4, depth, part)
            ys[4 * g : 4 * g + 4, q] = result
            for r in range(4 * g, 4 * g + 4):
                if r in HERE:
                    yr[r, q] = result[r - 4 * g]
        for r in range(4 * g, 4 * g + 4):
            if r in AWAY:
                b_cp[r] = send(ys.at[r], yr.at[r], b_ss.at[r], b_rs.at[r], origin(r))

    sum_cp = {}
    for r in AWAY:
        b_cp[r].wait_recv()
    run = rows // RUNS
    for i in range(RUNS):
        at = slice(i * run, (i + 1) * run)
        for q in range(NC):
            part_l[q, at] = dot(pl_t[at, :], stack(yr, FROM_LOW, q)).astype(BF16)
        sum_cp[0, i] = send(
            part_l.at[:, at, :], sum_h.at[:, at, :], sum_ss.at[0, i], sum_rs.at[0, i], low
        )
        for q in range(NC):
            part_h[q, at] = dot(ph_t[at, :], stack(yr, FROM_HIGH, q)).astype(BF16)
        sum_cp[1, i] = send(
            part_h.at[:, at, :], sum_l.at[:, at, :], sum_ss.at[1, i], sum_rs.at[1, i], high
        )
    for q in range(NC):
        acc[q] = mixed[q].astype(F32) + dot(po_t[...], stack(yr, OWN, q))
    got_cot.wait()
    got_gain.wait()
    ggp[...] = jnp.zeros_like(ggp)

    def norm_rows(j, carry):
        at = pl.ds(pl.multiple_of(j * TILE, TILE), TILE)
        cols = [slice(q * part, (q + 1) * part) for q in range(NC)]
        resid = [
            acc[q, at, :] + sum_h[q, at, :].astype(F32) + sum_l[q, at, :].astype(F32)
            for q in range(NC)
        ]
        mean = sum(jnp.sum(v, axis=1, keepdims=True) for v in resid) / width
        resid = [v - mean for v in resid]
        var = sum(jnp.sum(v * v, axis=1, keepdims=True) for v in resid) / width
        inv_std = lax.rsqrt(var + norm_eps)
        normed = [v * inv_std for v in resid]
        grads, m1, m2 = [], 0.0, 0.0
        for q in range(NC):
            gain = gain_ref[0:1, cols[q]]
            cot_f = cot[at, cols[q]].astype(F32)
            cot[at, cols[q]] = (normed[q] * gain).astype(BF16)
            ggp[0:1, cols[q]] += jnp.sum(cot_f * normed[q], axis=0, keepdims=True)
            grad = cot_f * gain
            grads.append(grad)
            m1 += jnp.sum(grad, axis=1, keepdims=True)
            m2 += jnp.sum(grad * normed[q], axis=1, keepdims=True)
        m1, m2 = m1 / width, m2 / width
        for q in range(NC):
            grad = inv_std * (grads[q] - m1 - normed[q] * m2)
            acc[q, at, :] = grad
            grd[q, at, :] = grad.astype(BF16)
        return carry

    raw2_cp, c_cp = {}, {}
    for i in range(RUNS):
        sum_cp[0, i].wait_recv()
        sum_cp[1, i].wait_recv()
        lax.fori_loop(i * run // TILE, (i + 1) * run // TILE, norm_rows, 0)
        src = grd.at[:, i * run : (i + 1) * run, :]
        to_high, to_low = (d.at[:, i * run : (i + 1) * run, :] for d in (raw_l, raw_h))
        raw2_cp[0, i] = send(src, to_high, raw2_ss.at[0, i], raw2_rs.at[0, i], high)
        raw2_cp[1, i] = send(src, to_low, raw2_ss.at[1, i], raw2_rs.at[1, i], low)

    def spread(vector, source, target, gathered, send_sems, recv_sems):
        source[...] = jnp.zeros_like(source)
        for j in range(width // 128):
            source[j : j + 1, :] = vector[0:1, j * 128 : (j + 1) * 128]
        target[...] = source[...].astype(BF16)
        gathered[co, z] = target[...]
        copies = {}
        for k in range(1, RING):
            copies[k] = send(
                target, gathered.at[co, z], send_sems.at[k], recv_sems.at[k],
                ((z + k) % RING) * 2 + co,
            )
        return copies

    def exchange(copies, gathered, send_sems, recv_sems):
        for k in range(1, RING):
            copies[k].wait_recv()
        copies[0] = send(
            gathered.at[co], gathered.at[co], send_sems.at[0], recv_sems.at[0],
            z * 2 + (co + 1) % 2,
        )

    gn_cp = spread(ggp, small, gain_s, gain_r, gn_ss, gn_rs)
    put_norm = pltpu.make_async_copy(cot, no_h, out_sem.at[0])
    put_norm.start()
    for k in mix_cp:
        mix_cp[k].wait_send()
    for k in a_cp:
        a_cp[k].wait_send()
    for k in sum_cp:
        sum_cp[k].wait_send()
    for q in range(NC):
        expand(po_m, grd[q], OWN, q, xs, gr)
    for i in range(RUNS):
        raw2_cp[0, i].wait_recv()
        raw2_cp[1, i].wait_recv()
    for q in range(NC):
        expand(pl_m, raw_l[q], FROM_LOW, q, xs, gr)
        expand(ph_m, raw_h[q], FROM_HIGH, q, xs, gr)
    for r in AWAY:
        c_cp[r] = send(xs.at[r], gr.at[r], c_ss.at[r], c_rs.at[r], target(r))

    rcol[...] = jnp.zeros_like(rcol)
    mine_row = lax.broadcasted_iota(jnp.int32, (N, part), 0) == dp
    d_cp = {}

    def send_back(r, i):
        c = (xm + 1 + i) % 4
        d_cp[r, i] = send(ds.at[r, c], yr.at[r, c], d_ss.at[r, i], d_rs.at[r, i], origin(r))

    for g in range(NG):
        at = slice(g * group, (g + 1) * group)
        for r in range(4 * g, 4 * g + 4):
            if r in AWAY:
                c_cp[r].wait_recv()
        share = gate[at, :]
        grad_act, grad_gate = 0.0, 0.0
        for q in range(NC):
            grad = gr[4 * g : 4 * g + 4, q].reshape(group, part).astype(F32)
            result = ys[4 * g : 4 * g + 4, q].reshape(group, part).astype(F32)
            grad_gate += jnp.sum(grad * result, axis=1, keepdims=True)
            grad_out = (share * grad).astype(BF16)
            gr[4 * g : 4 * g + 4, q] = grad_out.reshape(4, depth, part)
            grad_act += dot_nt(grad_out, wout[:, q * part : (q + 1) * part])
        grad_logit = grad_gate * (1.0 - share)
        glog[at, :] = grad_logit
        gp[at, :] = (grad_act * pre[at, :]).astype(BF16)
        for i in range(NC):
            c = (xm + 1 + i) % 4
            weights = jnp.sum(jnp.where(mine_row, rt4[c].astype(F32), 0.0), axis=0, keepdims=True)
            back = dot_nt(gp[at, :], win[pl.ds(pl.multiple_of(c * part, part), part), :])
            back = (back + grad_logit * weights).astype(BF16).reshape(4, depth, part)
            ds[4 * g : 4 * g + 4, c] = back
            for r in range(4 * g, 4 * g + 4):
                if r in HERE:
                    yr[r, c] = back[r - 4 * g]
                else:
                    send_back(r, i)

    for g in range(NG):
        at = slice(g * group, (g + 1) * group)
        for q in range(NC):
            block = xr[4 * g : 4 * g + 4, q].reshape(group, part).astype(F32)
            rcol[0:1, q * part : (q + 1) * part] += jnp.sum(
                glog[at, :] * block, axis=0, keepdims=True
            )
    cl_cp = spread(rcol, small, col_s, col_r, cl_ss, cl_rs)
    for q in range(NC):
        cols = slice(q * part, (q + 1) * part)
        gwi[cols, :] = dot_tn(xr[:, q].reshape(slots, part), gp[...]).astype(BF16)
    put_gwi = pltpu.make_async_copy(gwi, gwi_h, out_sem.at[1])
    put_gwi.start()

    def out_gradient(q):
        gwo[:, q * part : (q + 1) * part] = dot_tn(act[...], gr[:, q].reshape(slots, part)).astype(BF16)

    sum2_cp, e_cp = {}, {}

    def sum_back(i):
        c = (xm + 1 + i) % 4
        for r in AWAY:
            d_cp[r, i].wait_recv()
        part_l[c] = dot(pl_t[...], stack(yr, FROM_LOW, c)).astype(BF16)
        sum2_cp[0, i] = send(part_l.at[c], sum_h.at[c], sum2_ss.at[0, i], sum2_rs.at[0, i], low)
        part_h[c] = dot(ph_t[...], stack(yr, FROM_HIGH, c)).astype(BF16)
        sum2_cp[1, i] = send(part_h.at[c], sum_l.at[c], sum2_ss.at[1, i], sum2_rs.at[1, i], high)
        acc[c] += dot(po_t[...], stack(yr, OWN, c))

    def finish_chunk(i):
        c = (xm + 1 + i) % 4
        sum2_cp[0, i].wait_recv()
        sum2_cp[1, i].wait_recv()
        total = acc[c] + sum_h[c].astype(F32) + sum_l[c].astype(F32)
        tok_t[pl.ds(c * tokens4, tokens4)] = total.astype(BF16).T.reshape(tokens4, head, rows)
        for yy in range(4):
            to = c * tokens4 + (ym + yy) % 4
            if i == NC - 1 and yy == 0:
                gt_t[ex] = tok_t[ex]
                continue
            k = i * 4 + yy
            e_cp[k] = pltpu.make_async_remote_copy(
                src_ref=tok_t.at[to], dst_ref=gt_t.at[ex],
                send_sem=e_ss.at[k], recv_sem=e_rs.at[k],
                device_id=(dp, to), device_id_type=MESH,
            )
            e_cp[k].start()

    sum_back(0)
    out_gradient(0)
    out_gradient(1)
    sum_back(1)
    finish_chunk(0)
    out_gradient(2)
    out_gradient(3)
    put_gwo = pltpu.make_async_copy(gwo, gwo_h, out_sem.at[2])
    put_gwo.start()
    exchange(gn_cp, gain_r, gn_ss, gn_rs)
    exchange(cl_cp, col_r, cl_ss, cl_rs)
    sum_back(2)
    finish_chunk(1)

    gn_cp[0].wait_recv()
    cl_cp[0].wait_recv()
    total = 0.0
    for e in range(N):
        total += gain_r[e % 2, e // 2].astype(F32)
    small[...] = total
    for j in range(width // 128):
        gg_ref[0:1, j * 128 : (j + 1) * 128] = small[j : j + 1, :]
    for e in range(N):
        small[...] = col_r[e % 2, e // 2].astype(F32)
        for j in range(width // 128):
            gr_ref[e : e + 1, j * 128 : (j + 1) * 128] = small[j : j + 1, :]

    sum_back(3)
    finish_chunk(2)
    finish_chunk(3)

    for i in range(NC):
        c = (xm + NC - 1 - i) % 4
        for yy in range(4):
            if i < NC - 1 or yy:
                e_cp[i * 4 + yy].wait_recv()
        turned = gt_t[pl.ds(c * tokens4, tokens4)].reshape(part, rows).T
        tok[:, pl.ds(pl.multiple_of(c * part, part), part)] = turned
    put_gt = pltpu.make_async_copy(tok, gt_h, out_sem.at[3])
    put_gt.start()
    for copies in (
        ids_cp, raw_cp, b_cp, raw2_cp, c_cp, d_cp, sum2_cp, e_cp, gn_cp, cl_cp,
    ):
        for k in copies:
            copies[k].wait_send()
    put_norm.wait()
    put_gwi.wait()
    put_gwo.wait()
    put_gt.wait()


def store_kernel(pieces, *refs):
    count = len(pieces)
    sems = refs[2 * count]
    copies = []
    for k, cut in enumerate(pieces):
        size = refs[k].shape[0] // cut
        for i in range(cut):
            at = slice(i * size, (i + 1) * size)
            copies.append(
                pltpu.make_async_copy(refs[k].at[at, :], refs[count + k].at[at, :], sems.at[len(copies)])
            )
    for copy in copies:
        copy.start()
    for copy in copies:
        copy.wait()


def body(tokens, route_ids, router, norm_gain, w_in, w_out, cotangent):
    rows, width = tokens.shape[0], tokens.shape[2]
    hidden = w_in.shape[3]
    depth = 3 * rows // N
    slots = N * depth
    part = width // NC
    head = width // N
    group = 4 * depth
    shape = jax.ShapeDtypeStruct
    vmem = pl.BlockSpec(memory_space=pltpu.VMEM)
    anywhere = pl.BlockSpec(memory_space=pl.ANY)
    hbm = pl.BlockSpec(memory_space=pltpu.HBM)
    dma = pltpu.SemaphoreType.DMA
    keep = functools.partial(pltpu.with_memory_space_constraint, memory_space=pltpu.HBM)
    blocks = pltpu.VMEM((N, NC, depth, part), BF16)
    flipped = pltpu.VMEM((N, head, rows), BF16)
    row_block = pltpu.VMEM((rows, width), BF16)
    chunks = pltpu.VMEM((NC, rows, part), BF16)
    ids = pltpu.VMEM((8, rows), jnp.int32)
    out = pl.pallas_call(
        kernel,
        out_shape=(
            shape((rows, width), BF16),
            shape((rows, width), BF16),
            shape((N, width), F32),
            shape((1, width), F32),
            shape((width, hidden), BF16),
            shape((hidden, width), BF16),
        ),
        in_specs=[hbm] * 7,
        out_specs=[anywhere, anywhere, vmem, vmem, anywhere, anywhere],
        scratch_shapes=[
            row_block,
            pltpu.VMEM((2, rows), jnp.int32),
            pltpu.VMEM((N, width), BF16),
            pltpu.VMEM((1, width), F32),
            flipped,
            flipped,
            chunks,
            row_block,
            pltpu.VMEM((width, hidden), BF16),
            pltpu.VMEM((hidden, width), BF16),
            pltpu.VMEM((NC, N, part), BF16),
            ids, ids, ids,
            pltpu.VMEM((7 * depth, rows), BF16),
            pltpu.VMEM((7 * depth, rows), BF16),
            pltpu.VMEM((2 * depth, rows), BF16),
            pltpu.VMEM((rows, 7 * depth), BF16),
            pltpu.VMEM((rows, 7 * depth), BF16),
            pltpu.VMEM((rows, 2 * depth), BF16),
            chunks, chunks,
            blocks,
            blocks,
            pltpu.VMEM((slots, hidden), F32),
            pltpu.VMEM((slots, N), F32),
            pltpu.VMEM((slots, 1), F32),
            pltpu.VMEM((slots, hidden), BF16),
            blocks,
            blocks,
            chunks, chunks, chunks, chunks,
            pltpu.VMEM((NC, rows, part), F32),
            chunks,
            blocks,
            pltpu.VMEM((slots, hidden), BF16),
            blocks,
            pltpu.VMEM((slots, 1), F32),
            pltpu.VMEM((width, hidden), BF16),
            pltpu.VMEM((hidden, width), BF16),
            flipped,
            pltpu.VMEM((8, width), F32),
            pltpu.VMEM((8, width), F32),
            pltpu.VMEM((16, 128), F32),
            pltpu.VMEM((16, 128), BF16),
            pltpu.VMEM((2, RING, 16, 128), BF16),
            pltpu.VMEM((16, 128), BF16),
            pltpu.VMEM((2, RING, 16, 128), BF16),
            dma((7,)),
            dma((2,)), dma((2,)),
            dma((N,)), dma((N,)),
            dma((2, NC)), dma((2, NC)),
            dma((N, NC)), dma((N, NC)),
            dma((N,)), dma((N,)),
            dma((2, RUNS)), dma((2, RUNS)),
            dma((2, RUNS)), dma((2, RUNS)),
            dma((N,)), dma((N,)),
            dma((N, NC)), dma((N, NC)),
            dma((2, NC)), dma((2, NC)),
            dma((N,)), dma((N,)),
            dma((N,)), dma((N,)),
            dma((N,)), dma((N,)),
            dma((4,)),
        ],
        name="rank_mixer",
        compiler_params=pltpu.CompilerParams(
            collective_id=0, has_side_effects=True, vmem_limit_bytes=46 << 20
        ),
    )(
        keep(tokens.reshape(rows, width)),
        keep(route_ids.reshape(rows, 2).T),
        keep(router.reshape(width, N).T),
        keep(norm_gain.reshape(1, width)),
        keep(w_in.reshape(width, hidden)),
        keep(w_out.reshape(hidden, width)),
        keep(cotangent.reshape(rows, width)),
    )
    pieces = (2, 2, 1, 1, 4, 4)
    out = pl.pallas_call(
        functools.partial(store_kernel, pieces),
        out_shape=tuple(shape(v.shape, v.dtype) for v in out),
        in_specs=[anywhere] * 6,
        out_specs=[hbm] * 6,
        scratch_shapes=[dma((sum(pieces),))],
        name="store",
        compiler_params=pltpu.CompilerParams(vmem_limit_bytes=1 << 20),
    )(*out)
    normed_out, grad_tokens, grad_router, grad_gain, grad_w_in, grad_w_out = out
    return (
        normed_out.reshape(rows, 1, width),
        grad_tokens.reshape(rows, 1, width),
        grad_router.T.reshape(1, width, N),
        grad_gain,
        grad_w_in.reshape(1, 1, width, hidden),
        grad_w_out.reshape(1, 1, hidden, width),
    )


def solution(mesh):
    return jax.shard_map(
        body,
        mesh=mesh,
        in_specs=(
            P("dp", "expert", None),
            P("expert", "dp", None),
            P("expert", None, None),
            P("expert", None),
            P("expert", "dp", None, None),
            P("expert", "dp", None, None),
            P("dp", "expert", None),
        ),
        out_specs=(
            P("dp", "expert", None),
            P("dp", "expert", None),
            P("expert", None, None),
            P("expert", None),
            P("expert", "dp", None, None),
            P("expert", "dp", None, None),
        ),
        check_vma=False,
    )
```

```python
import functools

import jax
import jax.numpy as jnp
from jax import lax
from jax.experimental import pallas as pl
from jax.experimental.pallas import tpu as pltpu
from jax.sharding import PartitionSpec as P

MESH = pl.DeviceIdType.MESH
F32 = jnp.float32
BF16 = jnp.bfloat16

gelu_coef = 0.7978845608028654
cubic_coef = 0.044715
norm_eps = 1e-05

N = 16
NC = 4
NG = 4
RING = 8
STEPS = (0, 1, -1, 2, -2, 3, -3, 4)
HOPS = (0, 0, 0, 0, 0, 0, -1, -1, 1, 1, -2, -2, 2, 2, 3, -3)
FROM_LOW = (4, 5, 8, 9, 12, 13, 14)
FROM_HIGH = (2, 3, 6, 7, 10, 11, 15)
OWN = (0, 1)
HERE = (0, 2, 4)
AWAY = tuple(r for r in range(N) if r not in HERE)
TILE = 32
RUNS = 4


def dot(a, b):
    return lax.dot_general(a, b, (((1,), (0,)), ((), ())), preferred_element_type=F32)


def dot_nt(a, b):
    return lax.dot_general(a, b, (((1,), (1,)), ((), ())), preferred_element_type=F32)


def dot_tn(a, b):
    return lax.dot_general(a, b, (((0,), (0,)), ((), ())), preferred_element_type=F32)


def gelu_and_slope(value):
    inner = gelu_coef * (value + cubic_coef * value * value * value)
    tangent = jnp.tanh(inner)
    half = 0.5 * (1.0 + tangent)
    slope = half + 0.5 * value * (1.0 - tangent * tangent) * gelu_coef * (
        1.0 + 3.0 * cubic_coef * value * value
    )
    return value * half, slope


def kernel(
    tok_h, ids_h, rt_h, gain_h, win_h, wout_h, cot_h,
    no_h, gt_h, gr_ref, gg_ref, gwi_h, gwo_h,
    tok, ids_ref, rt_ref, gain_ref, tok_t, mix_t, mixed, cot, win, wout, rt4,
    ids_own, ids_low, ids_high, pl_m, ph_m, po_m, pl_t, ph_t, po_t,
    raw_lt, raw_ht, mix_lt, mix_ht, raw_l, raw_h, xs, xr, pre, logit, gate, act, ys, yr,
    part_l, part_h, sum_h, sum_l, acc, grd, gr, gp, ds, glog,
    gwi, gwo, gt_t, ggp, rcol, small,
    gain_s, gain_r, col_s, col_r,
    load_sem, ids_ss, ids_rs, mix_ss, mix_rs, raw_ss, raw_rs, side_ss, side_rs, a_ss, a_rs, b_ss, b_rs,
    sum_ss, sum_rs, raw2_ss, raw2_rs, c_ss, c_rs, d_ss, d_rs, sum2_ss, sum2_rs,
    e_ss, e_rs, gn_ss, gn_rs, cl_ss, cl_rs, out_sem,
):
    rows, width = tok.shape
    head = width // N
    part = width // NC
    hidden = win.shape[1]
    depth = xs.shape[2]
    group = depth * 4
    slots = N * depth
    tokens4 = N // NC
    dp = lax.axis_index("dp")
    ex = lax.axis_index("expert")
    z, co = dp // 2, dp % 2
    xm, ym = ex // 4, ex % 4

    def partner(r):
        return ((z + STEPS[r // 2] + RING) % RING) * 2 + (co + r % 2) % 2

    def target(r):
        return ((z + HOPS[r] + RING) % RING) * 2 + (co + r % 2) % 2

    def origin(r):
        return ((z - HOPS[r] + RING) % RING) * 2 + (co + r % 2) % 2

    high = ((z + 1) % RING) * 2 + co
    low = ((z + RING - 1) % RING) * 2 + co

    def send(src, dst, send_sem, recv_sem, to):
        copy = pltpu.make_async_remote_copy(
            src_ref=src, dst_ref=dst, send_sem=send_sem, recv_sem=recv_sem,
            device_id=(to, ex), device_id_type=MESH,
        )
        copy.start()
        return copy

    def load(src, dst, k):
        copy = pltpu.make_async_copy(src, dst, load_sem.at[k])
        copy.start()
        return copy

    got_tok = load(tok_h, tok, 0)
    got_ids = load(ids_h, ids_ref, 1)

    barrier = pltpu.get_barrier_semaphore()
    for r in range(1, N):
        pl.semaphore_signal(barrier, inc=1, device_id=(partner(r), ex), device_id_type=MESH)
    for k in range(1, N):
        pl.semaphore_signal(barrier, inc=1, device_id=(dp, (ex + k) % N), device_id_type=MESH)
    got_tok.wait()
    got_ids.wait()
    got_win = load(win_h, win, 4)
    got_wout = load(wout_h, wout, 5)
    got_rt = load(rt_h, rt_ref, 2)
    got_gain = load(gain_h, gain_ref, 3)
    got_cot = load(cot_h, cot, 6)
    ids_own[...] = jnp.zeros_like(ids_own)
    ids_own[0:2, :] = ids_ref[...]

    ids_cp, raw_cp, mix_cp = {}, {}, {}
    for i in range(NC):
        c = (xm - i + 4) % 4
        turned = tok[:, pl.ds(pl.multiple_of(c * part, part), part)].T
        tok_t[pl.ds(c * tokens4, tokens4)] = turned.reshape(tokens4, head, rows)
        if i == 0:
            mix_t[ex] = tok_t[ex]
            pl.semaphore_wait(barrier, 2 * (N - 1))
        heads = pl.ds(c * tokens4, tokens4)
        raw_cp[0, i] = send(
            tok_t.at[heads], raw_lt.at[heads], raw_ss.at[0, i], raw_rs.at[0, i], high
        )
        raw_cp[1, i] = send(
            tok_t.at[heads], raw_ht.at[heads], raw_ss.at[1, i], raw_rs.at[1, i], low
        )
        for yy in range(4):
            k = i * 4 + yy
            to = c * 4 + (ym + yy) % 4
            if k == 0:
                continue
            mix_cp[k] = pltpu.make_async_remote_copy(
                src_ref=tok_t.at[to], dst_ref=mix_t.at[ex],
                send_sem=mix_ss.at[k], recv_sem=mix_rs.at[k],
                device_id=(dp, to), device_id_type=MESH,
            )
            mix_cp[k].start()
        if i == 0:
            ids_cp[0] = send(ids_own, ids_low, ids_ss.at[0], ids_rs.at[0], high)
            ids_cp[1] = send(ids_own, ids_high, ids_ss.at[1], ids_rs.at[1], low)

    label = lax.broadcasted_iota(jnp.int32, (N, rows), 0)
    earlier = (
        lax.broadcasted_iota(jnp.int32, (rows, rows), 0)
        < lax.broadcasted_iota(jnp.int32, (rows, rows), 1)
    ).astype(F32)
    earlier = earlier.astype(BF16)
    slot = lax.broadcasted_iota(jnp.int32, (depth, rows), 0)

    def place(ids, members, matrix, flipped):
        ids0, ids1 = ids[0:1, :], ids[1:2, :]
        hot0 = (label == ids0).astype(F32)
        hot1 = (label == ids1).astype(F32)
        before = dot((hot0 + hot1).astype(BF16), earlier)
        at0 = jnp.sum(before * hot0, axis=0, keepdims=True).astype(jnp.int32)
        at1 = jnp.sum(before * hot1, axis=0, keepdims=True).astype(jnp.int32)
        blocks = []
        for r in members:
            e = target(r)
            goal0 = jnp.where(ids0 == e, at0, -1)
            goal1 = jnp.where(ids1 == e, at1, -1)
            blocks.append(jnp.logical_or(slot == goal0, slot == goal1).astype(F32))
        placed = jnp.concatenate(blocks, axis=0)
        matrix[...] = placed.astype(BF16)
        flipped[...] = placed.T.astype(BF16)

    def stack(blocks, members, q):
        return jnp.concatenate([blocks[r, q] for r in members], axis=0)

    def expand(matrix, values, members, q, out, arrived):
        sent = dot(matrix[...], values).astype(BF16)
        for n, r in enumerate(members):
            into = arrived if r in HERE else out
            into[r, q] = sent[n * depth : (n + 1) * depth]

    a_cp, side_cp = {}, {}
    sides = ((raw_lt, mix_lt, raw_l), (raw_ht, mix_ht, raw_h))

    def send_mixed(r, i):
        c = (xm + i) % 4
        a_cp[r, i] = send(xs.at[r, c], xr.at[r, c], a_ss.at[r, i], a_rs.at[r, i], target(r))

    def relay(i):
        c = (xm - i + 4) % 4
        for n, (whole, gathered, _) in enumerate(sides):
            raw_cp[n, i].wait_recv()
            for yy in range(4):
                k = i * 4 + yy
                to = c * 4 + (ym + yy) % 4
                if k == 0:
                    gathered[ex] = whole[ex]
                    continue
                side_cp[n, k] = pltpu.make_async_remote_copy(
                    src_ref=whole.at[to], dst_ref=gathered.at[ex],
                    send_sem=side_ss.at[n, k], recv_sem=side_rs.at[n, k],
                    device_id=(dp, to), device_id_type=MESH,
                )
                side_cp[n, k].start()

    def own_chunk(i):
        c = (xm + i) % 4
        for yy in range(4):
            if i * 4 + yy:
                mix_cp[i * 4 + yy].wait_recv()
        mixed[c] = mix_t[pl.ds(c * tokens4, tokens4)].reshape(part, rows).T
        expand(po_m, mixed[c], OWN, c, xs, xr)
        send_mixed(1, i)

    def pass_on(i):
        c = (xm + i) % 4
        for n, (_, gathered, plain) in enumerate(sides):
            for yy in range(4):
                if i * 4 + yy:
                    side_cp[n, i * 4 + yy].wait_recv()
            plain[c] = gathered[pl.ds(c * tokens4, tokens4)].reshape(part, rows).T
            if n == 0:
                expand(pl_m, plain[c], FROM_LOW, c, xs, xr)
            else:
                expand(ph_m, plain[c], FROM_HIGH, c, xs, xr)
        for r in AWAY[1:]:
            send_mixed(r, i)

    place(ids_own, OWN, po_m, po_t)
    ids_cp[0].wait_recv()
    ids_cp[1].wait_recv()
    place(ids_low, FROM_LOW, pl_m, pl_t)
    place(ids_high, FROM_HIGH, ph_m, ph_t)
    relay(0)
    for i in range(NC):
        own_chunk(i)
        if i + 1 < NC:
            relay(i + 1)
        pass_on(i)

    got_rt.wait()
    got_win.wait()
    got_wout.wait()
    for c in range(NC):
        rt4[c] = rt_ref[:, c * part : (c + 1) * part]
    mine = lax.broadcasted_iota(jnp.int32, (group, N), 1) == dp
    for i in range(NC - 1):
        c = (xm + i) % 4
        for r in AWAY:
            a_cp[r, i].wait_recv()
        for g in range(NG):
            at = slice(g * group, (g + 1) * group)
            block = xr[4 * g : 4 * g + 4, c].reshape(group, part)
            more = dot(block, win[pl.ds(pl.multiple_of(c * part, part), part), :])
            more_logit = dot_nt(block, rt4[c])
            if i == 0:
                pre[at, :] = more
                logit[at, :] = more_logit
            else:
                pre[at, :] += more
                logit[at, :] += more_logit
    b_cp = {}
    c = (xm + NC - 1) % 4
    for g in range(NG):
        at = slice(g * group, (g + 1) * group)
        for r in range(4 * g, 4 * g + 4):
            if r in AWAY:
                a_cp[r, NC - 1].wait_recv()
        block = xr[4 * g : 4 * g + 4, c].reshape(group, part)
        value = pre[at, :] + dot(block, win[pl.ds(pl.multiple_of(c * part, part), part), :])
        score = logit[at, :] + dot_nt(block, rt4[c])
        share = jax.nn.sigmoid(jnp.sum(jnp.where(mine, score, 0.0), axis=1, keepdims=True))
        gate[at, :] = share
        activated, slope = gelu_and_slope(value)
        pre[at, :] = slope
        act[at, :] = activated.astype(BF16)
        for q in range(NC):
            out = dot(act[at, :], wout[:, q * part : (q + 1) * part])
            result = (share * out).astype(BF16).reshape(4, depth, part)
            ys[4 * g : 4 * g + 4, q] = result
            for r in range(4 * g, 4 * g + 4):
                if r in HERE:
                    yr[r, q] = result[r - 4 * g]
        for r in range(4 * g, 4 * g + 4):
            if r in AWAY:
                b_cp[r] = send(ys.at[r], yr.at[r], b_ss.at[r], b_rs.at[r], origin(r))

    sum_cp = {}
    for r in AWAY:
        b_cp[r].wait_recv()
    run = rows // RUNS
    for i in range(RUNS):
        at = slice(i * run, (i + 1) * run)
        for q in range(NC):
            part_l[q, at] = dot(pl_t[at, :], stack(yr, FROM_LOW, q)).astype(BF16)
        sum_cp[0, i] = send(
            part_l.at[:, at, :], sum_h.at[:, at, :], sum_ss.at[0, i], sum_rs.at[0, i], low
        )
        for q in range(NC):
            part_h[q, at] = dot(ph_t[at, :], stack(yr, FROM_HIGH, q)).astype(BF16)
        sum_cp[1, i] = send(
            part_h.at[:, at, :], sum_l.at[:, at, :], sum_ss.at[1, i], sum_rs.at[1, i], high
        )
    for q in range(NC):
        acc[q] = mixed[q].astype(F32) + dot(po_t[...], stack(yr, OWN, q))
    got_cot.wait()
    got_gain.wait()
    ggp[...] = jnp.zeros_like(ggp)

    def norm_rows(j, carry):
        at = pl.ds(pl.multiple_of(j * TILE, TILE), TILE)
        cols = [slice(q * part, (q + 1) * part) for q in range(NC)]
        resid = [
            acc[q, at, :] + sum_h[q, at, :].astype(F32) + sum_l[q, at, :].astype(F32)
            for q in range(NC)
        ]
        mean = sum(jnp.sum(v, axis=1, keepdims=True) for v in resid) / width
        resid = [v - mean for v in resid]
        var = sum(jnp.sum(v * v, axis=1, keepdims=True) for v in resid) / width
        inv_std = lax.rsqrt(var + norm_eps)
        normed = [v * inv_std for v in resid]
        grads, m1, m2 = [], 0.0, 0.0
        for q in range(NC):
            gain = gain_ref[0:1, cols[q]]
            cot_f = cot[at, cols[q]].astype(F32)
            cot[at, cols[q]] = (normed[q] * gain).astype(BF16)
            ggp[0:1, cols[q]] += jnp.sum(cot_f * normed[q], axis=0, keepdims=True)
            grad = cot_f * gain
            grads.append(grad)
            m1 += jnp.sum(grad, axis=1, keepdims=True)
            m2 += jnp.sum(grad * normed[q], axis=1, keepdims=True)
        m1, m2 = m1 / width, m2 / width
        for q in range(NC):
            grad = inv_std * (grads[q] - m1 - normed[q] * m2)
            acc[q, at, :] = grad
            grd[q, at, :] = grad.astype(BF16)
        return carry

    raw2_cp, c_cp = {}, {}
    for i in range(RUNS):
        sum_cp[0, i].wait_recv()
        sum_cp[1, i].wait_recv()
        lax.fori_loop(i * run // TILE, (i + 1) * run // TILE, norm_rows, 0)
        src = grd.at[:, i * run : (i + 1) * run, :]
        to_high, to_low = (d.at[:, i * run : (i + 1) * run, :] for d in (raw_l, raw_h))
        raw2_cp[0, i] = send(src, to_high, raw2_ss.at[0, i], raw2_rs.at[0, i], high)
        raw2_cp[1, i] = send(src, to_low, raw2_ss.at[1, i], raw2_rs.at[1, i], low)

    def spread(vector, source, target, gathered, send_sems, recv_sems):
        source[...] = jnp.zeros_like(source)
        for j in range(width // 128):
            source[j : j + 1, :] = vector[0:1, j * 128 : (j + 1) * 128]
        target[...] = source[...].astype(BF16)
        gathered[co, z] = target[...]
        copies = {}
        for k in range(1, RING):
            copies[k] = send(
                target, gathered.at[co, z], send_sems.at[k], recv_sems.at[k],
                ((z + k) % RING) * 2 + co,
            )
        return copies

    def exchange(copies, gathered, send_sems, recv_sems):
        for k in range(1, RING):
            copies[k].wait_recv()
        copies[0] = send(
            gathered.at[co], gathered.at[co], send_sems.at[0], recv_sems.at[0],
            z * 2 + (co + 1) % 2,
        )

    gn_cp = spread(ggp, small, gain_s, gain_r, gn_ss, gn_rs)
    put_norm = pltpu.make_async_copy(cot, no_h, out_sem.at[0])
    put_norm.start()
    for copies in (mix_cp, raw_cp):
        for k in copies:
            copies[k].wait_send()
    for k in a_cp:
        a_cp[k].wait_send()
    for k in sum_cp:
        sum_cp[k].wait_send()
    for q in range(NC):
        expand(po_m, grd[q], OWN, q, xs, gr)
    for i in range(RUNS):
        raw2_cp[0, i].wait_recv()
        raw2_cp[1, i].wait_recv()
    for q in range(NC):
        expand(pl_m, raw_l[q], FROM_LOW, q, xs, gr)
        expand(ph_m, raw_h[q], FROM_HIGH, q, xs, gr)
    for r in AWAY:
        c_cp[r] = send(xs.at[r], gr.at[r], c_ss.at[r], c_rs.at[r], target(r))

    rcol[...] = jnp.zeros_like(rcol)
    mine_row = lax.broadcasted_iota(jnp.int32, (N, part), 0) == dp
    d_cp = {}

    def send_back(r, i):
        c = (xm + 1 + i) % 4
        d_cp[r, i] = send(ds.at[r, c], yr.at[r, c], d_ss.at[r, i], d_rs.at[r, i], origin(r))

    for g in range(NG):
        at = slice(g * group, (g + 1) * group)
        for r in range(4 * g, 4 * g + 4):
            if r in AWAY:
                c_cp[r].wait_recv()
        share = gate[at, :]
        grad_act, grad_gate = 0.0, 0.0
        for q in range(NC):
            grad = gr[4 * g : 4 * g + 4, q].reshape(group, part).astype(F32)
            result = ys[4 * g : 4 * g + 4, q].reshape(group, part).astype(F32)
            grad_gate += jnp.sum(grad * result, axis=1, keepdims=True)
            grad_out = (share * grad).astype(BF16)
            gr[4 * g : 4 * g + 4, q] = grad_out.reshape(4, depth, part)
            grad_act += dot_nt(grad_out, wout[:, q * part : (q + 1) * part])
        grad_logit = grad_gate * (1.0 - share)
        glog[at, :] = grad_logit
        gp[at, :] = (grad_act * pre[at, :]).astype(BF16)
        for i in range(NC):
            c = (xm + 1 + i) % 4
            weights = jnp.sum(jnp.where(mine_row, rt4[c].astype(F32), 0.0), axis=0, keepdims=True)
            back = dot_nt(gp[at, :], win[pl.ds(pl.multiple_of(c * part, part), part), :])
            back = (back + grad_logit * weights).astype(BF16).reshape(4, depth, part)
            ds[4 * g : 4 * g + 4, c] = back
            for r in range(4 * g, 4 * g + 4):
                if r in HERE:
                    yr[r, c] = back[r - 4 * g]
                else:
                    send_back(r, i)

    for g in range(NG):
        at = slice(g * group, (g + 1) * group)
        for q in range(NC):
            block = xr[4 * g : 4 * g + 4, q].reshape(group, part).astype(F32)
            rcol[0:1, q * part : (q + 1) * part] += jnp.sum(
                glog[at, :] * block, axis=0, keepdims=True
            )
    cl_cp = spread(rcol, small, col_s, col_r, cl_ss, cl_rs)
    for q in range(NC):
        cols = slice(q * part, (q + 1) * part)
        gwi[cols, :] = dot_tn(xr[:, q].reshape(slots, part), gp[...]).astype(BF16)
    put_gwi = pltpu.make_async_copy(gwi, gwi_h, out_sem.at[1])
    put_gwi.start()

    def out_gradient(q):
        gwo[:, q * part : (q + 1) * part] = dot_tn(act[...], gr[:, q].reshape(slots, part)).astype(BF16)

    sum2_cp, e_cp = {}, {}

    def sum_back(i):
        c = (xm + 1 + i) % 4
        for r in AWAY:
            d_cp[r, i].wait_recv()
        part_l[c] = dot(pl_t[...], stack(yr, FROM_LOW, c)).astype(BF16)
        sum2_cp[0, i] = send(part_l.at[c], sum_h.at[c], sum2_ss.at[0, i], sum2_rs.at[0, i], low)
        part_h[c] = dot(ph_t[...], stack(yr, FROM_HIGH, c)).astype(BF16)
        sum2_cp[1, i] = send(part_h.at[c], sum_l.at[c], sum2_ss.at[1, i], sum2_rs.at[1, i], high)
        acc[c] += dot(po_t[...], stack(yr, OWN, c))

    def finish_chunk(i):
        c = (xm + 1 + i) % 4
        sum2_cp[0, i].wait_recv()
        sum2_cp[1, i].wait_recv()
        total = acc[c] + sum_h[c].astype(F32) + sum_l[c].astype(F32)
        tok_t[pl.ds(c * tokens4, tokens4)] = total.astype(BF16).T.reshape(tokens4, head, rows)
        for yy in range(4):
            to = c * tokens4 + (ym + yy) % 4
            if i == NC - 1 and yy == 0:
                gt_t[ex] = tok_t[ex]
                continue
            k = i * 4 + yy
            e_cp[k] = pltpu.make_async_remote_copy(
                src_ref=tok_t.at[to], dst_ref=gt_t.at[ex],
                send_sem=e_ss.at[k], recv_sem=e_rs.at[k],
                device_id=(dp, to), device_id_type=MESH,
            )
            e_cp[k].start()

    sum_back(0)
    out_gradient(0)
    out_gradient(1)
    sum_back(1)
    finish_chunk(0)
    out_gradient(2)
    out_gradient(3)
    put_gwo = pltpu.make_async_copy(gwo, gwo_h, out_sem.at[2])
    put_gwo.start()
    exchange(gn_cp, gain_r, gn_ss, gn_rs)
    exchange(cl_cp, col_r, cl_ss, cl_rs)
    sum_back(2)
    finish_chunk(1)

    gn_cp[0].wait_recv()
    cl_cp[0].wait_recv()
    total = 0.0
    for e in range(N):
        total += gain_r[e % 2, e // 2].astype(F32)
    small[...] = total
    for j in range(width // 128):
        gg_ref[0:1, j * 128 : (j + 1) * 128] = small[j : j + 1, :]
    for e in range(N):
        small[...] = col_r[e % 2, e // 2].astype(F32)
        for j in range(width // 128):
            gr_ref[e : e + 1, j * 128 : (j + 1) * 128] = small[j : j + 1, :]

    sum_back(3)
    finish_chunk(2)
    finish_chunk(3)

    for i in range(NC):
        c = (xm + NC - 1 - i) % 4
        for yy in range(4):
            if i < NC - 1 or yy:
                e_cp[i * 4 + yy].wait_recv()
        turned = gt_t[pl.ds(c * tokens4, tokens4)].reshape(part, rows).T
        tok[:, pl.ds(pl.multiple_of(c * part, part), part)] = turned
    put_gt = pltpu.make_async_copy(tok, gt_h, out_sem.at[3])
    put_gt.start()
    for copies in (
        ids_cp, side_cp, b_cp, raw2_cp, c_cp, d_cp, sum2_cp, e_cp, gn_cp, cl_cp,
    ):
        for k in copies:
            copies[k].wait_send()
    put_norm.wait()
    put_gwi.wait()
    put_gwo.wait()
    put_gt.wait()


def store_kernel(pieces, *refs):
    count = len(pieces)
    sems = refs[2 * count]
    copies = []
    for k, cut in enumerate(pieces):
        size = refs[k].shape[0] // cut
        for i in range(cut):
            at = slice(i * size, (i + 1) * size)
            copies.append(
                pltpu.make_async_copy(refs[k].at[at, :], refs[count + k].at[at, :], sems.at[len(copies)])
            )
    for copy in copies:
        copy.start()
    for copy in copies:
        copy.wait()


def body(tokens, route_ids, router, norm_gain, w_in, w_out, cotangent):
    rows, width = tokens.shape[0], tokens.shape[2]
    hidden = w_in.shape[3]
    depth = 3 * rows // N
    slots = N * depth
    part = width // NC
    head = width // N
    group = 4 * depth
    shape = jax.ShapeDtypeStruct
    vmem = pl.BlockSpec(memory_space=pltpu.VMEM)
    anywhere = pl.BlockSpec(memory_space=pl.ANY)
    hbm = pl.BlockSpec(memory_space=pltpu.HBM)
    dma = pltpu.SemaphoreType.DMA
    keep = functools.partial(pltpu.with_memory_space_constraint, memory_space=pltpu.HBM)
    blocks = pltpu.VMEM((N, NC, depth, part), BF16)
    flipped = pltpu.VMEM((N, head, rows), BF16)
    row_block = pltpu.VMEM((rows, width), BF16)
    chunks = pltpu.VMEM((NC, rows, part), BF16)
    ids = pltpu.VMEM((8, rows), jnp.int32)
    out = pl.pallas_call(
        kernel,
        out_shape=(
            shape((rows, width), BF16),
            shape((rows, width), BF16),
            shape((N, width), F32),
            shape((1, width), F32),
            shape((width, hidden), BF16),
            shape((hidden, width), BF16),
        ),
        in_specs=[hbm] * 7,
        out_specs=[anywhere, anywhere, vmem, vmem, anywhere, anywhere],
        scratch_shapes=[
            row_block,
            pltpu.VMEM((2, rows), jnp.int32),
            pltpu.VMEM((N, width), BF16),
            pltpu.VMEM((1, width), F32),
            flipped,
            flipped,
            chunks,
            row_block,
            pltpu.VMEM((width, hidden), BF16),
            pltpu.VMEM((hidden, width), BF16),
            pltpu.VMEM((NC, N, part), BF16),
            ids, ids, ids,
            pltpu.VMEM((7 * depth, rows), BF16),
            pltpu.VMEM((7 * depth, rows), BF16),
            pltpu.VMEM((2 * depth, rows), BF16),
            pltpu.VMEM((rows, 7 * depth), BF16),
            pltpu.VMEM((rows, 7 * depth), BF16),
            pltpu.VMEM((rows, 2 * depth), BF16),
            flipped, flipped, flipped, flipped,
            chunks, chunks,
            blocks,
            blocks,
            pltpu.VMEM((slots, hidden), F32),
            pltpu.VMEM((slots, N), F32),
            pltpu.VMEM((slots, 1), F32),
            pltpu.VMEM((slots, hidden), BF16),
            blocks,
            blocks,
            chunks, chunks, chunks, chunks,
            pltpu.VMEM((NC, rows, part), F32),
            chunks,
            blocks,
            pltpu.VMEM((slots, hidden), BF16),
            blocks,
            pltpu.VMEM((slots, 1), F32),
            pltpu.VMEM((width, hidden), BF16),
            pltpu.VMEM((hidden, width), BF16),
            flipped,
            pltpu.VMEM((8, width), F32),
            pltpu.VMEM((8, width), F32),
            pltpu.VMEM((16, 128), F32),
            pltpu.VMEM((16, 128), BF16),
            pltpu.VMEM((2, RING, 16, 128), BF16),
            pltpu.VMEM((16, 128), BF16),
            pltpu.VMEM((2, RING, 16, 128), BF16),
            dma((7,)),
            dma((2,)), dma((2,)),
            dma((N,)), dma((N,)),
            dma((2, NC)), dma((2, NC)),
            dma((2, N)), dma((2, N)),
            dma((N, NC)), dma((N, NC)),
            dma((N,)), dma((N,)),
            dma((2, RUNS)), dma((2, RUNS)),
            dma((2, RUNS)), dma((2, RUNS)),
            dma((N,)), dma((N,)),
            dma((N, NC)), dma((N, NC)),
            dma((2, NC)), dma((2, NC)),
            dma((N,)), dma((N,)),
            dma((N,)), dma((N,)),
            dma((N,)), dma((N,)),
            dma((4,)),
        ],
        name="rank_mixer",
        compiler_params=pltpu.CompilerParams(
            collective_id=0, has_side_effects=True, vmem_limit_bytes=46 << 20
        ),
    )(
        keep(tokens.reshape(rows, width)),
        keep(route_ids.reshape(rows, 2).T),
        keep(router.reshape(width, N).T),
        keep(norm_gain.reshape(1, width)),
        keep(w_in.reshape(width, hidden)),
        keep(w_out.reshape(hidden, width)),
        keep(cotangent.reshape(rows, width)),
    )
    pieces = (2, 2, 1, 1, 4, 4)
    out = pl.pallas_call(
        functools.partial(store_kernel, pieces),
        out_shape=tuple(shape(v.shape, v.dtype) for v in out),
        in_specs=[anywhere] * 6,
        out_specs=[hbm] * 6,
        scratch_shapes=[dma((sum(pieces),))],
        name="store",
        compiler_params=pltpu.CompilerParams(vmem_limit_bytes=1 << 20),
    )(*out)
    normed_out, grad_tokens, grad_router, grad_gain, grad_w_in, grad_w_out = out
    return (
        normed_out.reshape(rows, 1, width),
        grad_tokens.reshape(rows, 1, width),
        grad_router.T.reshape(1, width, N),
        grad_gain,
        grad_w_in.reshape(1, 1, width, hidden),
        grad_w_out.reshape(1, 1, hidden, width),
    )


def solution(mesh):
    return jax.shard_map(
        body,
        mesh=mesh,
        in_specs=(
            P("dp", "expert", None),
            P("expert", "dp", None),
            P("expert", None, None),
            P("expert", None),
            P("expert", "dp", None, None),
            P("expert", "dp", None, None),
            P("dp", "expert", None),
        ),
        out_specs=(
            P("dp", "expert", None),
            P("dp", "expert", None),
            P("expert", None, None),
            P("expert", None),
            P("expert", "dp", None, None),
            P("expert", "dp", None, None),
        ),
        check_vma=False,
    )
```

```python
import functools

import jax
import jax.numpy as jnp
from jax import lax
from jax.experimental import pallas as pl
from jax.experimental.pallas import tpu as pltpu
from jax.sharding import PartitionSpec as P

MESH = pl.DeviceIdType.MESH
F32 = jnp.float32
BF16 = jnp.bfloat16

gelu_coef = 0.7978845608028654
cubic_coef = 0.044715
norm_eps = 1e-05

N = 16
NC = 4
NG = 4
RING = 8
STEPS = (0, 1, -1, 2, -2, 3, -3, 4)
HOPS = (0, 0, 0, 0, 0, 0, -1, -1, 1, 1, -2, -2, 2, 2, 3, -3)
FROM_LOW = (4, 5, 8, 9, 12, 13, 14)
FROM_HIGH = (2, 3, 6, 7, 10, 11, 15)
OWN = (0, 1)
HERE = (0, 2, 4)
AWAY = tuple(r for r in range(N) if r not in HERE)
TILE = 32
RUNS = 4


def dot(a, b):
    return lax.dot_general(a, b, (((1,), (0,)), ((), ())), preferred_element_type=F32)


def dot_nt(a, b):
    return lax.dot_general(a, b, (((1,), (1,)), ((), ())), preferred_element_type=F32)


def dot_tn(a, b):
    return lax.dot_general(a, b, (((0,), (0,)), ((), ())), preferred_element_type=F32)


def gelu_and_slope(value):
    inner = gelu_coef * (value + cubic_coef * value * value * value)
    tangent = jnp.tanh(inner)
    half = 0.5 * (1.0 + tangent)
    slope = half + 0.5 * value * (1.0 - tangent * tangent) * gelu_coef * (
        1.0 + 3.0 * cubic_coef * value * value
    )
    return value * half, slope


def kernel(
    tok_h, ids_h, rt_h, gain_h, win_h, wout_h, cot_h,
    no_h, gt_h, gr_ref, gg_ref, gwi_h, gwo_h,
    tok, ids_ref, rt_ref, gain_ref, tok_t, mix_t, mixed, cot, win, wout, rt4,
    ids_own, ids_low, ids_high, pl_m, ph_m, po_m, pl_t, ph_t, po_t,
    raw_lt, raw_ht, mix_lt, mix_ht, raw_l, raw_h, xs, xr, pre, logit, gate, act, ys, yr,
    part_l, part_h, sum_h, sum_l, acc, grd, gr, gp, ds, glog,
    gwi, gwo, gt_t, ggp, rcol, small,
    gain_s, gain_r, col_s, col_r,
    load_sem, ids_ss, ids_rs, mix_ss, mix_rs, raw_ss, raw_rs, side_ss, side_rs, a_ss, a_rs, b_ss, b_rs,
    sum_ss, sum_rs, raw2_ss, raw2_rs, c_ss, c_rs, d_ss, d_rs, sum2_ss, sum2_rs,
    e_ss, e_rs, gn_ss, gn_rs, cl_ss, cl_rs, out_sem,
):
    rows, width = tok.shape
    head = width // N
    part = width // NC
    hidden = win.shape[1]
    depth = xs.shape[2]
    group = depth * 4
    slots = N * depth
    tokens4 = N // NC
    dp = lax.axis_index("dp")
    ex = lax.axis_index("expert")
    z, co = dp // 2, dp % 2
    xm, ym = ex // 4, ex % 4

    def partner(r):
        return ((z + STEPS[r // 2] + RING) % RING) * 2 + (co + r % 2) % 2

    def target(r):
        return ((z + HOPS[r] + RING) % RING) * 2 + (co + r % 2) % 2

    def origin(r):
        return ((z - HOPS[r] + RING) % RING) * 2 + (co + r % 2) % 2

    high = ((z + 1) % RING) * 2 + co
    low = ((z + RING - 1) % RING) * 2 + co

    def send(src, dst, send_sem, recv_sem, to):
        copy = pltpu.make_async_remote_copy(
            src_ref=src, dst_ref=dst, send_sem=send_sem, recv_sem=recv_sem,
            device_id=(to, ex), device_id_type=MESH,
        )
        copy.start()
        return copy

    def load(src, dst, k):
        copy = pltpu.make_async_copy(src, dst, load_sem.at[k])
        copy.start()
        return copy

    got_tok = load(tok_h, tok, 0)
    got_ids = load(ids_h, ids_ref, 1)

    barrier = pltpu.get_barrier_semaphore()
    for r in range(1, N):
        pl.semaphore_signal(barrier, inc=1, device_id=(partner(r), ex), device_id_type=MESH)
    for k in range(1, N):
        pl.semaphore_signal(barrier, inc=1, device_id=(dp, (ex + k) % N), device_id_type=MESH)
    got_tok.wait()
    got_ids.wait()
    got_win = load(win_h, win, 4)
    got_wout = load(wout_h, wout, 5)
    got_rt = load(rt_h, rt_ref, 2)
    got_gain = load(gain_h, gain_ref, 3)
    got_cot = load(cot_h, cot, 6)
    ids_own[...] = jnp.zeros_like(ids_own)
    ids_own[0:2, :] = ids_ref[...]

    ids_cp, raw_cp, mix_cp = {}, {}, {}
    for i in range(NC):
        c = (xm - i + 4) % 4
        turned = tok[:, pl.ds(pl.multiple_of(c * part, part), part)].T
        tok_t[pl.ds(c * tokens4, tokens4)] = turned.reshape(tokens4, head, rows)
        if i == 0:
            mix_t[ex] = tok_t[ex]
            pl.semaphore_wait(barrier, 2 * (N - 1))
        heads = pl.ds(c * tokens4, tokens4)
        raw_cp[0, i] = send(
            tok_t.at[heads], raw_lt.at[heads], raw_ss.at[0, i], raw_rs.at[0, i], high
        )
        raw_cp[1, i] = send(
            tok_t.at[heads], raw_ht.at[heads], raw_ss.at[1, i], raw_rs.at[1, i], low
        )
        for yy in range(4):
            k = i * 4 + yy
            to = c * 4 + (ym + yy) % 4
            if k == 0:
                continue
            mix_cp[k] = pltpu.make_async_remote_copy(
                src_ref=tok_t.at[to], dst_ref=mix_t.at[ex],
                send_sem=mix_ss.at[k], recv_sem=mix_rs.at[k],
                device_id=(dp, to), device_id_type=MESH,
            )
            mix_cp[k].start()
        if i == 0:
            ids_cp[0] = send(ids_own, ids_low, ids_ss.at[0], ids_rs.at[0], high)
            ids_cp[1] = send(ids_own, ids_high, ids_ss.at[1], ids_rs.at[1], low)

    label = lax.broadcasted_iota(jnp.int32, (N, rows), 0)
    earlier = (
        lax.broadcasted_iota(jnp.int32, (rows, rows), 0)
        < lax.broadcasted_iota(jnp.int32, (rows, rows), 1)
    ).astype(F32)
    earlier = earlier.astype(BF16)
    slot = lax.broadcasted_iota(jnp.int32, (depth, rows), 0)

    def place(ids, members, matrix, flipped):
        ids0, ids1 = ids[0:1, :], ids[1:2, :]
        hot0 = (label == ids0).astype(F32)
        hot1 = (label == ids1).astype(F32)
        before = dot((hot0 + hot1).astype(BF16), earlier)
        at0 = jnp.sum(before * hot0, axis=0, keepdims=True).astype(jnp.int32)
        at1 = jnp.sum(before * hot1, axis=0, keepdims=True).astype(jnp.int32)
        blocks = []
        for r in members:
            e = target(r)
            goal0 = jnp.where(ids0 == e, at0, -1)
            goal1 = jnp.where(ids1 == e, at1, -1)
            blocks.append(jnp.logical_or(slot == goal0, slot == goal1).astype(F32))
        placed = jnp.concatenate(blocks, axis=0)
        matrix[...] = placed.astype(BF16)
        flipped[...] = placed.T.astype(BF16)

    def stack(blocks, members, q):
        return jnp.concatenate([blocks[r, q] for r in members], axis=0)

    def expand(matrix, values, members, q, out, arrived, first=0):
        at = slice(first * depth, (first + len(members)) * depth)
        sent = dot(matrix[at, :], values).astype(BF16)
        for n, r in enumerate(members):
            into = arrived if r in HERE else out
            into[r, q] = sent[n * depth : (n + 1) * depth]

    a_cp, side_cp = {}, {}
    sides = ((raw_lt, mix_lt, raw_l), (raw_ht, mix_ht, raw_h))

    def send_mixed(r, i):
        c = (xm + i) % 4
        a_cp[r, i] = send(xs.at[r, c], xr.at[r, c], a_ss.at[r, i], a_rs.at[r, i], target(r))

    def relay(i):
        c = (xm - i + 4) % 4
        for n, (whole, gathered, _) in enumerate(sides):
            raw_cp[n, i].wait_recv()
            for yy in range(4):
                k = i * 4 + yy
                to = c * 4 + (ym + yy) % 4
                if k == 0:
                    gathered[ex] = whole[ex]
                    continue
                side_cp[n, k] = pltpu.make_async_remote_copy(
                    src_ref=whole.at[to], dst_ref=gathered.at[ex],
                    send_sem=side_ss.at[n, k], recv_sem=side_rs.at[n, k],
                    device_id=(dp, to), device_id_type=MESH,
                )
                side_cp[n, k].start()

    def own_chunk(i):
        c = (xm + i) % 4
        for yy in range(4):
            if i * 4 + yy:
                mix_cp[i * 4 + yy].wait_recv()
        mixed[c] = mix_t[pl.ds(c * tokens4, tokens4)].reshape(part, rows).T
        expand(po_m, mixed[c], OWN, c, xs, xr)
        send_mixed(1, i)

    def pass_on(i):
        c = (xm + i) % 4
        for n, (_, gathered, plain) in enumerate(sides):
            for yy in range(4):
                if i * 4 + yy:
                    side_cp[n, i * 4 + yy].wait_recv()
            plain[c] = gathered[pl.ds(c * tokens4, tokens4)].reshape(part, rows).T
            if n == 0:
                expand(pl_m, plain[c], FROM_LOW, c, xs, xr)
            else:
                expand(ph_m, plain[c], FROM_HIGH, c, xs, xr)
        for r in AWAY[1:]:
            send_mixed(r, i)

    place(ids_own, OWN, po_m, po_t)
    ids_cp[0].wait_recv()
    ids_cp[1].wait_recv()
    place(ids_low, FROM_LOW, pl_m, pl_t)
    place(ids_high, FROM_HIGH, ph_m, ph_t)
    relay(0)
    for i in range(NC):
        own_chunk(i)
        if i + 1 < NC:
            relay(i + 1)
        pass_on(i)

    got_rt.wait()
    got_win.wait()
    got_wout.wait()
    for c in range(NC):
        rt4[c] = rt_ref[:, c * part : (c + 1) * part]
    mine = lax.broadcasted_iota(jnp.int32, (group, N), 1) == dp
    for i in range(NC - 1):
        c = (xm + i) % 4
        for r in AWAY:
            a_cp[r, i].wait_recv()
        for g in range(NG):
            at = slice(g * group, (g + 1) * group)
            block = xr[4 * g : 4 * g + 4, c].reshape(group, part)
            more = dot(block, win[pl.ds(pl.multiple_of(c * part, part), part), :])
            more_logit = dot_nt(block, rt4[c])
            if i == 0:
                pre[at, :] = more
                logit[at, :] = more_logit
            else:
                pre[at, :] += more
                logit[at, :] += more_logit
    b_cp = {}
    c = (xm + NC - 1) % 4
    for g in range(NG):
        at = slice(g * group, (g + 1) * group)
        for r in range(4 * g, 4 * g + 4):
            if r in AWAY:
                a_cp[r, NC - 1].wait_recv()
        block = xr[4 * g : 4 * g + 4, c].reshape(group, part)
        value = pre[at, :] + dot(block, win[pl.ds(pl.multiple_of(c * part, part), part), :])
        score = logit[at, :] + dot_nt(block, rt4[c])
        share = jax.nn.sigmoid(jnp.sum(jnp.where(mine, score, 0.0), axis=1, keepdims=True))
        gate[at, :] = share
        activated, slope = gelu_and_slope(value)
        pre[at, :] = slope
        act[at, :] = activated.astype(BF16)
        for q in range(NC):
            out = dot(act[at, :], wout[:, q * part : (q + 1) * part])
            result = (share * out).astype(BF16).reshape(4, depth, part)
            ys[4 * g : 4 * g + 4, q] = result
            for r in range(4 * g, 4 * g + 4):
                if r in HERE:
                    yr[r, q] = result[r - 4 * g]
        for r in range(4 * g, 4 * g + 4):
            if r in AWAY:
                b_cp[r] = send(ys.at[r], yr.at[r], b_ss.at[r], b_rs.at[r], origin(r))

    sum_cp = {}
    for r in AWAY:
        b_cp[r].wait_recv()
    run = rows // RUNS
    for i in range(RUNS):
        at = slice(i * run, (i + 1) * run)
        for q in range(NC):
            part_l[q, at] = dot(pl_t[at, :], stack(yr, FROM_LOW, q)).astype(BF16)
        sum_cp[0, i] = send(
            part_l.at[:, at, :], sum_h.at[:, at, :], sum_ss.at[0, i], sum_rs.at[0, i], low
        )
        for q in range(NC):
            part_h[q, at] = dot(ph_t[at, :], stack(yr, FROM_HIGH, q)).astype(BF16)
        sum_cp[1, i] = send(
            part_h.at[:, at, :], sum_l.at[:, at, :], sum_ss.at[1, i], sum_rs.at[1, i], high
        )
    for q in range(NC):
        acc[q] = mixed[q].astype(F32) + dot(po_t[...], stack(yr, OWN, q))
    got_cot.wait()
    got_gain.wait()
    ggp[...] = jnp.zeros_like(ggp)

    def norm_rows(j, carry):
        at = pl.ds(pl.multiple_of(j * TILE, TILE), TILE)
        cols = [slice(q * part, (q + 1) * part) for q in range(NC)]
        resid = [
            acc[q, at, :] + sum_h[q, at, :].astype(F32) + sum_l[q, at, :].astype(F32)
            for q in range(NC)
        ]
        mean = sum(jnp.sum(v, axis=1, keepdims=True) for v in resid) / width
        resid = [v - mean for v in resid]
        var = sum(jnp.sum(v * v, axis=1, keepdims=True) for v in resid) / width
        inv_std = lax.rsqrt(var + norm_eps)
        normed = [v * inv_std for v in resid]
        grads, m1, m2 = [], 0.0, 0.0
        for q in range(NC):
            gain = gain_ref[0:1, cols[q]]
            cot_f = cot[at, cols[q]].astype(F32)
            cot[at, cols[q]] = (normed[q] * gain).astype(BF16)
            ggp[0:1, cols[q]] += jnp.sum(cot_f * normed[q], axis=0, keepdims=True)
            grad = cot_f * gain
            grads.append(grad)
            m1 += jnp.sum(grad, axis=1, keepdims=True)
            m2 += jnp.sum(grad * normed[q], axis=1, keepdims=True)
        m1, m2 = m1 / width, m2 / width
        for q in range(NC):
            grad = inv_std * (grads[q] - m1 - normed[q] * m2)
            acc[q, at, :] = grad
            grd[q, at, :] = grad.astype(BF16)
        return carry

    raw2_cp, c_cp = {}, {}
    for i in range(RUNS):
        sum_cp[0, i].wait_recv()
        sum_cp[1, i].wait_recv()
        lax.fori_loop(i * run // TILE, (i + 1) * run // TILE, norm_rows, 0)
        src = grd.at[:, i * run : (i + 1) * run, :]
        to_high, to_low = (d.at[:, i * run : (i + 1) * run, :] for d in (raw_l, raw_h))
        raw2_cp[0, i] = send(src, to_high, raw2_ss.at[0, i], raw2_rs.at[0, i], high)
        raw2_cp[1, i] = send(src, to_low, raw2_ss.at[1, i], raw2_rs.at[1, i], low)

    def spread(vector, source, target, gathered, send_sems, recv_sems):
        source[...] = jnp.zeros_like(source)
        for j in range(width // 128):
            source[j : j + 1, :] = vector[0:1, j * 128 : (j + 1) * 128]
        target[...] = source[...].astype(BF16)
        gathered[co, z] = target[...]
        copies = {}
        for k in range(1, RING):
            copies[k] = send(
                target, gathered.at[co, z], send_sems.at[k], recv_sems.at[k],
                ((z + k) % RING) * 2 + co,
            )
        return copies

    def exchange(copies, gathered, send_sems, recv_sems):
        for k in range(1, RING):
            copies[k].wait_recv()
        copies[0] = send(
            gathered.at[co], gathered.at[co], send_sems.at[0], recv_sems.at[0],
            z * 2 + (co + 1) % 2,
        )

    gn_cp = spread(ggp, small, gain_s, gain_r, gn_ss, gn_rs)
    put_norm = pltpu.make_async_copy(cot, no_h, out_sem.at[0])
    put_norm.start()
    for copies in (mix_cp, raw_cp):
        for k in copies:
            copies[k].wait_send()
    for k in a_cp:
        a_cp[k].wait_send()
    for k in sum_cp:
        sum_cp[k].wait_send()
    for q in range(NC):
        expand(po_m, grd[q], OWN, q, xs, gr)
    def send_gradient(r):
        c_cp[r] = send(xs.at[r], gr.at[r], c_ss.at[r], c_rs.at[r], target(r))

    send_gradient(1)
    for first, last in ((0, 4), (4, 7)):
        for n, (matrix, values, members) in enumerate(
            ((pl_m, raw_l, FROM_LOW), (ph_m, raw_h, FROM_HIGH))
        ):
            if first == 0:
                for i in range(RUNS):
                    raw2_cp[n, i].wait_recv()
            for q in range(NC):
                expand(matrix, values[q], members[first:last], q, xs, gr, first)
            for r in members[first:last]:
                if r in AWAY:
                    send_gradient(r)

    rcol[...] = jnp.zeros_like(rcol)
    mine_row = lax.broadcasted_iota(jnp.int32, (N, part), 0) == dp
    d_cp = {}

    def send_back(r, i):
        c = (xm + 1 + i) % 4
        d_cp[r, i] = send(ds.at[r, c], yr.at[r, c], d_ss.at[r, i], d_rs.at[r, i], origin(r))

    for g in range(NG):
        at = slice(g * group, (g + 1) * group)
        for r in range(4 * g, 4 * g + 4):
            if r in AWAY:
                c_cp[r].wait_recv()
        share = gate[at, :]
        grad_act, grad_gate = 0.0, 0.0
        for q in range(NC):
            grad = gr[4 * g : 4 * g + 4, q].reshape(group, part).astype(F32)
            result = ys[4 * g : 4 * g + 4, q].reshape(group, part).astype(F32)
            grad_gate += jnp.sum(grad * result, axis=1, keepdims=True)
            grad_out = (share * grad).astype(BF16)
            gr[4 * g : 4 * g + 4, q] = grad_out.reshape(4, depth, part)
            grad_act += dot_nt(grad_out, wout[:, q * part : (q + 1) * part])
        grad_logit = grad_gate * (1.0 - share)
        glog[at, :] = grad_logit
        gp[at, :] = (grad_act * pre[at, :]).astype(BF16)
        for i in range(NC):
            c = (xm + 1 + i) % 4
            weights = jnp.sum(jnp.where(mine_row, rt4[c].astype(F32), 0.0), axis=0, keepdims=True)
            back = dot_nt(gp[at, :], win[pl.ds(pl.multiple_of(c * part, part), part), :])
            back = (back + grad_logit * weights).astype(BF16).reshape(4, depth, part)
            ds[4 * g : 4 * g + 4, c] = back
            for r in range(4 * g, 4 * g + 4):
                if r in HERE:
                    yr[r, c] = back[r - 4 * g]
                else:
                    send_back(r, i)

    for g in range(NG):
        at = slice(g * group, (g + 1) * group)
        for q in range(NC):
            block = xr[4 * g : 4 * g + 4, q].reshape(group, part).astype(F32)
            rcol[0:1, q * part : (q + 1) * part] += jnp.sum(
                glog[at, :] * block, axis=0, keepdims=True
            )
    cl_cp = spread(rcol, small, col_s, col_r, cl_ss, cl_rs)
    for q in range(NC):
        cols = slice(q * part, (q + 1) * part)
        gwi[cols, :] = dot_tn(xr[:, q].reshape(slots, part), gp[...]).astype(BF16)
    put_gwi = pltpu.make_async_copy(gwi, gwi_h, out_sem.at[1])
    put_gwi.start()

    def out_gradient(q):
        gwo[:, q * part : (q + 1) * part] = dot_tn(act[...], gr[:, q].reshape(slots, part)).astype(BF16)

    sum2_cp, e_cp = {}, {}

    def sum_back(i):
        c = (xm + 1 + i) % 4
        for r in AWAY:
            d_cp[r, i].wait_recv()
        part_l[c] = dot(pl_t[...], stack(yr, FROM_LOW, c)).astype(BF16)
        sum2_cp[0, i] = send(part_l.at[c], sum_h.at[c], sum2_ss.at[0, i], sum2_rs.at[0, i], low)
        part_h[c] = dot(ph_t[...], stack(yr, FROM_HIGH, c)).astype(BF16)
        sum2_cp[1, i] = send(part_h.at[c], sum_l.at[c], sum2_ss.at[1, i], sum2_rs.at[1, i], high)
        acc[c] += dot(po_t[...], stack(yr, OWN, c))

    def finish_chunk(i):
        c = (xm + 1 + i) % 4
        sum2_cp[0, i].wait_recv()
        sum2_cp[1, i].wait_recv()
        total = acc[c] + sum_h[c].astype(F32) + sum_l[c].astype(F32)
        tok_t[pl.ds(c * tokens4, tokens4)] = total.astype(BF16).T.reshape(tokens4, head, rows)
        for yy in range(4):
            to = c * tokens4 + (ym + yy) % 4
            if i == NC - 1 and yy == 0:
                gt_t[ex] = tok_t[ex]
                continue
            k = i * 4 + yy
            e_cp[k] = pltpu.make_async_remote_copy(
                src_ref=tok_t.at[to], dst_ref=gt_t.at[ex],
                send_sem=e_ss.at[k], recv_sem=e_rs.at[k],
                device_id=(dp, to), device_id_type=MESH,
            )
            e_cp[k].start()

    sum_back(0)
    out_gradient(0)
    out_gradient(1)
    sum_back(1)
    finish_chunk(0)
    out_gradient(2)
    out_gradient(3)
    put_gwo = pltpu.make_async_copy(gwo, gwo_h, out_sem.at[2])
    put_gwo.start()
    exchange(gn_cp, gain_r, gn_ss, gn_rs)
    exchange(cl_cp, col_r, cl_ss, cl_rs)
    sum_back(2)
    finish_chunk(1)

    sum_back(3)

    gn_cp[0].wait_recv()
    cl_cp[0].wait_recv()
    total = 0.0
    for e in range(N):
        total += gain_r[e % 2, e // 2].astype(F32)
    small[...] = total
    for j in range(width // 128):
        gg_ref[0:1, j * 128 : (j + 1) * 128] = small[j : j + 1, :]
    for e in range(N):
        small[...] = col_r[e % 2, e // 2].astype(F32)
        for j in range(width // 128):
            gr_ref[e : e + 1, j * 128 : (j + 1) * 128] = small[j : j + 1, :]

    finish_chunk(2)
    finish_chunk(3)

    for i in range(NC):
        c = (xm + NC - 1 - i) % 4
        for yy in range(4):
            if i < NC - 1 or yy:
                e_cp[i * 4 + yy].wait_recv()
        turned = gt_t[pl.ds(c * tokens4, tokens4)].reshape(part, rows).T
        tok[:, pl.ds(pl.multiple_of(c * part, part), part)] = turned
    put_gt = pltpu.make_async_copy(tok, gt_h, out_sem.at[3])
    put_gt.start()
    for copies in (
        ids_cp, side_cp, b_cp, raw2_cp, c_cp, d_cp, sum2_cp, e_cp, gn_cp, cl_cp,
    ):
        for k in copies:
            copies[k].wait_send()
    put_norm.wait()
    put_gwi.wait()
    put_gwo.wait()
    put_gt.wait()


def store_kernel(pieces, *refs):
    count = len(pieces)
    sems = refs[2 * count]
    copies = []
    for k, cut in enumerate(pieces):
        size = refs[k].shape[0] // cut
        for i in range(cut):
            at = slice(i * size, (i + 1) * size)
            copies.append(
                pltpu.make_async_copy(refs[k].at[at, :], refs[count + k].at[at, :], sems.at[len(copies)])
            )
    for copy in copies:
        copy.start()
    for copy in copies:
        copy.wait()


def body(tokens, route_ids, router, norm_gain, w_in, w_out, cotangent):
    rows, width = tokens.shape[0], tokens.shape[2]
    hidden = w_in.shape[3]
    depth = 3 * rows // N
    slots = N * depth
    part = width // NC
    head = width // N
    group = 4 * depth
    shape = jax.ShapeDtypeStruct
    vmem = pl.BlockSpec(memory_space=pltpu.VMEM)
    anywhere = pl.BlockSpec(memory_space=pl.ANY)
    hbm = pl.BlockSpec(memory_space=pltpu.HBM)
    dma = pltpu.SemaphoreType.DMA
    keep = functools.partial(pltpu.with_memory_space_constraint, memory_space=pltpu.HBM)
    blocks = pltpu.VMEM((N, NC, depth, part), BF16)
    flipped = pltpu.VMEM((N, head, rows), BF16)
    row_block = pltpu.VMEM((rows, width), BF16)
    chunks = pltpu.VMEM((NC, rows, part), BF16)
    ids = pltpu.VMEM((8, rows), jnp.int32)
    out = pl.pallas_call(
        kernel,
        out_shape=(
            shape((rows, width), BF16),
            shape((rows, width), BF16),
            shape((N, width), F32),
            shape((1, width), F32),
            shape((width, hidden), BF16),
            shape((hidden, width), BF16),
        ),
        in_specs=[hbm] * 7,
        out_specs=[anywhere, anywhere, vmem, vmem, anywhere, anywhere],
        scratch_shapes=[
            row_block,
            pltpu.VMEM((2, rows), jnp.int32),
            pltpu.VMEM((N, width), BF16),
            pltpu.VMEM((1, width), F32),
            flipped,
            flipped,
            chunks,
            row_block,
            pltpu.VMEM((width, hidden), BF16),
            pltpu.VMEM((hidden, width), BF16),
            pltpu.VMEM((NC, N, part), BF16),
            ids, ids, ids,
            pltpu.VMEM((7 * depth, rows), BF16),
            pltpu.VMEM((7 * depth, rows), BF16),
            pltpu.VMEM((2 * depth, rows), BF16),
            pltpu.VMEM((rows, 7 * depth), BF16),
            pltpu.VMEM((rows, 7 * depth), BF16),
            pltpu.VMEM((rows, 2 * depth), BF16),
            flipped, flipped, flipped, flipped,
            chunks, chunks,
            blocks,
            blocks,
            pltpu.VMEM((slots, hidden), F32),
            pltpu.VMEM((slots, N), F32),
            pltpu.VMEM((slots, 1), F32),
            pltpu.VMEM((slots, hidden), BF16),
            blocks,
            blocks,
            chunks, chunks, chunks, chunks,
            pltpu.VMEM((NC, rows, part), F32),
            chunks,
            blocks,
            pltpu.VMEM((slots, hidden), BF16),
            blocks,
            pltpu.VMEM((slots, 1), F32),
            pltpu.VMEM((width, hidden), BF16),
            pltpu.VMEM((hidden, width), BF16),
            flipped,
            pltpu.VMEM((8, width), F32),
            pltpu.VMEM((8, width), F32),
            pltpu.VMEM((16, 128), F32),
            pltpu.VMEM((16, 128), BF16),
            pltpu.VMEM((2, RING, 16, 128), BF16),
            pltpu.VMEM((16, 128), BF16),
            pltpu.VMEM((2, RING, 16, 128), BF16),
            dma((7,)),
            dma((2,)), dma((2,)),
            dma((N,)), dma((N,)),
            dma((2, NC)), dma((2, NC)),
            dma((2, N)), dma((2, N)),
            dma((N, NC)), dma((N, NC)),
            dma((N,)), dma((N,)),
            dma((2, RUNS)), dma((2, RUNS)),
            dma((2, RUNS)), dma((2, RUNS)),
            dma((N,)), dma((N,)),
            dma((N, NC)), dma((N, NC)),
            dma((2, NC)), dma((2, NC)),
            dma((N,)), dma((N,)),
            dma((N,)), dma((N,)),
            dma((N,)), dma((N,)),
            dma((4,)),
        ],
        name="rank_mixer",
        compiler_params=pltpu.CompilerParams(
            collective_id=0, has_side_effects=True, vmem_limit_bytes=46 << 20
        ),
    )(
        keep(tokens.reshape(rows, width)),
        keep(route_ids.reshape(rows, 2).T),
        keep(router.reshape(width, N).T),
        keep(norm_gain.reshape(1, width)),
        keep(w_in.reshape(width, hidden)),
        keep(w_out.reshape(hidden, width)),
        keep(cotangent.reshape(rows, width)),
    )
    pieces = (2, 2, 1, 1, 4, 4)
    out = pl.pallas_call(
        functools.partial(store_kernel, pieces),
        out_shape=tuple(shape(v.shape, v.dtype) for v in out),
        in_specs=[anywhere] * 6,
        out_specs=[hbm] * 6,
        scratch_shapes=[dma((sum(pieces),))],
        name="store",
        compiler_params=pltpu.CompilerParams(vmem_limit_bytes=1 << 20),
    )(*out)
    normed_out, grad_tokens, grad_router, grad_gain, grad_w_in, grad_w_out = out
    return (
        normed_out.reshape(rows, 1, width),
        grad_tokens.reshape(rows, 1, width),
        grad_router.T.reshape(1, width, N),
        grad_gain,
        grad_w_in.reshape(1, 1, width, hidden),
        grad_w_out.reshape(1, 1, hidden, width),
    )


def solution(mesh):
    return jax.shard_map(
        body,
        mesh=mesh,
        in_specs=(
            P("dp", "expert", None),
            P("expert", "dp", None),
            P("expert", None, None),
            P("expert", None),
            P("expert", "dp", None, None),
            P("expert", "dp", None, None),
            P("dp", "expert", None),
        ),
        out_specs=(
            P("dp", "expert", None),
            P("dp", "expert", None),
            P("expert", None, None),
            P("expert", None),
            P("expert", "dp", None, None),
            P("expert", "dp", None, None),
        ),
        check_vma=False,
    )
```

```python
import functools

import jax
import jax.numpy as jnp
from jax import lax
from jax.experimental import pallas as pl
from jax.experimental.pallas import tpu as pltpu
from jax.sharding import PartitionSpec as P

MESH = pl.DeviceIdType.MESH
F32 = jnp.float32
BF16 = jnp.bfloat16

gelu_coef = 0.7978845608028654
cubic_coef = 0.044715
norm_eps = 1e-05

N = 16
NC = 4
NG = 4
RING = 8
STEPS = (0, 1, -1, 2, -2, 3, -3, 4)
HOPS = (0, 0, 0, 0, 0, 0, -1, -1, 1, 1, -2, -2, 2, 2, 3, -3)
FROM_LOW = (4, 5, 8, 9, 12, 13, 14)
FROM_HIGH = (2, 3, 6, 7, 10, 11, 15)
OWN = (0, 1)
HERE = (0, 2, 4)
AWAY = tuple(r for r in range(N) if r not in HERE)
TILE = 32
RUNS = 4


def dot(a, b):
    return lax.dot_general(a, b, (((1,), (0,)), ((), ())), preferred_element_type=F32)


def dot_nt(a, b):
    return lax.dot_general(a, b, (((1,), (1,)), ((), ())), preferred_element_type=F32)


def dot_tn(a, b):
    return lax.dot_general(a, b, (((0,), (0,)), ((), ())), preferred_element_type=F32)


def gelu_and_slope(value):
    inner = gelu_coef * (value + cubic_coef * value * value * value)
    tangent = jnp.tanh(inner)
    half = 0.5 * (1.0 + tangent)
    slope = half + 0.5 * value * (1.0 - tangent * tangent) * gelu_coef * (
        1.0 + 3.0 * cubic_coef * value * value
    )
    return value * half, slope


def kernel(
    tok_h, ids_h, rt_h, gain_h, win_h, wout_h, cot_h,
    no_h, gt_h, gr_ref, gg_ref, gwi_h, gwo_h,
    tok, ids_ref, rt_ref, gain_ref, tok_t, mix_t, mixed, cot, win, wout, rt4,
    ids_own, ids_low, ids_high, pl_m, ph_m, po_m, pl_t, ph_t, po_t,
    raw_lt, raw_ht, mix_lt, mix_ht, raw_l, raw_h, xs, xr, pre, logit, gate, act, ys, yr,
    part_l, part_h, sum_h, sum_l, acc, grd, gr, gp, ds, glog,
    gwi, gwo, gt_t, ggp, rcol, small,
    gain_s, gain_r, col_s, col_r,
    load_sem, ids_ss, ids_rs, mix_ss, mix_rs, raw_ss, raw_rs, side_ss, side_rs, a_ss, a_rs, b_ss, b_rs,
    sum_ss, sum_rs, raw2_ss, raw2_rs, c_ss, c_rs, d_ss, d_rs, sum2_ss, sum2_rs,
    e_ss, e_rs, gn_ss, gn_rs, cl_ss, cl_rs, out_sem, put_sem,
):
    rows, width = tok.shape
    head = width // N
    part = width // NC
    hidden = win.shape[1]
    depth = xs.shape[2]
    group = depth * 4
    slots = N * depth
    tokens4 = N // NC
    dp = lax.axis_index("dp")
    ex = lax.axis_index("expert")
    z, co = dp // 2, dp % 2
    xm, ym = ex // 4, ex % 4

    def partner(r):
        return ((z + STEPS[r // 2] + RING) % RING) * 2 + (co + r % 2) % 2

    def target(r):
        return ((z + HOPS[r] + RING) % RING) * 2 + (co + r % 2) % 2

    def origin(r):
        return ((z - HOPS[r] + RING) % RING) * 2 + (co + r % 2) % 2

    high = ((z + 1) % RING) * 2 + co
    low = ((z + RING - 1) % RING) * 2 + co

    def send(src, dst, send_sem, recv_sem, to):
        copy = pltpu.make_async_remote_copy(
            src_ref=src, dst_ref=dst, send_sem=send_sem, recv_sem=recv_sem,
            device_id=(to, ex), device_id_type=MESH,
        )
        copy.start()
        return copy

    def load(src, dst, k):
        copy = pltpu.make_async_copy(src, dst, load_sem.at[k])
        copy.start()
        return copy

    got_tok = load(tok_h, tok, 0)
    got_ids = load(ids_h, ids_ref, 1)

    barrier = pltpu.get_barrier_semaphore()
    for r in range(1, N):
        pl.semaphore_signal(barrier, inc=1, device_id=(partner(r), ex), device_id_type=MESH)
    for k in range(1, N):
        pl.semaphore_signal(barrier, inc=1, device_id=(dp, (ex + k) % N), device_id_type=MESH)
    got_tok.wait()
    got_ids.wait()
    got_win = load(win_h, win, 4)
    got_wout = load(wout_h, wout, 5)
    got_rt = load(rt_h, rt_ref, 2)
    got_gain = load(gain_h, gain_ref, 3)
    got_cot = load(cot_h, cot, 6)
    ids_own[...] = jnp.zeros_like(ids_own)
    ids_own[0:2, :] = ids_ref[...]

    ids_cp, raw_cp, mix_cp = {}, {}, {}
    for i in range(NC):
        c = (xm - i + 4) % 4
        turned = tok[:, pl.ds(pl.multiple_of(c * part, part), part)].T
        tok_t[pl.ds(c * tokens4, tokens4)] = turned.reshape(tokens4, head, rows)
        if i == 0:
            mix_t[ex] = tok_t[ex]
            pl.semaphore_wait(barrier, 2 * (N - 1))
        heads = pl.ds(c * tokens4, tokens4)
        raw_cp[0, i] = send(
            tok_t.at[heads], raw_lt.at[heads], raw_ss.at[0, i], raw_rs.at[0, i], high
        )
        raw_cp[1, i] = send(
            tok_t.at[heads], raw_ht.at[heads], raw_ss.at[1, i], raw_rs.at[1, i], low
        )
        for yy in range(4):
            k = i * 4 + yy
            to = c * 4 + (ym + yy) % 4
            if k == 0:
                continue
            mix_cp[k] = pltpu.make_async_remote_copy(
                src_ref=tok_t.at[to], dst_ref=mix_t.at[ex],
                send_sem=mix_ss.at[k], recv_sem=mix_rs.at[k],
                device_id=(dp, to), device_id_type=MESH,
            )
            mix_cp[k].start()
        if i == 0:
            ids_cp[0] = send(ids_own, ids_low, ids_ss.at[0], ids_rs.at[0], high)
            ids_cp[1] = send(ids_own, ids_high, ids_ss.at[1], ids_rs.at[1], low)

    label = lax.broadcasted_iota(jnp.int32, (N, rows), 0)
    earlier = (
        lax.broadcasted_iota(jnp.int32, (rows, rows), 0)
        < lax.broadcasted_iota(jnp.int32, (rows, rows), 1)
    ).astype(F32)
    earlier = earlier.astype(BF16)
    slot = lax.broadcasted_iota(jnp.int32, (depth, rows), 0)

    def place(ids, members, matrix, flipped):
        ids0, ids1 = ids[0:1, :], ids[1:2, :]
        hot0 = (label == ids0).astype(F32)
        hot1 = (label == ids1).astype(F32)
        before = dot((hot0 + hot1).astype(BF16), earlier)
        at0 = jnp.sum(before * hot0, axis=0, keepdims=True).astype(jnp.int32)
        at1 = jnp.sum(before * hot1, axis=0, keepdims=True).astype(jnp.int32)
        blocks = []
        for r in members:
            e = target(r)
            goal0 = jnp.where(ids0 == e, at0, -1)
            goal1 = jnp.where(ids1 == e, at1, -1)
            blocks.append(jnp.logical_or(slot == goal0, slot == goal1).astype(F32))
        placed = jnp.concatenate(blocks, axis=0)
        matrix[...] = placed.astype(BF16)
        flipped[...] = placed.T.astype(BF16)

    def stack(blocks, members, q):
        return jnp.concatenate([blocks[r, q] for r in members], axis=0)

    def expand(matrix, values, members, q, out, arrived, first=0):
        at = slice(first * depth, (first + len(members)) * depth)
        sent = dot(matrix[at, :], values).astype(BF16)
        for n, r in enumerate(members):
            into = arrived if r in HERE else out
            into[r, q] = sent[n * depth : (n + 1) * depth]

    a_cp, side_cp = {}, {}
    sides = ((raw_lt, mix_lt, raw_l), (raw_ht, mix_ht, raw_h))

    def send_mixed(r, i):
        c = (xm + i) % 4
        a_cp[r, i] = send(xs.at[r, c], xr.at[r, c], a_ss.at[r, i], a_rs.at[r, i], target(r))

    def relay(i):
        c = (xm - i + 4) % 4
        for n, (whole, gathered, _) in enumerate(sides):
            raw_cp[n, i].wait_recv()
            for yy in range(4):
                k = i * 4 + yy
                to = c * 4 + (ym + yy) % 4
                if k == 0:
                    gathered[ex] = whole[ex]
                    continue
                side_cp[n, k] = pltpu.make_async_remote_copy(
                    src_ref=whole.at[to], dst_ref=gathered.at[ex],
                    send_sem=side_ss.at[n, k], recv_sem=side_rs.at[n, k],
                    device_id=(dp, to), device_id_type=MESH,
                )
                side_cp[n, k].start()

    def own_chunk(i):
        c = (xm + i) % 4
        for yy in range(4):
            if i * 4 + yy:
                mix_cp[i * 4 + yy].wait_recv()
        mixed[c] = mix_t[pl.ds(c * tokens4, tokens4)].reshape(part, rows).T
        expand(po_m, mixed[c], OWN, c, xs, xr)
        send_mixed(1, i)

    def pass_on(i):
        c = (xm + i) % 4
        for n, (_, gathered, plain) in enumerate(sides):
            for yy in range(4):
                if i * 4 + yy:
                    side_cp[n, i * 4 + yy].wait_recv()
            plain[c] = gathered[pl.ds(c * tokens4, tokens4)].reshape(part, rows).T
            if n == 0:
                expand(pl_m, plain[c], FROM_LOW, c, xs, xr)
            else:
                expand(ph_m, plain[c], FROM_HIGH, c, xs, xr)
        for r in AWAY[1:]:
            send_mixed(r, i)

    place(ids_own, OWN, po_m, po_t)
    ids_cp[0].wait_recv()
    ids_cp[1].wait_recv()
    place(ids_low, FROM_LOW, pl_m, pl_t)
    place(ids_high, FROM_HIGH, ph_m, ph_t)
    relay(0)
    for i in range(NC):
        own_chunk(i)
        if i + 1 < NC:
            relay(i + 1)
        pass_on(i)

    got_rt.wait()
    got_win.wait()
    got_wout.wait()
    for c in range(NC):
        rt4[c] = rt_ref[:, c * part : (c + 1) * part]
    mine = lax.broadcasted_iota(jnp.int32, (group, N), 1) == dp
    for i in range(NC - 1):
        c = (xm + i) % 4
        for r in AWAY:
            a_cp[r, i].wait_recv()
        for g in range(NG):
            at = slice(g * group, (g + 1) * group)
            block = xr[4 * g : 4 * g + 4, c].reshape(group, part)
            more = dot(block, win[pl.ds(pl.multiple_of(c * part, part), part), :])
            more_logit = dot_nt(block, rt4[c])
            if i == 0:
                pre[at, :] = more
                logit[at, :] = more_logit
            else:
                pre[at, :] += more
                logit[at, :] += more_logit
    b_cp = {}
    c = (xm + NC - 1) % 4
    for g in range(NG):
        at = slice(g * group, (g + 1) * group)
        for r in range(4 * g, 4 * g + 4):
            if r in AWAY:
                a_cp[r, NC - 1].wait_recv()
        block = xr[4 * g : 4 * g + 4, c].reshape(group, part)
        value = pre[at, :] + dot(block, win[pl.ds(pl.multiple_of(c * part, part), part), :])
        score = logit[at, :] + dot_nt(block, rt4[c])
        share = jax.nn.sigmoid(jnp.sum(jnp.where(mine, score, 0.0), axis=1, keepdims=True))
        gate[at, :] = share
        activated, slope = gelu_and_slope(value)
        pre[at, :] = slope
        act[at, :] = activated.astype(BF16)
        for q in range(NC):
            out = dot(act[at, :], wout[:, q * part : (q + 1) * part])
            result = (share * out).astype(BF16).reshape(4, depth, part)
            ys[4 * g : 4 * g + 4, q] = result
            for r in range(4 * g, 4 * g + 4):
                if r in HERE:
                    yr[r, q] = result[r - 4 * g]
        for r in range(4 * g, 4 * g + 4):
            if r in AWAY:
                b_cp[r] = send(ys.at[r], yr.at[r], b_ss.at[r], b_rs.at[r], origin(r))

    sum_cp = {}
    for r in AWAY:
        b_cp[r].wait_recv()
    run = rows // RUNS
    for i in range(RUNS):
        at = slice(i * run, (i + 1) * run)
        for q in range(NC):
            part_l[q, at] = dot(pl_t[at, :], stack(yr, FROM_LOW, q)).astype(BF16)
        sum_cp[0, i] = send(
            part_l.at[:, at, :], sum_h.at[:, at, :], sum_ss.at[0, i], sum_rs.at[0, i], low
        )
        for q in range(NC):
            part_h[q, at] = dot(ph_t[at, :], stack(yr, FROM_HIGH, q)).astype(BF16)
        sum_cp[1, i] = send(
            part_h.at[:, at, :], sum_l.at[:, at, :], sum_ss.at[1, i], sum_rs.at[1, i], high
        )
    for q in range(NC):
        acc[q] = mixed[q].astype(F32) + dot(po_t[...], stack(yr, OWN, q))
    got_cot.wait()
    got_gain.wait()
    ggp[...] = jnp.zeros_like(ggp)

    def norm_rows(j, carry):
        at = pl.ds(pl.multiple_of(j * TILE, TILE), TILE)
        cols = [slice(q * part, (q + 1) * part) for q in range(NC)]
        resid = [
            acc[q, at, :] + sum_h[q, at, :].astype(F32) + sum_l[q, at, :].astype(F32)
            for q in range(NC)
        ]
        mean = sum(jnp.sum(v, axis=1, keepdims=True) for v in resid) / width
        resid = [v - mean for v in resid]
        var = sum(jnp.sum(v * v, axis=1, keepdims=True) for v in resid) / width
        inv_std = lax.rsqrt(var + norm_eps)
        normed = [v * inv_std for v in resid]
        grads, m1, m2 = [], 0.0, 0.0
        for q in range(NC):
            gain = gain_ref[0:1, cols[q]]
            cot_f = cot[at, cols[q]].astype(F32)
            cot[at, cols[q]] = (normed[q] * gain).astype(BF16)
            ggp[0:1, cols[q]] += jnp.sum(cot_f * normed[q], axis=0, keepdims=True)
            grad = cot_f * gain
            grads.append(grad)
            m1 += jnp.sum(grad, axis=1, keepdims=True)
            m2 += jnp.sum(grad * normed[q], axis=1, keepdims=True)
        m1, m2 = m1 / width, m2 / width
        for q in range(NC):
            grad = inv_std * (grads[q] - m1 - normed[q] * m2)
            acc[q, at, :] = grad
            grd[q, at, :] = grad.astype(BF16)
        return carry

    raw2_cp, c_cp = {}, {}
    for i in range(RUNS):
        sum_cp[0, i].wait_recv()
        sum_cp[1, i].wait_recv()
        lax.fori_loop(i * run // TILE, (i + 1) * run // TILE, norm_rows, 0)
        src = grd.at[:, i * run : (i + 1) * run, :]
        to_high, to_low = (d.at[:, i * run : (i + 1) * run, :] for d in (raw_l, raw_h))
        raw2_cp[0, i] = send(src, to_high, raw2_ss.at[0, i], raw2_rs.at[0, i], high)
        raw2_cp[1, i] = send(src, to_low, raw2_ss.at[1, i], raw2_rs.at[1, i], low)

    def spread(vector, source, target, gathered, send_sems, recv_sems):
        source[...] = jnp.zeros_like(source)
        for j in range(width // 128):
            source[j : j + 1, :] = vector[0:1, j * 128 : (j + 1) * 128]
        target[...] = source[...].astype(BF16)
        gathered[co, z] = target[...]
        copies = {}
        for k in range(1, RING):
            copies[k] = send(
                target, gathered.at[co, z], send_sems.at[k], recv_sems.at[k],
                ((z + k) % RING) * 2 + co,
            )
        return copies

    def exchange(copies, gathered, send_sems, recv_sems):
        for k in range(1, RING):
            copies[k].wait_recv()
        copies[0] = send(
            gathered.at[co], gathered.at[co], send_sems.at[0], recv_sems.at[0],
            z * 2 + (co + 1) % 2,
        )

    gn_cp = spread(ggp, small, gain_s, gain_r, gn_ss, gn_rs)
    put_norm = pltpu.make_async_copy(cot, no_h, out_sem.at[0])
    put_norm.start()
    for copies in (mix_cp, raw_cp):
        for k in copies:
            copies[k].wait_send()
    for k in a_cp:
        a_cp[k].wait_send()
    for k in sum_cp:
        sum_cp[k].wait_send()
    for q in range(NC):
        expand(po_m, grd[q], OWN, q, xs, gr)
    def send_gradient(r):
        c_cp[r] = send(xs.at[r], gr.at[r], c_ss.at[r], c_rs.at[r], target(r))

    send_gradient(1)
    for first, last in ((0, 4), (4, 7)):
        for n, (matrix, values, members) in enumerate(
            ((pl_m, raw_l, FROM_LOW), (ph_m, raw_h, FROM_HIGH))
        ):
            if first == 0:
                for i in range(RUNS):
                    raw2_cp[n, i].wait_recv()
            for q in range(NC):
                expand(matrix, values[q], members[first:last], q, xs, gr, first)
            for r in members[first:last]:
                if r in AWAY:
                    send_gradient(r)

    rcol[...] = jnp.zeros_like(rcol)
    mine_row = lax.broadcasted_iota(jnp.int32, (N, part), 0) == dp
    d_cp = {}

    def send_back(r, i):
        c = (xm + 1 + i) % 4
        d_cp[r, i] = send(ds.at[r, c], yr.at[r, c], d_ss.at[r, i], d_rs.at[r, i], origin(r))

    for g in range(NG):
        at = slice(g * group, (g + 1) * group)
        for r in range(4 * g, 4 * g + 4):
            if r in AWAY:
                c_cp[r].wait_recv()
        share = gate[at, :]
        grad_act, grad_gate = 0.0, 0.0
        for q in range(NC):
            grad = gr[4 * g : 4 * g + 4, q].reshape(group, part).astype(F32)
            result = ys[4 * g : 4 * g + 4, q].reshape(group, part).astype(F32)
            grad_gate += jnp.sum(grad * result, axis=1, keepdims=True)
            grad_out = (share * grad).astype(BF16)
            gr[4 * g : 4 * g + 4, q] = grad_out.reshape(4, depth, part)
            grad_act += dot_nt(grad_out, wout[:, q * part : (q + 1) * part])
        grad_logit = grad_gate * (1.0 - share)
        glog[at, :] = grad_logit
        gp[at, :] = (grad_act * pre[at, :]).astype(BF16)
        for i in range(NC):
            c = (xm + 1 + i) % 4
            weights = jnp.sum(jnp.where(mine_row, rt4[c].astype(F32), 0.0), axis=0, keepdims=True)
            back = dot_nt(gp[at, :], win[pl.ds(pl.multiple_of(c * part, part), part), :])
            back = (back + grad_logit * weights).astype(BF16).reshape(4, depth, part)
            ds[4 * g : 4 * g + 4, c] = back
            for r in range(4 * g, 4 * g + 4):
                if r in HERE:
                    yr[r, c] = back[r - 4 * g]
                else:
                    send_back(r, i)

    for g in range(NG):
        at = slice(g * group, (g + 1) * group)
        for q in range(NC):
            block = xr[4 * g : 4 * g + 4, q].reshape(group, part).astype(F32)
            rcol[0:1, q * part : (q + 1) * part] += jnp.sum(
                glog[at, :] * block, axis=0, keepdims=True
            )
    cl_cp = spread(rcol, small, col_s, col_r, cl_ss, cl_rs)
    for q in range(NC):
        cols = slice(q * part, (q + 1) * part)
        gwi[cols, :] = dot_tn(xr[:, q].reshape(slots, part), gp[...]).astype(BF16)
    put_gwi = pltpu.make_async_copy(gwi, gwi_h, out_sem.at[1])
    put_gwi.start()

    def out_gradient(q):
        gwo[:, q * part : (q + 1) * part] = dot_tn(act[...], gr[:, q].reshape(slots, part)).astype(BF16)

    sum2_cp, e_cp = {}, {}

    def sum_back(i):
        c = (xm + 1 + i) % 4
        for r in AWAY:
            d_cp[r, i].wait_recv()
        part_l[c] = dot(pl_t[...], stack(yr, FROM_LOW, c)).astype(BF16)
        sum2_cp[0, i] = send(part_l.at[c], sum_h.at[c], sum2_ss.at[0, i], sum2_rs.at[0, i], low)
        part_h[c] = dot(ph_t[...], stack(yr, FROM_HIGH, c)).astype(BF16)
        sum2_cp[1, i] = send(part_h.at[c], sum_l.at[c], sum2_ss.at[1, i], sum2_rs.at[1, i], high)
        acc[c] += dot(po_t[...], stack(yr, OWN, c))

    def finish_chunk(i):
        c = (xm + 1 + i) % 4
        sum2_cp[0, i].wait_recv()
        sum2_cp[1, i].wait_recv()
        total = acc[c] + sum_h[c].astype(F32) + sum_l[c].astype(F32)
        tok_t[pl.ds(c * tokens4, tokens4)] = total.astype(BF16).T.reshape(tokens4, head, rows)
        for yy in range(4):
            to = c * tokens4 + (ym + yy) % 4
            if i == NC - 1 and yy == 0:
                gt_t[ex] = tok_t[ex]
                continue
            k = i * 4 + yy
            e_cp[k] = pltpu.make_async_remote_copy(
                src_ref=tok_t.at[to], dst_ref=gt_t.at[ex],
                send_sem=e_ss.at[k], recv_sem=e_rs.at[k],
                device_id=(dp, to), device_id_type=MESH,
            )
            e_cp[k].start()

    sum_back(0)
    out_gradient(0)
    out_gradient(1)
    sum_back(1)
    finish_chunk(0)
    out_gradient(2)
    out_gradient(3)
    put_gwo = pltpu.make_async_copy(gwo, gwo_h, out_sem.at[2])
    put_gwo.start()
    for copies in (ids_cp, side_cp, b_cp, raw2_cp, c_cp):
        for k in copies:
            copies[k].wait_send()
    exchange(gn_cp, gain_r, gn_ss, gn_rs)
    exchange(cl_cp, col_r, cl_ss, cl_rs)
    sum_back(2)
    finish_chunk(1)

    sum_back(3)

    gn_cp[0].wait_recv()
    cl_cp[0].wait_recv()
    total = 0.0
    for e in range(N):
        total += gain_r[e % 2, e // 2].astype(F32)
    small[...] = total
    for j in range(width // 128):
        gg_ref[0:1, j * 128 : (j + 1) * 128] = small[j : j + 1, :]
    for e in range(N):
        small[...] = col_r[e % 2, e // 2].astype(F32)
        for j in range(width // 128):
            gr_ref[e : e + 1, j * 128 : (j + 1) * 128] = small[j : j + 1, :]

    finish_chunk(2)
    for copies in (d_cp, gn_cp, cl_cp):
        for k in copies:
            copies[k].wait_send()
    put_gt = []

    def place_tokens(i):
        c = (xm + NC - 1 - i) % 4
        for yy in range(4):
            if i < NC - 1 or yy:
                e_cp[i * 4 + yy].wait_recv()
        cols = pl.ds(pl.multiple_of(c * part, part), part)
        tok[:, cols] = gt_t[pl.ds(c * tokens4, tokens4)].reshape(part, rows).T
        put_gt.append(
            pltpu.make_async_copy(tok.at[:, cols], gt_h.at[:, cols], put_sem.at[i])
        )
        put_gt[i].start()

    place_tokens(0)
    place_tokens(1)
    put_norm.wait()
    put_gwi.wait()
    put_gwo.wait()
    finish_chunk(3)
    place_tokens(2)
    place_tokens(3)

    for copies in (sum2_cp, e_cp):
        for k in copies:
            copies[k].wait_send()
    for put in put_gt:
        put.wait()


def store_kernel(pieces, *refs):
    count = len(pieces)
    sems = refs[2 * count]
    copies = []
    for k, cut in enumerate(pieces):
        size = refs[k].shape[0] // cut
        for i in range(cut):
            at = slice(i * size, (i + 1) * size)
            copies.append(
                pltpu.make_async_copy(refs[k].at[at, :], refs[count + k].at[at, :], sems.at[len(copies)])
            )
    for copy in copies:
        copy.start()
    for copy in copies:
        copy.wait()


def body(tokens, route_ids, router, norm_gain, w_in, w_out, cotangent):
    rows, width = tokens.shape[0], tokens.shape[2]
    hidden = w_in.shape[3]
    depth = 3 * rows // N
    slots = N * depth
    part = width // NC
    head = width // N
    group = 4 * depth
    shape = jax.ShapeDtypeStruct
    vmem = pl.BlockSpec(memory_space=pltpu.VMEM)
    anywhere = pl.BlockSpec(memory_space=pl.ANY)
    hbm = pl.BlockSpec(memory_space=pltpu.HBM)
    dma = pltpu.SemaphoreType.DMA
    keep = functools.partial(pltpu.with_memory_space_constraint, memory_space=pltpu.HBM)
    blocks = pltpu.VMEM((N, NC, depth, part), BF16)
    flipped = pltpu.VMEM((N, head, rows), BF16)
    row_block = pltpu.VMEM((rows, width), BF16)
    chunks = pltpu.VMEM((NC, rows, part), BF16)
    ids = pltpu.VMEM((8, rows), jnp.int32)
    out = pl.pallas_call(
        kernel,
        out_shape=(
            shape((rows, width), BF16),
            shape((rows, width), BF16),
            shape((N, width), F32),
            shape((1, width), F32),
            shape((width, hidden), BF16),
            shape((hidden, width), BF16),
        ),
        in_specs=[hbm] * 7,
        out_specs=[anywhere, anywhere, vmem, vmem, anywhere, anywhere],
        scratch_shapes=[
            row_block,
            pltpu.VMEM((2, rows), jnp.int32),
            pltpu.VMEM((N, width), BF16),
            pltpu.VMEM((1, width), F32),
            flipped,
            flipped,
            chunks,
            row_block,
            pltpu.VMEM((width, hidden), BF16),
            pltpu.VMEM((hidden, width), BF16),
            pltpu.VMEM((NC, N, part), BF16),
            ids, ids, ids,
            pltpu.VMEM((7 * depth, rows), BF16),
            pltpu.VMEM((7 * depth, rows), BF16),
            pltpu.VMEM((2 * depth, rows), BF16),
            pltpu.VMEM((rows, 7 * depth), BF16),
            pltpu.VMEM((rows, 7 * depth), BF16),
            pltpu.VMEM((rows, 2 * depth), BF16),
            flipped, flipped, flipped, flipped,
            chunks, chunks,
            blocks,
            blocks,
            pltpu.VMEM((slots, hidden), F32),
            pltpu.VMEM((slots, N), F32),
            pltpu.VMEM((slots, 1), F32),
            pltpu.VMEM((slots, hidden), BF16),
            blocks,
            blocks,
            chunks, chunks, chunks, chunks,
            pltpu.VMEM((NC, rows, part), F32),
            chunks,
            blocks,
            pltpu.VMEM((slots, hidden), BF16),
            blocks,
            pltpu.VMEM((slots, 1), F32),
            pltpu.VMEM((width, hidden), BF16),
            pltpu.VMEM((hidden, width), BF16),
            flipped,
            pltpu.VMEM((8, width), F32),
            pltpu.VMEM((8, width), F32),
            pltpu.VMEM((16, 128), F32),
            pltpu.VMEM((16, 128), BF16),
            pltpu.VMEM((2, RING, 16, 128), BF16),
            pltpu.VMEM((16, 128), BF16),
            pltpu.VMEM((2, RING, 16, 128), BF16),
            dma((7,)),
            dma((2,)), dma((2,)),
            dma((N,)), dma((N,)),
            dma((2, NC)), dma((2, NC)),
            dma((2, N)), dma((2, N)),
            dma((N, NC)), dma((N, NC)),
            dma((N,)), dma((N,)),
            dma((2, RUNS)), dma((2, RUNS)),
            dma((2, RUNS)), dma((2, RUNS)),
            dma((N,)), dma((N,)),
            dma((N, NC)), dma((N, NC)),
            dma((2, NC)), dma((2, NC)),
            dma((N,)), dma((N,)),
            dma((N,)), dma((N,)),
            dma((N,)), dma((N,)),
            dma((3,)),
            dma((NC,)),
        ],
        name="rank_mixer",
        compiler_params=pltpu.CompilerParams(
            collective_id=0, has_side_effects=True, vmem_limit_bytes=46 << 20
        ),
    )(
        keep(tokens.reshape(rows, width)),
        keep(route_ids.reshape(rows, 2).T),
        keep(router.reshape(width, N).T),
        keep(norm_gain.reshape(1, width)),
        keep(w_in.reshape(width, hidden)),
        keep(w_out.reshape(hidden, width)),
        keep(cotangent.reshape(rows, width)),
    )
    pieces = (2, 2, 1, 1, 4, 4)
    out = pl.pallas_call(
        functools.partial(store_kernel, pieces),
        out_shape=tuple(shape(v.shape, v.dtype) for v in out),
        in_specs=[anywhere] * 6,
        out_specs=[hbm] * 6,
        scratch_shapes=[dma((sum(pieces),))],
        name="store",
        compiler_params=pltpu.CompilerParams(vmem_limit_bytes=1 << 20),
    )(*out)
    normed_out, grad_tokens, grad_router, grad_gain, grad_w_in, grad_w_out = out
    return (
        normed_out.reshape(rows, 1, width),
        grad_tokens.reshape(rows, 1, width),
        grad_router.T.reshape(1, width, N),
        grad_gain,
        grad_w_in.reshape(1, 1, width, hidden),
        grad_w_out.reshape(1, 1, hidden, width),
    )


def solution(mesh):
    return jax.shard_map(
        body,
        mesh=mesh,
        in_specs=(
            P("dp", "expert", None),
            P("expert", "dp", None),
            P("expert", None, None),
            P("expert", None),
            P("expert", "dp", None, None),
            P("expert", "dp", None, None),
            P("dp", "expert", None),
        ),
        out_specs=(
            P("dp", "expert", None),
            P("dp", "expert", None),
            P("expert", None, None),
            P("expert", None),
            P("expert", "dp", None, None),
            P("expert", "dp", None, None),
        ),
        check_vma=False,
    )
```

```python
import functools

import jax
import jax.numpy as jnp
from jax import lax
from jax.experimental import pallas as pl
from jax.experimental.pallas import tpu as pltpu
from jax.sharding import PartitionSpec as P

MESH = pl.DeviceIdType.MESH
F32 = jnp.float32
BF16 = jnp.bfloat16

gelu_coef = 0.7978845608028654
cubic_coef = 0.044715
norm_eps = 1e-05

N = 16
NC = 4
NG = 4
RING = 8
STEPS = (0, 1, -1, 2, -2, 3, -3, 4)
HOPS = (0, 0, 0, 0, 0, 0, -1, -1, 1, 1, -2, -2, 2, 2, 3, -3)
FROM_LOW = (4, 5, 8, 9, 12, 13, 14)
FROM_HIGH = (2, 3, 6, 7, 10, 11, 15)
OWN = (0, 1)
HERE = (0, 2, 4)
AWAY = tuple(r for r in range(N) if r not in HERE)
TILE = 32
RUNS = 8


def dot(a, b):
    return lax.dot_general(a, b, (((1,), (0,)), ((), ())), preferred_element_type=F32)


def dot_nt(a, b):
    return lax.dot_general(a, b, (((1,), (1,)), ((), ())), preferred_element_type=F32)


def dot_tn(a, b):
    return lax.dot_general(a, b, (((0,), (0,)), ((), ())), preferred_element_type=F32)


def gelu_and_slope(value):
    inner = gelu_coef * (value + cubic_coef * value * value * value)
    tangent = jnp.tanh(inner)
    half = 0.5 * (1.0 + tangent)
    slope = half + 0.5 * value * (1.0 - tangent * tangent) * gelu_coef * (
        1.0 + 3.0 * cubic_coef * value * value
    )
    return value * half, slope


def kernel(
    tok_h, ids_h, rt_h, gain_h, win_h, wout_h, cot_h,
    no_h, gt_h, gr_ref, gg_ref, gwi_h, gwo_h,
    tok, ids_ref, rt_ref, gain_ref, tok_t, mix_t, mixed, cot, win, wout, rt4,
    ids_own, ids_low, ids_high, pl_m, ph_m, po_m, pl_t, ph_t, po_t,
    raw_lt, raw_ht, mix_lt, mix_ht, raw_l, raw_h, xs, xr, pre, logit, gate, act, ys, yr,
    part_l, part_h, sum_h, sum_l, acc, grd, gr, gp, ds, glog,
    gwi, gwo, gt_t, ggp, rcol, small,
    gain_s, gain_r, col_s, col_r,
    load_sem, ids_ss, ids_rs, mix_ss, mix_rs, raw_ss, raw_rs, side_ss, side_rs, a_ss, a_rs, b_ss, b_rs,
    sum_ss, sum_rs, raw2_ss, raw2_rs, c_ss, c_rs, d_ss, d_rs, sum2_ss, sum2_rs,
    e_ss, e_rs, gn_ss, gn_rs, cl_ss, cl_rs, out_sem, put_sem,
):
    rows, width = tok.shape
    head = width // N
    part = width // NC
    hidden = win.shape[1]
    depth = xs.shape[2]
    group = depth * 4
    slots = N * depth
    tokens4 = N // NC
    dp = lax.axis_index("dp")
    ex = lax.axis_index("expert")
    z, co = dp // 2, dp % 2
    xm, ym = ex // 4, ex % 4

    def partner(r):
        return ((z + STEPS[r // 2] + RING) % RING) * 2 + (co + r % 2) % 2

    def target(r):
        return ((z + HOPS[r] + RING) % RING) * 2 + (co + r % 2) % 2

    def origin(r):
        return ((z - HOPS[r] + RING) % RING) * 2 + (co + r % 2) % 2

    high = ((z + 1) % RING) * 2 + co
    low = ((z + RING - 1) % RING) * 2 + co

    def send(src, dst, send_sem, recv_sem, to):
        copy = pltpu.make_async_remote_copy(
            src_ref=src, dst_ref=dst, send_sem=send_sem, recv_sem=recv_sem,
            device_id=(to, ex), device_id_type=MESH,
        )
        copy.start()
        return copy

    def load(src, dst, k):
        copy = pltpu.make_async_copy(src, dst, load_sem.at[k])
        copy.start()
        return copy

    got_tok = load(tok_h, tok, 0)
    got_ids = load(ids_h, ids_ref, 1)

    barrier = pltpu.get_barrier_semaphore()
    for r in range(1, N):
        pl.semaphore_signal(barrier, inc=1, device_id=(partner(r), ex), device_id_type=MESH)
    for k in range(1, N):
        pl.semaphore_signal(barrier, inc=1, device_id=(dp, (ex + k) % N), device_id_type=MESH)
    got_tok.wait()
    got_ids.wait()
    got_win = load(win_h, win, 4)
    got_wout = load(wout_h, wout, 5)
    got_rt = load(rt_h, rt_ref, 2)
    got_gain = load(gain_h, gain_ref, 3)
    got_cot = load(cot_h, cot, 6)
    ids_own[...] = jnp.zeros_like(ids_own)
    ids_own[0:2, :] = ids_ref[...]

    ids_cp, raw_cp, mix_cp = {}, {}, {}
    for i in range(NC):
        c = (xm - i + 4) % 4
        turned = tok[:, pl.ds(pl.multiple_of(c * part, part), part)].T
        tok_t[pl.ds(c * tokens4, tokens4)] = turned.reshape(tokens4, head, rows)
        if i == 0:
            mix_t[ex] = tok_t[ex]
            pl.semaphore_wait(barrier, 2 * (N - 1))
        heads = pl.ds(c * tokens4, tokens4)
        raw_cp[0, i] = send(
            tok_t.at[heads], raw_lt.at[heads], raw_ss.at[0, i], raw_rs.at[0, i], high
        )
        raw_cp[1, i] = send(
            tok_t.at[heads], raw_ht.at[heads], raw_ss.at[1, i], raw_rs.at[1, i], low
        )
        for yy in range(4):
            k = i * 4 + yy
            to = c * 4 + (ym + yy) % 4
            if k == 0:
                continue
            mix_cp[k] = pltpu.make_async_remote_copy(
                src_ref=tok_t.at[to], dst_ref=mix_t.at[ex],
                send_sem=mix_ss.at[k], recv_sem=mix_rs.at[k],
                device_id=(dp, to), device_id_type=MESH,
            )
            mix_cp[k].start()
        if i == 0:
            ids_cp[0] = send(ids_own, ids_low, ids_ss.at[0], ids_rs.at[0], high)
            ids_cp[1] = send(ids_own, ids_high, ids_ss.at[1], ids_rs.at[1], low)

    label = lax.broadcasted_iota(jnp.int32, (N, rows), 0)
    earlier = (
        lax.broadcasted_iota(jnp.int32, (rows, rows), 0)
        < lax.broadcasted_iota(jnp.int32, (rows, rows), 1)
    ).astype(F32)
    earlier = earlier.astype(BF16)
    slot = lax.broadcasted_iota(jnp.int32, (depth, rows), 0)

    def place(ids, members, matrix, flipped):
        ids0, ids1 = ids[0:1, :], ids[1:2, :]
        hot0 = (label == ids0).astype(F32)
        hot1 = (label == ids1).astype(F32)
        before = dot((hot0 + hot1).astype(BF16), earlier)
        at0 = jnp.sum(before * hot0, axis=0, keepdims=True).astype(jnp.int32)
        at1 = jnp.sum(before * hot1, axis=0, keepdims=True).astype(jnp.int32)
        blocks = []
        for r in members:
            e = target(r)
            goal0 = jnp.where(ids0 == e, at0, -1)
            goal1 = jnp.where(ids1 == e, at1, -1)
            blocks.append(jnp.logical_or(slot == goal0, slot == goal1).astype(F32))
        placed = jnp.concatenate(blocks, axis=0)
        matrix[...] = placed.astype(BF16)
        flipped[...] = placed.T.astype(BF16)

    def stack(blocks, members, q):
        return jnp.concatenate([blocks[r, q] for r in members], axis=0)

    def expand(matrix, values, members, q, out, arrived, first=0):
        at = slice(first * depth, (first + len(members)) * depth)
        sent = dot(matrix[at, :], values).astype(BF16)
        for n, r in enumerate(members):
            into = arrived if r in HERE else out
            into[r, q] = sent[n * depth : (n + 1) * depth]

    a_cp, side_cp = {}, {}
    sides = ((raw_lt, mix_lt, raw_l), (raw_ht, mix_ht, raw_h))

    def send_mixed(r, i):
        c = (xm + i) % 4
        a_cp[r, i] = send(xs.at[r, c], xr.at[r, c], a_ss.at[r, i], a_rs.at[r, i], target(r))

    def relay(i):
        c = (xm - i + 4) % 4
        for n, (whole, gathered, _) in enumerate(sides):
            raw_cp[n, i].wait_recv()
            for yy in range(4):
                k = i * 4 + yy
                to = c * 4 + (ym + yy) % 4
                if k == 0:
                    gathered[ex] = whole[ex]
                    continue
                side_cp[n, k] = pltpu.make_async_remote_copy(
                    src_ref=whole.at[to], dst_ref=gathered.at[ex],
                    send_sem=side_ss.at[n, k], recv_sem=side_rs.at[n, k],
                    device_id=(dp, to), device_id_type=MESH,
                )
                side_cp[n, k].start()

    def own_chunk(i):
        c = (xm + i) % 4
        for yy in range(4):
            if i * 4 + yy:
                mix_cp[i * 4 + yy].wait_recv()
        mixed[c] = mix_t[pl.ds(c * tokens4, tokens4)].reshape(part, rows).T
        expand(po_m, mixed[c], OWN, c, xs, xr)
        send_mixed(1, i)

    def pass_on(i):
        c = (xm + i) % 4
        for n, (_, gathered, plain) in enumerate(sides):
            for yy in range(4):
                if i * 4 + yy:
                    side_cp[n, i * 4 + yy].wait_recv()
            plain[c] = gathered[pl.ds(c * tokens4, tokens4)].reshape(part, rows).T
            if n == 0:
                expand(pl_m, plain[c], FROM_LOW, c, xs, xr)
            else:
                expand(ph_m, plain[c], FROM_HIGH, c, xs, xr)
        for r in AWAY[:0:-1]:
            send_mixed(r, i)

    place(ids_own, OWN, po_m, po_t)
    ids_cp[0].wait_recv()
    ids_cp[1].wait_recv()
    place(ids_low, FROM_LOW, pl_m, pl_t)
    place(ids_high, FROM_HIGH, ph_m, ph_t)
    relay(0)
    for i in range(NC):
        own_chunk(i)
        if i + 1 < NC:
            relay(i + 1)
        pass_on(i)

    got_rt.wait()
    got_win.wait()
    got_wout.wait()
    for c in range(NC):
        rt4[c] = rt_ref[:, c * part : (c + 1) * part]
    mine = lax.broadcasted_iota(jnp.int32, (group, N), 1) == dp
    for i in range(NC - 1):
        c = (xm + i) % 4
        for r in AWAY:
            a_cp[r, i].wait_recv()
        for g in range(NG):
            at = slice(g * group, (g + 1) * group)
            block = xr[4 * g : 4 * g + 4, c].reshape(group, part)
            more = dot(block, win[pl.ds(pl.multiple_of(c * part, part), part), :])
            more_logit = dot_nt(block, rt4[c])
            if i == 0:
                pre[at, :] = more
                logit[at, :] = more_logit
            else:
                pre[at, :] += more
                logit[at, :] += more_logit
    b_cp = {}
    c = (xm + NC - 1) % 4
    for g in (0, 3, 2, 1):
        at = slice(g * group, (g + 1) * group)
        for r in range(4 * g, 4 * g + 4):
            if r in AWAY:
                a_cp[r, NC - 1].wait_recv()
        block = xr[4 * g : 4 * g + 4, c].reshape(group, part)
        value = pre[at, :] + dot(block, win[pl.ds(pl.multiple_of(c * part, part), part), :])
        score = logit[at, :] + dot_nt(block, rt4[c])
        share = jax.nn.sigmoid(jnp.sum(jnp.where(mine, score, 0.0), axis=1, keepdims=True))
        gate[at, :] = share
        activated, slope = gelu_and_slope(value)
        pre[at, :] = slope
        act[at, :] = activated.astype(BF16)
        for q in range(NC):
            out = dot(act[at, :], wout[:, q * part : (q + 1) * part])
            result = (share * out).astype(BF16).reshape(4, depth, part)
            ys[4 * g : 4 * g + 4, q] = result
            for r in range(4 * g, 4 * g + 4):
                if r in HERE:
                    yr[r, q] = result[r - 4 * g]
        for r in range(4 * g, 4 * g + 4):
            if r in AWAY:
                b_cp[r] = send(ys.at[r], yr.at[r], b_ss.at[r], b_rs.at[r], origin(r))

    sum_cp = {}
    for r in AWAY:
        b_cp[r].wait_recv()
    run = rows // RUNS
    for i in range(RUNS):
        at = slice(i * run, (i + 1) * run)
        for q in range(NC):
            part_l[q, at] = dot(pl_t[at, :], stack(yr, FROM_LOW, q)).astype(BF16)
        sum_cp[0, i] = send(
            part_l.at[:, at, :], sum_h.at[:, at, :], sum_ss.at[0, i], sum_rs.at[0, i], low
        )
        for q in range(NC):
            part_h[q, at] = dot(ph_t[at, :], stack(yr, FROM_HIGH, q)).astype(BF16)
        sum_cp[1, i] = send(
            part_h.at[:, at, :], sum_l.at[:, at, :], sum_ss.at[1, i], sum_rs.at[1, i], high
        )
    for q in range(NC):
        acc[q] = mixed[q].astype(F32) + dot(po_t[...], stack(yr, OWN, q))
    got_cot.wait()
    got_gain.wait()
    ggp[...] = jnp.zeros_like(ggp)

    def norm_rows(j, carry):
        at = pl.ds(pl.multiple_of(j * TILE, TILE), TILE)
        cols = [slice(q * part, (q + 1) * part) for q in range(NC)]
        resid = [
            acc[q, at, :] + sum_h[q, at, :].astype(F32) + sum_l[q, at, :].astype(F32)
            for q in range(NC)
        ]
        mean = sum(jnp.sum(v, axis=1, keepdims=True) for v in resid) / width
        resid = [v - mean for v in resid]
        var = sum(jnp.sum(v * v, axis=1, keepdims=True) for v in resid) / width
        inv_std = lax.rsqrt(var + norm_eps)
        normed = [v * inv_std for v in resid]
        grads, m1, m2 = [], 0.0, 0.0
        for q in range(NC):
            gain = gain_ref[0:1, cols[q]]
            cot_f = cot[at, cols[q]].astype(F32)
            cot[at, cols[q]] = (normed[q] * gain).astype(BF16)
            ggp[0:1, cols[q]] += jnp.sum(cot_f * normed[q], axis=0, keepdims=True)
            grad = cot_f * gain
            grads.append(grad)
            m1 += jnp.sum(grad, axis=1, keepdims=True)
            m2 += jnp.sum(grad * normed[q], axis=1, keepdims=True)
        m1, m2 = m1 / width, m2 / width
        for q in range(NC):
            grad = inv_std * (grads[q] - m1 - normed[q] * m2)
            acc[q, at, :] = grad
            grd[q, at, :] = grad.astype(BF16)
        return carry

    raw2_cp, c_cp = {}, {}
    for i in range(RUNS):
        sum_cp[0, i].wait_recv()
        sum_cp[1, i].wait_recv()
        lax.fori_loop(i * run // TILE, (i + 1) * run // TILE, norm_rows, 0)
        src = grd.at[:, i * run : (i + 1) * run, :]
        to_high, to_low = (d.at[:, i * run : (i + 1) * run, :] for d in (raw_l, raw_h))
        raw2_cp[0, i] = send(src, to_high, raw2_ss.at[0, i], raw2_rs.at[0, i], high)
        raw2_cp[1, i] = send(src, to_low, raw2_ss.at[1, i], raw2_rs.at[1, i], low)

    def spread(vector, source, target, gathered, send_sems, recv_sems):
        source[...] = jnp.zeros_like(source)
        for j in range(width // 128):
            source[j : j + 1, :] = vector[0:1, j * 128 : (j + 1) * 128]
        target[...] = source[...].astype(BF16)
        gathered[co, z] = target[...]
        copies = {}
        for k in range(1, RING):
            copies[k] = send(
                target, gathered.at[co, z], send_sems.at[k], recv_sems.at[k],
                ((z + k) % RING) * 2 + co,
            )
        return copies

    def exchange(copies, gathered, send_sems, recv_sems):
        for k in range(1, RING):
            copies[k].wait_recv()
        copies[0] = send(
            gathered.at[co], gathered.at[co], send_sems.at[0], recv_sems.at[0],
            z * 2 + (co + 1) % 2,
        )

    gn_cp = spread(ggp, small, gain_s, gain_r, gn_ss, gn_rs)
    put_norm = pltpu.make_async_copy(cot, no_h, out_sem.at[0])
    put_norm.start()
    for copies in (mix_cp, raw_cp):
        for k in copies:
            copies[k].wait_send()
    for k in a_cp:
        a_cp[k].wait_send()
    for k in sum_cp:
        sum_cp[k].wait_send()
    for q in range(NC):
        expand(po_m, grd[q], OWN, q, xs, gr)
    def send_gradient(r):
        c_cp[r] = send(xs.at[r], gr.at[r], c_ss.at[r], c_rs.at[r], target(r))

    send_gradient(1)
    for first, last in ((4, 7), (0, 4)):
        for n, (matrix, values, members) in enumerate(
            ((pl_m, raw_l, FROM_LOW), (ph_m, raw_h, FROM_HIGH))
        ):
            if first:
                for i in range(RUNS):
                    raw2_cp[n, i].wait_recv()
            for q in range(NC):
                expand(matrix, values[q], members[first:last], q, xs, gr, first)
            for r in members[first:last]:
                if r in AWAY:
                    send_gradient(r)

    rcol[...] = jnp.zeros_like(rcol)
    mine_row = lax.broadcasted_iota(jnp.int32, (N, part), 0) == dp
    d_cp = {}

    def send_back(r, i):
        c = (xm + 1 + i) % 4
        d_cp[r, i] = send(ds.at[r, c], yr.at[r, c], d_ss.at[r, i], d_rs.at[r, i], origin(r))

    for g in (0, 3, 2, 1):
        at = slice(g * group, (g + 1) * group)
        for r in range(4 * g, 4 * g + 4):
            if r in AWAY:
                c_cp[r].wait_recv()
        share = gate[at, :]
        grad_act, grad_gate = 0.0, 0.0
        for q in range(NC):
            grad = gr[4 * g : 4 * g + 4, q].reshape(group, part).astype(F32)
            result = ys[4 * g : 4 * g + 4, q].reshape(group, part).astype(F32)
            grad_gate += jnp.sum(grad * result, axis=1, keepdims=True)
            grad_out = (share * grad).astype(BF16)
            gr[4 * g : 4 * g + 4, q] = grad_out.reshape(4, depth, part)
            grad_act += dot_nt(grad_out, wout[:, q * part : (q + 1) * part])
        grad_logit = grad_gate * (1.0 - share)
        glog[at, :] = grad_logit
        gp[at, :] = (grad_act * pre[at, :]).astype(BF16)
        for i in range(NC):
            c = (xm + 1 + i) % 4
            weights = jnp.sum(jnp.where(mine_row, rt4[c].astype(F32), 0.0), axis=0, keepdims=True)
            back = dot_nt(gp[at, :], win[pl.ds(pl.multiple_of(c * part, part), part), :])
            back = (back + grad_logit * weights).astype(BF16).reshape(4, depth, part)
            ds[4 * g : 4 * g + 4, c] = back
            for r in range(4 * g, 4 * g + 4):
                if r in HERE:
                    yr[r, c] = back[r - 4 * g]
                else:
                    send_back(r, i)

    for g in range(NG):
        at = slice(g * group, (g + 1) * group)
        for q in range(NC):
            block = xr[4 * g : 4 * g + 4, q].reshape(group, part).astype(F32)
            rcol[0:1, q * part : (q + 1) * part] += jnp.sum(
                glog[at, :] * block, axis=0, keepdims=True
            )
    cl_cp = spread(rcol, small, col_s, col_r, cl_ss, cl_rs)
    for q in range(NC):
        cols = slice(q * part, (q + 1) * part)
        gwi[cols, :] = dot_tn(xr[:, q].reshape(slots, part), gp[...]).astype(BF16)
    put_gwi = pltpu.make_async_copy(gwi, gwi_h, out_sem.at[1])
    put_gwi.start()

    def out_gradient(q):
        gwo[:, q * part : (q + 1) * part] = dot_tn(act[...], gr[:, q].reshape(slots, part)).astype(BF16)

    sum2_cp, e_cp = {}, {}

    def sum_back(i):
        c = (xm + 1 + i) % 4
        for r in AWAY:
            d_cp[r, i].wait_recv()
        part_l[c] = dot(pl_t[...], stack(yr, FROM_LOW, c)).astype(BF16)
        sum2_cp[0, i] = send(part_l.at[c], sum_h.at[c], sum2_ss.at[0, i], sum2_rs.at[0, i], low)
        part_h[c] = dot(ph_t[...], stack(yr, FROM_HIGH, c)).astype(BF16)
        sum2_cp[1, i] = send(part_h.at[c], sum_l.at[c], sum2_ss.at[1, i], sum2_rs.at[1, i], high)
        acc[c] += dot(po_t[...], stack(yr, OWN, c))

    def finish_chunk(i):
        c = (xm + 1 + i) % 4
        sum2_cp[0, i].wait_recv()
        sum2_cp[1, i].wait_recv()
        total = acc[c] + sum_h[c].astype(F32) + sum_l[c].astype(F32)
        tok_t[pl.ds(c * tokens4, tokens4)] = total.astype(BF16).T.reshape(tokens4, head, rows)
        for yy in range(4):
            to = c * tokens4 + (ym + yy) % 4
            if i == NC - 1 and yy == 0:
                gt_t[ex] = tok_t[ex]
                continue
            k = i * 4 + yy
            e_cp[k] = pltpu.make_async_remote_copy(
                src_ref=tok_t.at[to], dst_ref=gt_t.at[ex],
                send_sem=e_ss.at[k], recv_sem=e_rs.at[k],
                device_id=(dp, to), device_id_type=MESH,
            )
            e_cp[k].start()

    sum_back(0)
    out_gradient(0)
    out_gradient(1)
    sum_back(1)
    finish_chunk(0)
    out_gradient(2)
    out_gradient(3)
    put_gwo = pltpu.make_async_copy(gwo, gwo_h, out_sem.at[2])
    put_gwo.start()
    for copies in (ids_cp, side_cp, b_cp, raw2_cp, c_cp):
        for k in copies:
            copies[k].wait_send()
    exchange(gn_cp, gain_r, gn_ss, gn_rs)
    exchange(cl_cp, col_r, cl_ss, cl_rs)
    sum_back(2)
    finish_chunk(1)

    sum_back(3)

    gn_cp[0].wait_recv()
    cl_cp[0].wait_recv()
    total = 0.0
    for e in range(N):
        total += gain_r[e % 2, e // 2].astype(F32)
    small[...] = total
    for j in range(width // 128):
        gg_ref[0:1, j * 128 : (j + 1) * 128] = small[j : j + 1, :]
    for e in range(N):
        small[...] = col_r[e % 2, e // 2].astype(F32)
        for j in range(width // 128):
            gr_ref[e : e + 1, j * 128 : (j + 1) * 128] = small[j : j + 1, :]

    finish_chunk(2)
    for copies in (d_cp, gn_cp, cl_cp):
        for k in copies:
            copies[k].wait_send()
    put_gt = []

    def place_tokens(i):
        c = (xm + NC - 1 - i) % 4
        for yy in range(4):
            if i < NC - 1 or yy:
                e_cp[i * 4 + yy].wait_recv()
        cols = pl.ds(pl.multiple_of(c * part, part), part)
        tok[:, cols] = gt_t[pl.ds(c * tokens4, tokens4)].reshape(part, rows).T
        put_gt.append(
            pltpu.make_async_copy(tok.at[:, cols], gt_h.at[:, cols], put_sem.at[i])
        )
        put_gt[i].start()

    place_tokens(0)
    place_tokens(1)
    put_norm.wait()
    put_gwi.wait()
    put_gwo.wait()
    finish_chunk(3)
    place_tokens(2)
    place_tokens(3)

    for copies in (sum2_cp, e_cp):
        for k in copies:
            copies[k].wait_send()
    for put in put_gt:
        put.wait()


def store_kernel(pieces, *refs):
    count = len(pieces)
    sems = refs[2 * count]
    copies = []
    for k, cut in enumerate(pieces):
        size = refs[k].shape[0] // cut
        for i in range(cut):
            at = slice(i * size, (i + 1) * size)
            copies.append(
                pltpu.make_async_copy(refs[k].at[at, :], refs[count + k].at[at, :], sems.at[len(copies)])
            )
    for copy in copies:
        copy.start()
    for copy in copies:
        copy.wait()


def body(tokens, route_ids, router, norm_gain, w_in, w_out, cotangent):
    rows, width = tokens.shape[0], tokens.shape[2]
    hidden = w_in.shape[3]
    depth = 3 * rows // N
    slots = N * depth
    part = width // NC
    head = width // N
    group = 4 * depth
    shape = jax.ShapeDtypeStruct
    vmem = pl.BlockSpec(memory_space=pltpu.VMEM)
    anywhere = pl.BlockSpec(memory_space=pl.ANY)
    hbm = pl.BlockSpec(memory_space=pltpu.HBM)
    dma = pltpu.SemaphoreType.DMA
    keep = functools.partial(pltpu.with_memory_space_constraint, memory_space=pltpu.HBM)
    blocks = pltpu.VMEM((N, NC, depth, part), BF16)
    flipped = pltpu.VMEM((N, head, rows), BF16)
    row_block = pltpu.VMEM((rows, width), BF16)
    chunks = pltpu.VMEM((NC, rows, part), BF16)
    ids = pltpu.VMEM((8, rows), jnp.int32)
    out = pl.pallas_call(
        kernel,
        out_shape=(
            shape((rows, width), BF16),
            shape((rows, width), BF16),
            shape((N, width), F32),
            shape((1, width), F32),
            shape((width, hidden), BF16),
            shape((hidden, width), BF16),
        ),
        in_specs=[hbm] * 7,
        out_specs=[anywhere, anywhere, vmem, vmem, anywhere, anywhere],
        scratch_shapes=[
            row_block,
            pltpu.VMEM((2, rows), jnp.int32),
            pltpu.VMEM((N, width), BF16),
            pltpu.VMEM((1, width), F32),
            flipped,
            flipped,
            chunks,
            row_block,
            pltpu.VMEM((width, hidden), BF16),
            pltpu.VMEM((hidden, width), BF16),
            pltpu.VMEM((NC, N, part), BF16),
            ids, ids, ids,
            pltpu.VMEM((7 * depth, rows), BF16),
            pltpu.VMEM((7 * depth, rows), BF16),
            pltpu.VMEM((2 * depth, rows), BF16),
            pltpu.VMEM((rows, 7 * depth), BF16),
            pltpu.VMEM((rows, 7 * depth), BF16),
            pltpu.VMEM((rows, 2 * depth), BF16),
            flipped, flipped, flipped, flipped,
            chunks, chunks,
            blocks,
            blocks,
            pltpu.VMEM((slots, hidden), F32),
            pltpu.VMEM((slots, N), F32),
            pltpu.VMEM((slots, 1), F32),
            pltpu.VMEM((slots, hidden), BF16),
            blocks,
            blocks,
            chunks, chunks, chunks, chunks,
            pltpu.VMEM((NC, rows, part), F32),
            chunks,
            blocks,
            pltpu.VMEM((slots, hidden), BF16),
            blocks,
            pltpu.VMEM((slots, 1), F32),
            pltpu.VMEM((width, hidden), BF16),
            pltpu.VMEM((hidden, width), BF16),
            flipped,
            pltpu.VMEM((8, width), F32),
            pltpu.VMEM((8, width), F32),
            pltpu.VMEM((16, 128), F32),
            pltpu.VMEM((16, 128), BF16),
            pltpu.VMEM((2, RING, 16, 128), BF16),
            pltpu.VMEM((16, 128), BF16),
            pltpu.VMEM((2, RING, 16, 128), BF16),
            dma((7,)),
            dma((2,)), dma((2,)),
            dma((N,)), dma((N,)),
            dma((2, NC)), dma((2, NC)),
            dma((2, N)), dma((2, N)),
            dma((N, NC)), dma((N, NC)),
            dma((N,)), dma((N,)),
            dma((2, RUNS)), dma((2, RUNS)),
            dma((2, RUNS)), dma((2, RUNS)),
            dma((N,)), dma((N,)),
            dma((N, NC)), dma((N, NC)),
            dma((2, NC)), dma((2, NC)),
            dma((N,)), dma((N,)),
            dma((N,)), dma((N,)),
            dma((N,)), dma((N,)),
            dma((3,)),
            dma((NC,)),
        ],
        name="rank_mixer",
        compiler_params=pltpu.CompilerParams(
            collective_id=0, has_side_effects=True, vmem_limit_bytes=46 << 20
        ),
    )(
        keep(tokens.reshape(rows, width)),
        keep(route_ids.reshape(rows, 2).T),
        keep(router.reshape(width, N).T),
        keep(norm_gain.reshape(1, width)),
        keep(w_in.reshape(width, hidden)),
        keep(w_out.reshape(hidden, width)),
        keep(cotangent.reshape(rows, width)),
    )
    pieces = (2, 2, 1, 1, 4, 4)
    out = pl.pallas_call(
        functools.partial(store_kernel, pieces),
        out_shape=tuple(shape(v.shape, v.dtype) for v in out),
        in_specs=[anywhere] * 6,
        out_specs=[hbm] * 6,
        scratch_shapes=[dma((sum(pieces),))],
        name="store",
        compiler_params=pltpu.CompilerParams(vmem_limit_bytes=1 << 20),
    )(*out)
    normed_out, grad_tokens, grad_router, grad_gain, grad_w_in, grad_w_out = out
    return (
        normed_out.reshape(rows, 1, width),
        grad_tokens.reshape(rows, 1, width),
        grad_router.T.reshape(1, width, N),
        grad_gain,
        grad_w_in.reshape(1, 1, width, hidden),
        grad_w_out.reshape(1, 1, hidden, width),
    )


def solution(mesh):
    return jax.shard_map(
        body,
        mesh=mesh,
        in_specs=(
            P("dp", "expert", None),
            P("expert", "dp", None),
            P("expert", None, None),
            P("expert", None),
            P("expert", "dp", None, None),
            P("expert", "dp", None, None),
            P("dp", "expert", None),
        ),
        out_specs=(
            P("dp", "expert", None),
            P("dp", "expert", None),
            P("expert", None, None),
            P("expert", None),
            P("expert", "dp", None, None),
            P("expert", "dp", None, None),
        ),
        check_vma=False,
    )
```
